32 devices in a mesh: fsdp: 4 (over z), ctx: 4 (over y, x), tp: 2 (over core).
Axes of the slice: x: 2, y: 2, z: 4, core: 2. Of those that a mesh axis runs over, the one named last changes fastest.
Arguments:
- hidden_in: bfloat16 [16, 1024, 768], P('fsdp', 'ctx'), may hold values from -6 to 6
- lengths: int32 [16], P('fsdp'), may hold values from 256 to 1024, as said below
- out_grad: bfloat16 [16, 1024, 768], P('fsdp', 'ctx'), may hold values from -6 to 6
- w_qkv: bfloat16 [3, 768, 768], P(None, 'fsdp', 'tp'), may hold values from -0.21875 to 0.21875
- qv_bias: bfloat16 [2, 12, 64], P(None, 'tp', 'fsdp'), may hold values from -0.3125 to 0.3125
- w_out: bfloat16 [768, 768], P('tp', 'fsdp'), may hold values from -3.5 to 3.5
- out_biases: bfloat16 [2, 768], P(None, 'fsdp'), may hold values from -4 to 4
- norm_gains: bfloat16 [2, 768], P(None, 'fsdp'), may hold values from 0.25 to 1.75
- norm_biases: bfloat16 [2, 768], P(None, 'fsdp'), may hold values from -4 to 4
- w_in: bfloat16 [768, 3072], P(None, ('fsdp', 'tp')), may hold values from -0.21875 to 0.21875
- ffn_bias: bfloat16 [3072], P(('fsdp', 'tp')), may hold values from -6 to 6
- w_ffo: bfloat16 [3072, 768], P(('fsdp', 'tp')), may hold values from -0.109375 to 0.109375
Outputs:
- hidden_out: bfloat16 [16, 1024, 768], P('fsdp', 'ctx')
- hidden_grad: bfloat16 [16, 1024, 768], P('fsdp', 'ctx')
- grad_qkv: float32 [3, 768, 768], P(None, 'fsdp', 'tp')
- grad_qv_bias: float32 [2, 12, 64], P(None, 'tp', 'fsdp')
- grad_out: float32 [768, 768], P('tp', 'fsdp')
- grad_out_biases: float32 [2, 768], P(None, 'fsdp')
- grad_gains: float32 [2, 768], P(None, 'fsdp')
- grad_shifts: float32 [2, 768], P(None, 'fsdp')
- grad_in: float32 [768, 3072], P(None, ('fsdp', 'tp'))
- grad_ffn_bias: float32 [3072], P(('fsdp', 'tp'))
- grad_ffo: float32 [3072, 768], P(('fsdp', 'tp'))
The draws below stay inside these ranges and needn't reach their ends.
Inputs may be any that keep to these rules, and one draw needn't show every extreme that they name: lengths[s] counts the valid positions of slot s from its start; in every draw one slot has 1024 and one has 256.
All inputs are finite; a program needn't handle non-finite values.
Results may differ from the reference program's by a relative error of at most 0.019.
Values may be sent and summed in bfloat16 or wider, within the bound.
A program may use at most 192 MiB of HBM per device.

```python
import jax
import jax.numpy as jnp
from jax import lax

D = 768
HEADS = 12
HD = 64
FF = 3072
SLOTS = 16
SEQ = 1024


def draw_lengths(key, part):
    chosen_lengths = jax.random.randint(jax.random.fold_in(key, 1), (SLOTS,), SEQ // 4, SEQ + 1)
    slot_order = jax.random.permutation(jax.random.fold_in(key, 2), SLOTS)
    chosen_lengths = chosen_lengths.at[slot_order[0]].set(SEQ)
    chosen_lengths = chosen_lengths.at[slot_order[1]].set(SEQ // 4)
    return chosen_lengths.astype(jnp.int32)


def steps_of(rng, shape, shards, smallest, top_value):
    factor_of = 1.0
    for dim, parts in shards:
        steps = jax.random.uniform(jax.random.fold_in(jax.random.fold_in(rng, 6), dim), (parts,), jnp.float32, smallest / len(shards), top_value / len(shards))
        factor_of = factor_of * jnp.repeat(jnp.exp(steps), shape[dim] // parts).reshape((-1,) + (1,) * (len(shape) - 1 - dim))
    return factor_of


def normal_values(own_key, dims, width, most, pieces=(), dtype=jnp.bfloat16):
    gain = steps_of(own_key, dims, pieces, -0.22, 0.18) if pieces else 1.0
    drawn = jax.random.normal(own_key, dims, jnp.float32) * width * gain
    return jnp.minimum(jnp.maximum(drawn, -most), most).astype(dtype)


def setup_inputs(seed: int = 0) -> dict:
    keys = jax.random.split(jax.random.key(seed), 13)
    hidden_in = normal_values(keys[0], (SLOTS, SEQ, D), 1.0, 6.0, ((0, 4), (1, 4)))
    lengths = draw_lengths(jax.random.fold_in(keys[12], 71), 0)
    out_grad = normal_values(keys[2], (SLOTS, SEQ, D), 1.0, 6.0, ((0, 4), (1, 4)))
    w_qkv = normal_values(keys[3], (3, D, D), D ** -0.5, 0.21875, ((1, 4), (2, 2)))
    qv_bias = normal_values(keys[4], (2, HEADS, HD), 0.02, 0.3125, ((1, 2), (2, 4)))
    w_out = normal_values(keys[5], (D, D), (max(1, 4 * D // SEQ)) ** -0.5, 3.5, ((0, 2), (1, 4)))
    out_biases = normal_values(keys[6], (2, D), 0.3, 4.0, ((1, 4),))
    norm_gains = jnp.clip(1.0 + 0.15 * jax.random.normal(keys[7], (2, D), jnp.float32), 0.25, 1.75).astype(jnp.bfloat16)
    norm_biases = normal_values(keys[8], (2, D), 0.3, 4.0, ((1, 4),))
    w_in = normal_values(keys[9], (D, FF), D ** -0.5, 0.21875, ((1, 8),))
    ffn_bias = normal_values(keys[10], (FF,), 0.5, 6.0, ((0, 8),))
    w_ffo = normal_values(keys[11], (FF, D), FF ** -0.5, 0.109375, ((0, 8),))
    return dict(hidden_in=hidden_in, lengths=lengths, out_grad=out_grad, w_qkv=w_qkv, qv_bias=qv_bias, w_out=w_out, out_biases=out_biases, norm_gains=norm_gains, norm_biases=norm_biases, w_in=w_in, ffn_bias=ffn_bias, w_ffo=w_ffo)


epsilon = 1e-05
masked_value = -1e+30

@jax.custom_vjp
def low(v):
    return lax.optimization_barrier(v.astype(jnp.bfloat16)).astype(jnp.float32)

@jax.custom_vjp
def low_back(v):
    return v

def low_keep(v):
    return (low(v), None)

def low_pass(kept, grad):
    return (grad,)

def back_keep(v):
    return (v, None)

def back_low(kept, grad):
    return (low(grad),)
low.defvjp(low_keep, low_pass)
low_back.defvjp(back_keep, back_low)

def product(left, right):
    return jnp.dot(left, right, precision=lax.Precision.HIGHEST)

def norm_rows(residual, gain_row, shift_row):
    centre = lax.optimization_barrier(jnp.mean(residual, axis=-1, keepdims=True))
    centred = residual - centre
    spread = lax.optimization_barrier(jnp.mean(centred * centred, axis=-1, keepdims=True))
    return centred * lax.rsqrt(spread + epsilon) * gain_row + shift_row

def encoder_layer(tokens, key_mask, params):
    w_proj, proj_bias, w_back, branch_biases, gains, shifts, w_up, up_bias, w_down = params
    head_count = proj_bias.shape[1]
    head_dim = proj_bias.shape[2]
    score_scale = head_dim ** (-0.5)
    seq_len = tokens.shape[0]
    queries = low_back(low(product(tokens, w_proj[0]) + proj_bias[0].reshape(-1)))
    keys_all = low_back(low(product(tokens, w_proj[1])))
    values_all = low_back(low(product(tokens, w_proj[2]) + proj_bias[1].reshape(-1)))
    key_heads = keys_all.reshape(seq_len, head_count, head_dim)
    value_heads = values_all.reshape(seq_len, head_count, head_dim)
    block_rows = 512 if seq_len % 512 == 0 else seq_len
    query_blocks = queries.reshape(seq_len // block_rows, block_rows, head_count, head_dim)

    def attend(query_block):
        scores = low_back(score_scale * jnp.einsum('qhd,khd->hqk', query_block, key_heads, precision=lax.Precision.HIGHEST))
        scores = jnp.where(key_mask[None, None, :], scores, masked_value)
        highest = lax.optimization_barrier(jnp.max(scores, axis=-1, keepdims=True))
        log_total = highest + jnp.log(lax.optimization_barrier(jnp.sum(jnp.exp(scores - highest), axis=-1, keepdims=True)))
        weights_low = low(jnp.exp(scores - log_total))
        return jnp.einsum('hqk,khd->qhd', weights_low, value_heads, precision=lax.Precision.HIGHEST)
    attended = lax.map(jax.checkpoint(attend), query_blocks)
    attended = low_back(low(attended.reshape(seq_len, head_count * head_dim)))
    branch = low_back(product(attended, w_back) + branch_biases[0])
    first_norm = norm_rows(tokens + branch, gains[0], shifts[0])
    hidden_pre = low_back(product(low(first_norm), w_up) + up_bias)
    activated = low(jax.nn.gelu(hidden_pre, approximate=False))
    second_branch = low_back(product(activated, w_down) + branch_biases[1])
    return norm_rows(first_norm + second_branch, gains[1], shifts[1])

def reference(hidden_in, lengths, out_grad, w_qkv, qv_bias, w_out, out_biases, norm_gains, norm_biases, w_in, ffn_bias, w_ffo):
    params = tuple((weight_array.astype(jnp.float32) for weight_array in (w_qkv, qv_bias, w_out, out_biases, norm_gains, norm_biases, w_in, ffn_bias, w_ffo)))
    seq_len = hidden_in.shape[1]
    positions = lax.iota(jnp.int32, seq_len)

    def one_slot(totals, slot_items):
        tokens, length, cotangent = slot_items
        key_mask = positions < length
        output, pullback = jax.vjp(lambda token_rows, weights: encoder_layer(token_rows, key_mask, weights), tokens.astype(jnp.float32), params)
        grad_rows, grad_params = pullback(cotangent.astype(jnp.float32) * key_mask[:, None].astype(jnp.float32))
        totals = jax.tree.map(jnp.add, totals, grad_params)
        return (totals, (output.astype(jnp.bfloat16), grad_rows.astype(jnp.bfloat16)))
    zero_grads = jax.tree.map(jnp.zeros_like, params)
    totals, outputs = lax.scan(one_slot, zero_grads, (hidden_in, lengths, out_grad))
    return (outputs[0], outputs[1], totals[0], totals[1], totals[2], totals[3], totals[4], totals[5], totals[6], totals[7], totals[8])
```

```python
import functools

import jax
import jax.numpy as jnp
from jax import lax
from jax.experimental import pallas as pl
from jax.experimental.pallas import tpu as pltpu
from jax.sharding import PartitionSpec as P

f32 = jnp.float32
bf16 = jnp.bfloat16
MESH = pl.DeviceIdType.MESH
ANY = pl.BlockSpec(memory_space=pl.ANY)
VM = pl.BlockSpec(memory_space=pltpu.VMEM)
SM = pl.BlockSpec(memory_space=pltpu.SMEM)
DMA = pltpu.SemaphoreType.DMA
NN = (((1,), (0,)), ((), ()))
NT = (((1,), (1,)), ((), ()))
TN = (((0,), (0,)), ((), ()))
VMEM_BYTES = 60 << 20


def dot(left, right, dims=NN):
    return lax.dot_general(left, right, dims, preferred_element_type=f32)


def struct(shape, dtype):
    return jax.ShapeDtypeStruct(shape, dtype)


def place():
    z, c, t = lax.axis_index("fsdp"), lax.axis_index("ctx"), lax.axis_index("tp")
    along_x = c + 1 - 2 * (c % 2)
    along_y = c + 2 - 4 * (c // 2)
    n1 = along_x + t * (along_y - along_x)
    n2 = along_y + t * (along_x - along_y)
    return z, c, t, n1, n2, 3 - c


def remote(src, dst, send_sem, recv_sem, device):
    return pltpu.make_async_remote_copy(
        src_ref=src,
        dst_ref=dst,
        send_sem=send_sem,
        recv_sem=recv_sem,
        device_id=device,
        device_id_type=MESH,
    )


def meet(devices):
    barrier = pltpu.get_barrier_semaphore()
    for device in devices:
        pl.semaphore_signal(barrier, inc=1, device_id=device, device_id_type=MESH)
    pl.semaphore_wait(barrier, len(devices))


def tile(i, size):
    return pl.ds(pl.multiple_of(i * size, size), size)


def gather_kernel(
    x_in, og_in, qkv_in, out_in, up_in, down_in, small_in,
    xs, ogs, qkv, wout, wup, wdown, small,
    loc, xsend, xrecv, osend, orecv, fsend, frecv, zsend, zrecv, asend, arecv, bsend, brecv, csend, crecv,
):
    z, c, t, n1, n2, dg = place()
    half = 128
    planes = (n1, n2, dg)
    meet(
        [(z, p, t) for p in planes]
        + [((z + d) % 4, c, t) for d in (1, 2, 3)]
        + [(z, c, 1 - t)]
    )

    def region(w, zz, q):
        if w == 0:
            return qkv.at[:, pl.ds(pl.multiple_of(zz * 192 + q * 48, 16), 48), :]
        if w == 1:
            return wout.at[zz, tile(q, 96), :]
        if w == 2:
            return wup.at[zz, tile(q, 192), :]
        if w == 3:
            return wdown.at[zz, tile(q, 96), :]
        return small.at[zz]

    def mine(w):
        if w == 0:
            return qkv_in.at[:, tile(c, 48), :]
        if w == 1:
            return out_in.at[tile(c, 96), :]
        if w == 2:
            return up_in.at[tile(c, 192), :]
        if w == 3:
            return down_in.at[tile(c, 96), :]
        return small_in

    pending = []
    xcopies = []
    for i, p in enumerate(planes):
        cp = remote(x_in.at[p, tile(t, half), :], xs.at[t, c], xsend.at[i], xrecv.at[i], (z, p, t))
        cp.start()
        xcopies.append(cp)
    zcopies = {}

    def send_z(w):
        for d in (1, 2, 3):
            cp = remote(mine(w), region(w, z, c), zsend.at[w, d - 1], zrecv.at[w, d - 1], ((z + d) % 4, c, t))
            cp.start()
            zcopies[w, d] = cp

    send_z(0)
    send_z(4)
    send_z(1)
    send_z(2)
    send_z(3)
    local = [
        pltpu.make_async_copy(x_in.at[c, pl.ds(0, half), :], xs.at[0, c], loc.at[0]),
        pltpu.make_async_copy(x_in.at[c, pl.ds(half, half), :], xs.at[1, c], loc.at[1]),
        pltpu.make_async_copy(og_in.at[c, tile(t, half), :], ogs.at[c], loc.at[2]),
        pltpu.make_async_copy(qkv_in, qkv.at[:, tile(z, 192), :], loc.at[3]),
        pltpu.make_async_copy(out_in, wout.at[z], loc.at[4]),
        pltpu.make_async_copy(up_in, wup.at[z], loc.at[5]),
        pltpu.make_async_copy(down_in, wdown.at[z], loc.at[6]),
        pltpu.make_async_copy(small_in, small.at[z], loc.at[7]),
    ]
    for cp in local:
        cp.start()

    def spread(w):
        for d in (1, 2, 3):
            zcopies[w, d].wait_recv()
            zz = (z + 4 - d) % 4
            a = remote(region(w, zz, c), region(w, zz, c), asend.at[w, d - 1], arecv.at[w, d - 1], (z, n1, t))
            b = remote(region(w, zz, c), region(w, zz, c), bsend.at[w, d - 1], brecv.at[w, d - 1], (z, n2, t))
            a.start()
            b.start()
            pending.append((w, d, a, b))

    ccopies = []

    def finish(w):
        for w_, d, a, b in pending:
            if w_ == w:
                a.wait_recv()
                zz = (z + 4 - d) % 4
                cc = remote(region(w, zz, n1), region(w, zz, n1), csend.at[w, d - 1], crecv.at[w, d - 1], (z, n2, t))
                cc.start()
                ccopies.append(cc)

    spread(0)
    forwards = []
    for i, p in enumerate(planes):
        xcopies[i].wait_recv()
        cp = remote(xs.at[t, p], xs.at[t, p], fsend.at[i], frecv.at[i], (z, c, 1 - t))
        cp.start()
        forwards.append(cp)
    spread(1)
    finish(0)
    spread(2)
    finish(1)
    spread(3)
    finish(2)
    ocopies = []
    for i, p in enumerate(planes):
        cp = remote(og_in.at[p, tile(t, half), :], ogs.at[c], osend.at[i], orecv.at[i], (z, p, t))
        cp.start()
        ocopies.append(cp)
    finish(3)
    for cp in local:
        cp.wait()
    for cp in xcopies:
        cp.wait_send()
    for cp in ocopies + forwards:
        cp.wait()
    for (w, d), cp in zcopies.items():
        cp.wait_send()
        if w == 4:
            cp.wait_recv()
    for w, d, a, b in pending:
        a.wait_send()
        b.wait()
    for cp in ccopies:
        cp.wait()


def gather(x, og, w_qkv, w_out, w_in, w_ffo, small):
    return pl.pallas_call(
        gather_kernel,
        out_shape=(
            struct((2, 4, 128, 768), bf16),
            struct((4, 128, 768), bf16),
            struct((3, 768, 384), bf16),
            struct((4, 384, 192), bf16),
            struct((4, 768, 384), bf16),
            struct((4, 384, 768), bf16),
            struct((4, 16, 384), f32),
        ),
        in_specs=[ANY] * 7,
        out_specs=[ANY] * 7,
        scratch_shapes=[
            DMA((8,)), DMA((3,)), DMA((3,)), DMA((3,)), DMA((3,)), DMA((3,)), DMA((3,)),
            DMA((5, 3)), DMA((5, 3)), DMA((4, 3)), DMA((4, 3)), DMA((4, 3)), DMA((4, 3)), DMA((4, 3)), DMA((4, 3)),
        ],
        compiler_params=pltpu.CompilerParams(collective_id=0, has_side_effects=True),
        name="gather",
    )(x, og, w_qkv, w_out, w_in, w_ffo, small)


def split3(v):
    hi = v.astype(bf16).astype(f32)
    rest = v - hi
    mid = rest.astype(bf16).astype(f32)
    return hi, mid, rest - mid


def key_bias(length, rows):
    r = lax.broadcasted_iota(jnp.int32, (rows, 128), 0)
    position = (r % 512) // 128 * 256 + r // 512 * 128 + r % 128
    return jnp.where(position < length, 0.0, -1e30)


def attend_forward(q_ref, k_ref, v_ref, kb, out_ref, lse_ref, qe, ke, ve, block):
    rows_all = q_ref.shape[0]
    lane = lax.broadcasted_iota(jnp.int32, (rows_all, 128), 1)
    lse_ref[...] = jnp.zeros_like(lse_ref)

    def pair(hp, _):
        cols = tile(hp, 128)
        q, k, v = q_ref[:, cols].astype(f32), k_ref[:, cols].astype(f32), v_ref[:, cols].astype(f32)
        for j in range(2):
            own = (lane < 64) if j == 0 else (lane >= 64)
            e = 64 if j == 0 else 0
            one = jnp.where(lane == e, 1.0, 0.0)
            qe[j] = jnp.where(own, q, one).astype(bf16)
            ke[j] = jnp.where(own, k, jnp.where(lane == e, kb, 0.0)).astype(bf16)
            ve[j] = jnp.where(own, v, one).astype(bf16)

        def query_block(b, _):
            rows = tile(b, block)
            ln = lax.broadcasted_iota(jnp.int32, (block, 128), 1)
            outs, totals = [], []
            for j in range(2):
                e = 64 if j == 0 else 0
                s = dot(qe[j, rows, :], ke[j], NT)
                m = jnp.max(s, axis=1, keepdims=True)
                p = jnp.exp(s - m).astype(bf16)
                o = dot(p, ve[j])
                total = o[:, e : e + 1]
                outs.append(o * (1.0 / total))
                totals.append(m + jnp.log(total))
            out_ref[rows, cols] = jnp.where(ln < 64, outs[0], outs[1]).astype(bf16)
            cur = lse_ref[rows, :]
            cur = jnp.where(ln == 2 * hp, totals[0], cur)
            lse_ref[rows, :] = jnp.where(ln == 2 * hp + 1, totals[1], cur)
            return 0

        lax.fori_loop(0, rows_all // block, query_block, 0)
        return 0

    lax.fori_loop(0, q_ref.shape[1] // 128, pair, 0)


def attend_backward(
    q_ref, k_ref, v_ref, kb, mixed_ref, do_ref, lse_ref, dq_ref, dk_ref, dv_ref, qe, ke, ve, de, qz, dz, kt, dqt, block
):
    rows_all = q_ref.shape[0]
    lane = lax.broadcasted_iota(jnp.int32, (rows_all, 128), 1)

    def pair(hp, _):
        cols = tile(hp, 128)
        q, k, v = q_ref[:, cols].astype(f32), k_ref[:, cols].astype(f32), v_ref[:, cols].astype(f32)
        do = do_ref[:, cols].astype(f32)
        pr = do * mixed_ref[:, cols].astype(f32)
        lse_all = lse_ref[...]
        for j in range(2):
            own = (lane < 64) if j == 0 else (lane >= 64)
            e = 64 if j == 0 else 0
            delta = jnp.sum(jnp.where(own, pr, 0.0), axis=1, keepdims=True)
            lse = jnp.sum(jnp.where(lane == 2 * hp + j, lse_all, 0.0), axis=1, keepdims=True)
            lh, lm, ll = split3(-lse)
            dh, dm, dl = split3(-delta)
            qz[j] = jnp.where(own, q, 0.0).astype(bf16)
            dz[j] = jnp.where(own, do, 0.0).astype(bf16)
            side = jnp.where(lane == e, 1.0, 0.0)
            side = jnp.where(lane == e + 1, lh, side)
            side = jnp.where(lane == e + 2, lm, side)
            side = jnp.where(lane == e + 3, ll, side)
            qe[j] = jnp.where(own, q, side).astype(bf16)
            ones3 = jnp.where((lane > e) & (lane < e + 4), 1.0, 0.0)
            ke[j] = jnp.where(own, k, jnp.where(lane == e, kb, ones3)).astype(bf16)
            side = jnp.where(lane == e + 1, dh, 0.0)
            side = jnp.where(lane == e + 2, dm, side)
            side = jnp.where(lane == e + 3, dl, side)
            de[j] = jnp.where(own, do, side).astype(bf16)
            ve[j] = jnp.where(own, v, ones3).astype(bf16)
        kt[...] = k.T.astype(bf16)
        dqt[...] = jnp.zeros_like(dqt)

        def key_block(b, _):
            rows = tile(b, block)
            dv, dk = None, None
            for j in range(2):
                p = jnp.exp(dot(ke[j, rows, :], qe[j], NT))
                g = dot(ve[j, rows, :], de[j], NT)
                ds = (p * g).astype(bf16)
                a = dot(p.astype(bf16), dz[j])
                b_ = dot(ds, qz[j])
                dv = a if dv is None else dv + a
                dk = b_ if dk is None else dk + b_
                dqt[64 * j : 64 * j + 64, :] += dot(kt[64 * j : 64 * j + 64, rows], ds)
            dk_ref[rows, cols] = dk.astype(bf16)
            dv_ref[rows, cols] = dv.astype(bf16)
            return 0

        lax.fori_loop(0, rows_all // block, key_block, 0)
        dq_ref[:, cols] = (dqt[...] * 0.125).T.astype(bf16)
        return 0

    lax.fori_loop(0, q_ref.shape[1] // 128, pair, 0)


def forward_kernel(len_ref, xs, wqkv, bias, q_ref, k_ref, v_ref, mixed, lse, qe, ke, ve):
    c = lax.axis_index("ctx")

    def project(i, _):
        rows = tile(i, 256)
        xr = xs[rows, :]
        q_ref[rows, :] = ((dot(xr, wqkv[0]) + bias[0:1, :]).astype(bf16).astype(f32) * 0.125).astype(bf16)
        k_ref[rows, :] = dot(xr, wqkv[1]).astype(bf16)
        v_ref[rows, :] = (dot(xr, wqkv[2]) + bias[1:2, :]).astype(bf16)
        return 0

    lax.fori_loop(0, 4, project, 0)
    attend_forward(q_ref, k_ref, v_ref, key_bias(len_ref[c], 1024), mixed, lse, qe, ke, ve, 512)


def forward(lengths, xs, wqkv, bias):
    return pl.pallas_call(
        forward_kernel,
        out_shape=(struct((1024, 384), bf16),) * 4 + (struct((1024, 128), f32),),
        in_specs=[SM, VM, VM, VM],
        scratch_shapes=[pltpu.VMEM((2, 1024, 128), bf16)] * 3,
        compiler_params=pltpu.CompilerParams(vmem_limit_bytes=VMEM_BYTES),
        name="attention_forward",
    )(lengths, xs, wqkv, bias)


def backward_kernel(
    len_ref, xs, wqkv, q_ref, k_ref, v_ref, mixed, gmixed, lse, gres,
    dxown, dxother, gqkv, gbias, dq, dk, dv, qe, ke, ve, de, qz, dz, kt, dqt,
):
    c, t = lax.axis_index("ctx"), lax.axis_index("tp")
    attend_backward(
        q_ref, k_ref, v_ref, key_bias(len_ref[c], 1024), mixed, gmixed, lse, dq, dk, dv, qe, ke, ve, de, qz, dz, kt, dqt, 512
    )

    def rows_back(i, _):
        h = (i // 2 + 1 - t) % 2
        rows = pl.ds(pl.multiple_of(h * 512 + i % 2 * 256, 256), 256)
        part = dot(dq[rows, :], wqkv[0], NT) + dot(dk[rows, :], wqkv[1], NT) + dot(dv[rows, :], wqkv[2], NT)

        @pl.when(i < 2)
        def _():
            dxother[tile(i % 2, 256), :] = part

        @pl.when(i >= 2)
        def _():
            dxown[tile(i % 2, 256), :] = part + gres[tile(i % 2, 256), :]

        return 0

    lax.fori_loop(0, 4, rows_back, 0)

    def weights(i, _):
        xr = xs[:, tile(i, 128)]
        for p, g in enumerate((dq, dk, dv)):
            gqkv[p, tile(i, 128), :] = dot(xr, g[...], TN).astype(bf16)
        return 0

    lax.fori_loop(0, 6, weights, 0)
    gbias[...] = jnp.zeros_like(gbias)
    gbias[0:1, :] = jnp.sum(dq[...].astype(f32), axis=0, keepdims=True)
    gbias[1:2, :] = jnp.sum(dv[...].astype(f32), axis=0, keepdims=True)


def backward(lengths, xs, wqkv, q, k, v, mixed, gmixed, lse, gres):
    half = pltpu.VMEM((2, 1024, 128), bf16)
    return pl.pallas_call(
        backward_kernel,
        out_shape=(struct((512, 768), f32), struct((512, 768), f32), struct((3, 768, 384), bf16), struct((8, 384), f32)),
        in_specs=[SM] + [VM] * 9,
        scratch_shapes=[pltpu.VMEM((1024, 384), bf16)] * 3
        + [half] * 6
        + [pltpu.VMEM((128, 1024), bf16), pltpu.VMEM((128, 1024), f32)],
        compiler_params=pltpu.CompilerParams(vmem_limit_bytes=VMEM_BYTES),
        name="attention_backward",
    )(lengths, xs, wqkv, q, k, v, mixed, gmixed, lse, gres)


def gelu_pair(h):
    cdf = 0.5 * (1.0 + lax.erf(h * 0.7071067811865476))
    density = jnp.exp(h * h * -0.5) * 0.3989422804014327
    return h * cdf, cdf + h * density


def unit_rows(r):
    centred = r - jnp.mean(r, axis=-1, keepdims=True)
    spread = jnp.mean(centred * centred, axis=-1, keepdims=True)
    inverse = lax.rsqrt(spread + 1e-5)
    return centred * inverse, inverse


def norm_back(g, n, inverse):
    return inverse * (g - jnp.mean(g, axis=-1, keepdims=True) - n * jnp.mean(g * n, axis=-1, keepdims=True))


def column_sum(v):
    return jnp.sum(v, axis=0, keepdims=True)


def middle_kernel(
    len_ref, mixed, xs, ogs, wout4, wup, wdown, rowp, upb,
    hout, gres, gmixed, gup, gdown, gout, grow, gupb,
    wout, part, parta, partb, partc, recva, recvb, recvc, n1r, n2r, inv1, inv2, low1, low2, low3, act, slope, ghid, g2r,
    send, recv,
):
    c, t = lax.axis_index("ctx"), lax.axis_index("tp")
    z = lax.axis_index("fsdp")
    sibling = (z, c, 1 - t)
    meet([sibling])
    u = 1 - t
    copies = []

    def exchange(stage, i, src, dst):
        cp = remote(src, dst, send.at[stage, i], recv.at[stage, i], sibling)
        cp.start()
        copies.append(cp)
        return cp

    for j in range(4):
        spot = lax.broadcasted_iota(jnp.int32, (192, 768), 1) == lax.broadcasted_iota(jnp.int32, (192, 768), 0) + 192 * j
        piece = dot(wout4[j], jnp.where(spot, 1.0, 0.0).astype(bf16))
        if j == 0:
            part[...] = piece
        else:
            part[...] += piece
    wout[...] = part[...].astype(bf16)
    bias0, bias1 = rowp[0:1, :], rowp[1:2, :]
    gain0, gain1 = rowp[2:3, :], rowp[3:4, :]
    shift0, shift1 = rowp[4:5, :], rowp[5:6, :]

    def rows_of(h, i):
        return pl.ds(pl.multiple_of(h * 512 + i * 256, 256), 256)

    a = []
    for i in range(2):
        parta[i] = dot(mixed[rows_of(u, i), :], wout[...])
        a.append(exchange(0, i, parta.at[i], recva.at[i]))
    for i in range(2):
        parta[2 + i] = dot(mixed[rows_of(t, i), :], wout[...])
    b = []
    for i in range(2):
        a[i].wait_recv()
        r = xs[rows_of(t, i), :].astype(f32) + (parta[2 + i] + recva[i] + bias0)
        n, inverse = unit_rows(r)
        n1r[i] = n
        inv1[i] = jnp.broadcast_to(inverse, (256, 128))
        low1[t, i] = (n * gain0 + shift0).astype(bf16)
        b.append(exchange(1, i, low1.at[t, i], low1.at[t, i]))

    def up(h, i):
        def chunk(zz, _):
            hidden = dot(low1[h, i], wup[zz]) + upb[pl.ds(zz, 1), :]
            value, grad = gelu_pair(hidden)
            act[zz, rows_of(h, i), :] = value.astype(bf16)
            slope[zz, rows_of(h, i), :] = grad.astype(bf16)
            return 0

        lax.fori_loop(0, 4, chunk, 0)

    up(t, 0)
    up(t, 1)
    b[0].wait_recv()
    up(u, 0)
    b[1].wait_recv()
    up(u, 1)

    def down(h, i, target):
        rows = rows_of(h, i)
        total = dot(act[0, rows, :], wdown[0])
        for zz in range(1, 4):
            total += dot(act[zz, rows, :], wdown[zz])
        target[...] = total

    a = []
    for i in range(2):
        down(u, i, partb.at[i])
        a.append(exchange(2, i, partb.at[i], recvb.at[i]))
    for i in range(2):
        down(t, i, partb.at[2 + i])
    b = []
    gg1 = gs1 = gb1 = 0.0
    for i in range(2):
        a[i].wait_recv()
        n, inverse = unit_rows((n1r[i] * gain0 + shift0) + (partb[2 + i] + recvb[i] + bias1))
        hout[pl.ds(256 * i, 256), :] = (n * gain1 + shift1).astype(bf16)
        r = lax.broadcasted_iota(jnp.int32, (256, 768), 0) + 256 * i
        live = (r // 128 * 256 + t * 128 + r % 128) < len_ref[c]
        g = jnp.where(live, ogs[pl.ds(256 * i, 256), :].astype(f32), 0.0)
        gg1 = gg1 + column_sum(g * n)
        gs1 = gs1 + column_sum(g)
        g2 = norm_back(g * gain1, n, inverse)
        g2r[i] = g2
        low2[t, i] = g2.astype(bf16)
        b.append(exchange(3, i, low2.at[t, i], low2.at[t, i]))
        gb1 = gb1 + column_sum(low2[t, i].astype(f32))

    gupb[...] = jnp.zeros_like(gupb)

    def back(h, i):
        def chunk(zz, _):
            rows = rows_of(h, i)
            g = (dot(low2[h, i], wdown[zz], NT) * slope[zz, rows, :].astype(f32)).astype(bf16)
            ghid[zz, rows, :] = g
            gupb[pl.ds(zz, 1), :] += column_sum(g.astype(f32))
            return 0

        lax.fori_loop(0, 4, chunk, 0)

    back(t, 0)
    back(t, 1)
    b[0].wait_recv()
    back(u, 0)
    b[1].wait_recv()
    back(u, 1)

    def first_grad(h, i, target):
        rows = rows_of(h, i)
        total = dot(ghid[0, rows, :], wup[0], NT)
        for zz in range(1, 4):
            total += dot(ghid[zz, rows, :], wup[zz], NT)
        target[...] = total

    a = []
    for i in range(2):
        first_grad(u, i, partc.at[i])
        a.append(exchange(4, i, partc.at[i], recvc.at[i]))
    for i in range(2):
        first_grad(t, i, partc.at[2 + i])
    b = []
    gg0 = gs0 = gb0 = 0.0
    for i in range(2):
        a[i].wait_recv()
        g1 = g2r[i] + (partc[2 + i] + recvc[i])
        n = n1r[i]
        gg0 = gg0 + column_sum(g1 * n)
        gs0 = gs0 + column_sum(g1)
        g = norm_back(g1 * gain0, n, inv1[i][:, 0:1])
        gres[pl.ds(256 * i, 256), :] = g
        low3[t, i] = g.astype(bf16)
        b.append(exchange(5, i, low3.at[t, i], low3.at[t, i]))
        gb0 = gb0 + column_sum(low3[t, i].astype(f32))
    for k, v in enumerate((gb0, gb1, gg0, gg1, gs0, gs1)):
        grow[k : k + 1, :] = v
    grow[6:8, :] = jnp.zeros((2, 768), f32)

    def weights(zz, _):
        for k in range(3):
            down_rows = pl.ds(128 * k, 128)
            g = dot(act[zz, :, down_rows], low2[...].reshape(1024, 768), TN)
            gdown[zz, down_rows, :] = g.astype(bf16)
        for k in range(6):
            up_rows = pl.ds(128 * k, 128)
            g = dot(low1[:, :, :, up_rows].reshape(1024, 128), ghid[zz], TN)
            gup[zz, up_rows, :] = g.astype(bf16)
        return 0

    lax.fori_loop(0, 4, weights, 0)
    b[0].wait_recv()
    b[1].wait_recv()
    for h in range(2):
        for i in range(2):
            gmixed[rows_of(h, i), :] = dot(low3[h, i], wout[...], NT).astype(bf16)
    for k in range(3):
        mixed_rows = pl.ds(128 * k, 128)
        part[mixed_rows, :] = dot(mixed[:, mixed_rows], low3[...].reshape(1024, 768), TN)
    for j in range(4):
        gout[j] = part[:, 192 * j : 192 * j + 192].astype(bf16)
    for cp in copies:
        cp.wait_send()


def middle(lengths, mixed, xs, ogs, wout4, wup, wdown, rowp, upb):
    rows2 = pltpu.VMEM((2, 256, 768), f32)
    low = pltpu.VMEM((2, 2, 256, 768), bf16)
    wide = pltpu.VMEM((4, 1024, 384), bf16)
    return pl.pallas_call(
        middle_kernel,
        out_shape=(
            struct((512, 768), bf16),
            struct((512, 768), f32),
            struct((1024, 384), bf16),
            struct((4, 768, 384), bf16),
            struct((4, 384, 768), bf16),
            struct((4, 384, 192), bf16),
            struct((8, 768), f32),
            struct((4, 384), f32),
        ),
        in_specs=[SM] + [VM] * 8,
        scratch_shapes=[
            pltpu.VMEM((384, 768), bf16),
            pltpu.VMEM((384, 768), f32),
            pltpu.VMEM((4, 256, 768), f32), pltpu.VMEM((4, 256, 768), f32), pltpu.VMEM((4, 256, 768), f32),
            rows2, rows2, rows2, rows2, rows2,
            pltpu.VMEM((2, 256, 128), f32), pltpu.VMEM((2, 256, 128), f32),
            low, low, low, wide, wide, wide, rows2,
            DMA((6, 2)), DMA((6, 2)),
        ],
        compiler_params=pltpu.CompilerParams(collective_id=1, has_side_effects=True, vmem_limit_bytes=VMEM_BYTES),
        name="rows",
    )(lengths, mixed, xs, ogs, wout4, wup, wdown, rowp, upb)


def reduce_kernel(
    gqkv, gout, gup, gdown, gsmall, hout, dxown, dxother,
    oqkv, oout, oup, odown, osmall, oh, odx,
    r0, r1, r2, r3, s0, s1, s2, s3, z0, z1, z2, z3, sms, sm, smt, smr, smc, dxr, dxl,
    lsem, s1s, s1r, s2s, s2r, s3s, s3r, s4s, s4r, ms, mr, hs, hr, fs, fr,
):
    z, c, t, n1, n2, dg = place()
    sibling = (z, c, 1 - t)
    planes = (n1, n2, dg)
    meet([(z, p, t) for p in planes] + [((z + d) % 4, c, t) for d in (1, 2, 3)] + [sibling])
    grads = (gqkv, gout, gup, gdown)
    outs = (oqkv, oout, oup, odown)
    first = (r0, r1, r2, r3)
    second = (s0, s1, s2, s3)
    third = (z0, z1, z2, z3)
    quarter_rows = (48, 96, 192, 96)
    order = (3, 2, 1, 0)
    sends = []

    def go(src, dst, ss, rs, device):
        cp = remote(src, dst, ss, rs, device)
        cp.start()
        sends.append(cp)
        return cp

    def grad(w, q):
        rows = tile(q, quarter_rows[w])
        return grads[w].at[:, :, rows, :] if w == 0 else grads[w].at[:, rows, :]

    def shard(w, ref, zz):
        return ref.at[:, zz] if w == 0 else ref.at[zz]

    def out(w, q):
        rows = tile(q, quarter_rows[w])
        return outs[w].at[:, rows, :] if w == 0 else outs[w].at[rows, :]

    xch = go(dxother, dxr, ms.at[0], mr.at[0], sibling)
    xsm = go(gsmall, sms, ms.at[1], mr.at[1], sibling)
    stage1 = {}
    for w in order:
        stage1[w] = [
            go(grad(w, n1), first[w].at[0], s1s.at[w, 0], s1r.at[w, 0], (z, n1, t)),
            go(grad(w, dg), first[w].at[1], s1s.at[w, 1], s1r.at[w, 1], (z, n1, t)),
        ]
    hcopies = [go(hout.at[p], oh.at[c, tile(t, 128), :], hs.at[0, i], hr.at[0, i], (z, p, t)) for i, p in enumerate(planes)]
    local = [pltpu.make_async_copy(hout.at[c], oh.at[c, tile(t, 128), :], lsem.at[0])]
    local[0].start()
    selfs = [go(hout.at[c], oh.at[c, tile(t, 128), :], hs.at[0, 3], hr.at[0, 3], sibling)]
    xch.wait_recv()
    dxl[...] = (dxown[...] + dxr[...]).astype(bf16)
    dcopies = [go(dxl.at[p], odx.at[c, tile(t, 128), :], hs.at[1, i], hr.at[1, i], (z, p, t)) for i, p in enumerate(planes)]
    local.append(pltpu.make_async_copy(dxl.at[c], odx.at[c, tile(t, 128), :], lsem.at[1]))
    local[1].start()
    selfs.append(go(dxl.at[c], odx.at[c, tile(t, 128), :], hs.at[1, 3], hr.at[1, 3], sibling))
    xsm.wait_recv()
    shared = lax.broadcasted_iota(jnp.int32, (4, 16, 384), 1) < 6
    sm[...] = gsmall[...] + jnp.where(shared, sms[...], 0.0)
    small1 = [go(sm.at[(z + d) % 4], smr.at[d], ms.at[1 + d], mr.at[1 + d], ((z + d) % 4, c, t)) for d in (1, 2, 3)]
    stage2 = {}
    for w in order:
        stage1[w][1].wait_recv()
        first[w][1] = (grad(w, n2)[...].astype(f32) + first[w][1].astype(f32)).astype(bf16)
        stage2[w] = go(first[w].at[1], second[w].at[1], s2s.at[w], s2r.at[w], (z, n2, t))
        stage1[w][0].wait_recv()
        second[w][0] = (grad(w, c)[...].astype(f32) + first[w][0].astype(f32)).astype(bf16)
    for cp in small1:
        cp.wait_recv()
    smt[...] = (sm[z] + smr[1]) + (smr[2] + smr[3])
    small2 = [go(smt, smc.at[i], ms.at[5 + i], mr.at[5 + i], (z, p, t)) for i, p in enumerate(planes)]
    stage3 = {}
    for w in order:
        stage2[w].wait_recv()
        second[w][0] = (second[w][0].astype(f32) + second[w][1].astype(f32)).astype(bf16)
        stage3[w] = [
            go(
                shard(w, second[w].at[0], (z + d) % 4), third[w].at[d - 1],
                s3s.at[w, d - 1], s3r.at[w, d - 1], ((z + d) % 4, c, t),
            )
            for d in (1, 2, 3)
        ]
    fcopies = []
    for i, p in enumerate(planes):
        hcopies[i].wait_recv()
        fcopies.append(go(oh.at[p, tile(t, 128), :], oh.at[p, tile(t, 128), :], fs.at[0, i], fr.at[0, i], sibling))
        dcopies[i].wait_recv()
        fcopies.append(go(odx.at[p, tile(t, 128), :], odx.at[p, tile(t, 128), :], fs.at[1, i], fr.at[1, i], sibling))
    stage4 = []
    across = {}
    for w in order:
        for cp in stage3[w]:
            cp.wait_recv()
        mine = shard(w, second[w].at[0], z)[...].astype(f32)
        v = (mine + third[w][0].astype(f32)) + (third[w][1].astype(f32) + third[w][2].astype(f32))
        out(w, c)[...] = v.astype(bf16)
        across[w] = go(out(w, c), out(w, c), s4s.at[w, 0], s4r.at[w, 0], (z, n1, t))
        stage4.append(go(out(w, c), out(w, c), s4s.at[w, 1], s4r.at[w, 1], (z, n2, t)))
    for w in order:
        across[w].wait_recv()
        stage4.append(go(out(w, n1), out(w, n1), s4s.at[w, 2], s4r.at[w, 2], (z, n2, t)))
    for cp in small2:
        cp.wait_recv()
    osmall[...] = (smt[...] + smc[0]) + (smc[1] + smc[2])
    for cp in fcopies + stage4 + selfs:
        cp.wait_recv()
    for cp in local:
        cp.wait()
    for cp in sends:
        cp.wait_send()


def reduce(gqkv, gout, gup, gdown, gsmall, hout, dxown, dxother):
    quarters = ((3, 4, 48, 384), (4, 96, 192), (4, 192, 384), (4, 96, 768))
    shards = ((3, 48, 384), (96, 192), (192, 384), (96, 768))
    return pl.pallas_call(
        reduce_kernel,
        out_shape=(
            struct((3, 192, 384), bf16),
            struct((384, 192), bf16),
            struct((768, 384), bf16),
            struct((384, 768), bf16),
            struct((16, 384), f32),
            struct((4, 256, 768), bf16),
            struct((4, 256, 768), bf16),
        ),
        in_specs=[VM] * 8,
        out_specs=(VM,) * 5 + (ANY, ANY),
        scratch_shapes=[pltpu.VMEM((2,) + q, bf16) for q in quarters] * 2
        + [pltpu.VMEM((3,) + s, bf16) for s in shards]
        + [
            pltpu.VMEM((4, 16, 384), f32), pltpu.VMEM((4, 16, 384), f32), pltpu.VMEM((16, 384), f32),
            pltpu.VMEM((4, 16, 384), f32), pltpu.VMEM((3, 16, 384), f32),
            pltpu.VMEM((4, 128, 768), f32), pltpu.VMEM((4, 128, 768), bf16),
            DMA((2,)), DMA((4, 2)), DMA((4, 2)), DMA((4,)), DMA((4,)), DMA((4, 3)), DMA((4, 3)), DMA((4, 3)), DMA((4, 3)),
            DMA((8,)), DMA((8,)), DMA((2, 4)), DMA((2, 4)), DMA((2, 3)), DMA((2, 3)),
        ],
        compiler_params=pltpu.CompilerParams(collective_id=2, has_side_effects=True, vmem_limit_bytes=VMEM_BYTES),
        name="reduce",
    )(gqkv, gout, gup, gdown, gsmall, hout, dxown, dxother)


def pad_to(v, rows, columns):
    return jnp.pad(v, ((0, rows - v.shape[0]), (0, columns - v.shape[1])))


def per_slot(hidden_in, lengths, out_grad, w_qkv, qv_bias, w_out, out_biases, norm_gains, norm_biases, w_in, ffn_bias, w_ffo):
    small_in = jnp.concatenate(
        [
            pad_to(jnp.concatenate([out_biases, norm_gains, norm_biases], axis=0), 6, 384),
            pad_to(qv_bias.reshape(2, 96), 2, 384),
            ffn_bias.reshape(1, 384),
            jnp.zeros((7, 384), bf16),
        ],
        axis=0,
    ).astype(f32)
    xs, ogs, wqkv, wout4, wup, wdown, small = gather(hidden_in, out_grad, w_qkv, w_out, w_in, w_ffo, small_in)
    xs = xs.reshape(1024, 768)
    rowp = small[:, 0:6, 0:192].transpose(1, 0, 2).reshape(6, 768)
    bias = small[:, 6:8, 0:96].reshape(4, 2, 6, 16).transpose(1, 2, 0, 3).reshape(2, 384)
    upb = small[:, 8, :]
    q, k, v, mixed, lse = forward(lengths, xs, wqkv, bias)
    hout, gres, gmixed, gup, gdown, gout, grow, gupb = middle(
        lengths, mixed, xs, ogs.reshape(512, 768), wout4, wup, wdown, rowp, upb
    )
    dxown, dxother, gqkv, gbias = backward(lengths, xs, wqkv, q, k, v, mixed, gmixed, lse, gres)
    gsmall = jnp.concatenate(
        [
            jnp.pad(grow[0:6].reshape(6, 4, 192).transpose(1, 0, 2), ((0, 0), (0, 0), (0, 192))),
            jnp.pad(gbias[0:2].reshape(2, 6, 4, 16).transpose(2, 0, 1, 3).reshape(4, 2, 96), ((0, 0), (0, 0), (0, 288))),
            gupb[:, None, :],
            jnp.zeros((4, 7, 384), f32),
        ],
        axis=1,
    )
    oqkv, oout, oup, odown, osmall, oh, odx = reduce(
        gqkv.reshape(3, 4, 192, 384), gout, gup, gdown, gsmall,
        hout.reshape(4, 128, 768), dxown.reshape(4, 128, 768), dxother.reshape(4, 128, 768),
    )
    return (
        oh,
        odx,
        oqkv.astype(f32),
        osmall[6:8, 0:96].reshape(2, 6, 16),
        oout.astype(f32),
        osmall[0:2, 0:192],
        osmall[2:4, 0:192],
        osmall[4:6, 0:192],
        oup.astype(f32),
        osmall[8],
        odown.astype(f32),
    )


epsilon = 1e-05
masked_value = -1e30
heads_together = 2


def norm_rows(residual, gain_row, shift_row):
    centre = jnp.mean(residual, axis=-1, keepdims=True)
    centred = residual - centre
    spread = jnp.mean(centred * centred, axis=-1, keepdims=True)
    return centred * lax.rsqrt(spread + epsilon) * gain_row + shift_row


def gelu_exact(values):
    return jax.nn.gelu(values, approximate=False)


def split_heads(matrix, head_dim):
    return matrix.reshape(matrix.shape[0], matrix.shape[1] // head_dim, head_dim)


def block_scores(query_heads, key_heads, key_mask, score_scale):
    scores = (
        jnp.einsum("qhd,khd->hqk", query_heads, key_heads, preferred_element_type=jnp.float32)
        * score_scale
    )
    return jnp.where(key_mask[None, None, :], scores, masked_value)


def attend_slot(queries, key_value, length, score_scale, head_dim):
    gathered = lax.all_gather(key_value, "ctx", axis=1, tiled=True)
    seq_len = gathered.shape[1]
    key_mask = lax.iota(jnp.int32, seq_len) < length
    block_width = heads_together * head_dim
    outputs = []
    totals = []
    for head_block in range(queries.shape[1] // block_width):
        columns = slice(head_block * block_width, (head_block + 1) * block_width)
        query_heads = split_heads(queries[:, columns], head_dim)
        key_heads = split_heads(gathered[0][:, columns], head_dim)
        value_heads = split_heads(gathered[1][:, columns], head_dim)
        scores = block_scores(query_heads, key_heads, key_mask, score_scale)
        highest = jnp.max(scores, axis=-1, keepdims=True)
        log_total = highest + jnp.log(jnp.sum(jnp.exp(scores - highest), axis=-1, keepdims=True))
        weights_low = jnp.exp(scores - log_total).astype(jnp.bfloat16)
        attended = jnp.einsum(
            "hqk,khd->qhd", weights_low, value_heads, preferred_element_type=jnp.float32
        )
        outputs.append(attended.reshape(attended.shape[0], block_width))
        totals.append(log_total[:, :, 0])
    return (jnp.concatenate(outputs, axis=1).astype(jnp.bfloat16), jnp.concatenate(totals, axis=0))


def slot_grads(queries, key_value, length, grad_mixed, log_totals, score_scale, head_dim):
    gathered = lax.all_gather(key_value, "ctx", axis=1, tiled=True)
    seq_len = gathered.shape[1]
    key_mask = lax.iota(jnp.int32, seq_len) < length
    block_width = heads_together * head_dim
    query_grads = []
    key_grads = []
    value_grads = []
    inner_parts = []
    for head_block in range(queries.shape[1] // block_width):
        columns = slice(head_block * block_width, (head_block + 1) * block_width)
        heads_range = slice(head_block * heads_together, (head_block + 1) * heads_together)
        query_heads = split_heads(queries[:, columns], head_dim)
        key_heads = split_heads(gathered[0][:, columns], head_dim)
        value_heads = split_heads(gathered[1][:, columns], head_dim)
        grad_heads = split_heads(grad_mixed[:, columns], head_dim)
        scores = block_scores(query_heads, key_heads, key_mask, score_scale)
        softmax_rows = jnp.exp(scores - log_totals[heads_range, :, None])
        grad_weights = jnp.einsum(
            "qhd,khd->hqk", grad_heads, value_heads, preferred_element_type=jnp.float32
        )
        inner_sums = jnp.sum(softmax_rows * grad_weights, axis=-1)
        grad_scores = (softmax_rows * (grad_weights - inner_sums[:, :, None])).astype(jnp.bfloat16)
        grad_query = (
            jnp.einsum("hqk,khd->qhd", grad_scores, key_heads, preferred_element_type=jnp.float32)
            * score_scale
        )
        query_grads.append(grad_query.reshape(grad_query.shape[0], block_width))
        inner_parts.append(inner_sums)
        grad_key = (
            jnp.einsum("hqk,qhd->khd", grad_scores, query_heads, preferred_element_type=jnp.float32)
            * score_scale
        )
        grad_value = jnp.einsum(
            "hqk,qhd->khd",
            softmax_rows.astype(jnp.bfloat16),
            grad_heads,
            preferred_element_type=jnp.float32,
        )
        key_grads.append(grad_key.reshape(seq_len, block_width))
        value_grads.append(grad_value.reshape(seq_len, block_width))
    grad_queries = jnp.concatenate(query_grads, axis=1)
    key_terms = jnp.stack(
        [jnp.concatenate(key_grads, axis=1), jnp.concatenate(value_grads, axis=1)]
    )
    own_grads = lax.psum_scatter(
        key_terms.astype(jnp.bfloat16), "ctx", scatter_dimension=1, tiled=True
    ).astype(jnp.float32)
    return (grad_queries, own_grads)


def per_device(
    hidden_in,
    lengths,
    out_grad,
    w_qkv,
    qv_bias,
    w_out,
    out_biases,
    norm_gains,
    norm_biases,
    w_in,
    ffn_bias,
    w_ffo,
):
    w_proj, proj_bias, w_back, branch_biases, gains, shifts, w_up, up_bias, w_down = (
        lax.all_gather(w_qkv, "fsdp", axis=1, tiled=True),
        lax.all_gather(qv_bias, "fsdp", axis=2, tiled=True),
        lax.all_gather(w_out, "fsdp", axis=1, tiled=True),
        lax.all_gather(out_biases, "fsdp", axis=1, tiled=True),
        lax.all_gather(norm_gains, "fsdp", axis=1, tiled=True),
        lax.all_gather(norm_biases, "fsdp", axis=1, tiled=True),
        lax.all_gather(w_in, "fsdp", axis=1, tiled=True),
        lax.all_gather(ffn_bias, "fsdp", axis=0, tiled=True),
        lax.all_gather(w_ffo, "fsdp", axis=0, tiled=True),
    )
    slot_count, block_len, model_width = hidden_in.shape
    token_count = slot_count * block_len
    head_dim = proj_bias.shape[2]
    score_scale = head_dim ** (-0.5)
    local_width = w_proj.shape[2]
    contract_rows = (((0,), (0,)), ((), ()))
    contract_cols = (((1,), (1,)), ((), ()))
    bias_table = jnp.stack(
        [
            proj_bias[0].reshape(local_width).astype(jnp.float32),
            jnp.zeros((local_width,), jnp.float32),
            proj_bias[1].reshape(local_width).astype(jnp.float32),
        ]
    )
    projected = (
        jnp.einsum("sbd,pdc->spbc", hidden_in, w_proj, preferred_element_type=jnp.float32)
        + bias_table[None, :, None, :]
    ).astype(jnp.bfloat16)
    queries = projected[:, 0]
    key_values = projected[:, 1:]
    attended, log_totals = lax.map(
        lambda slot_items: attend_slot(
            slot_items[0], slot_items[1], slot_items[2], score_scale, head_dim
        ),
        (queries, key_values, lengths),
    )
    mixed_rows = attended.reshape(token_count, local_width)
    token_rows = hidden_in.reshape(token_count, model_width)
    branch = lax.psum(
        jnp.dot(mixed_rows, w_back, preferred_element_type=jnp.float32), "tp"
    ) + branch_biases[0].astype(jnp.float32)
    first_norm, first_pull = jax.vjp(
        norm_rows,
        token_rows.astype(jnp.float32) + branch,
        gains[0].astype(jnp.float32),
        shifts[0].astype(jnp.float32),
    )
    first_low = first_norm.astype(jnp.bfloat16)
    hidden_pre = jnp.dot(first_low, w_up, preferred_element_type=jnp.float32) + up_bias.astype(
        jnp.float32
    )
    activated, gelu_pull = jax.vjp(gelu_exact, hidden_pre)
    activated_low = activated.astype(jnp.bfloat16)
    second_branch = lax.psum(
        jnp.dot(activated_low, w_down, preferred_element_type=jnp.float32), "tp"
    ) + branch_biases[1].astype(jnp.float32)
    output_rows, second_pull = jax.vjp(
        norm_rows,
        first_norm + second_branch,
        gains[1].astype(jnp.float32),
        shifts[1].astype(jnp.float32),
    )
    hidden_out = output_rows.astype(jnp.bfloat16).reshape(slot_count, block_len, model_width)
    own_start = lax.axis_index("ctx") * block_len
    positions = own_start + lax.iota(jnp.int32, block_len)
    row_mask = (positions[None, :] < lengths[:, None]).astype(jnp.float32).reshape(token_count, 1)
    grad_output = out_grad.reshape(token_count, model_width).astype(jnp.float32) * row_mask
    grad_second, grad_gain_two, grad_shift_two = second_pull(grad_output)
    grad_second_low = grad_second.astype(jnp.bfloat16)
    grad_down = lax.dot_general(
        activated_low, grad_second_low, contract_rows, preferred_element_type=jnp.float32
    )
    grad_act = lax.dot_general(
        grad_second_low, w_down, contract_cols, preferred_element_type=jnp.float32
    )
    (grad_pre,) = gelu_pull(grad_act)
    grad_pre_low = grad_pre.astype(jnp.bfloat16)
    grad_up = lax.dot_general(
        first_low, grad_pre_low, contract_rows, preferred_element_type=jnp.float32
    )
    grad_first = grad_second + lax.psum(
        lax.dot_general(grad_pre_low, w_up, contract_cols, preferred_element_type=jnp.float32), "tp"
    )
    grad_resid, grad_gain_one, grad_shift_one = first_pull(grad_first)
    grad_branch_low = grad_resid.astype(jnp.bfloat16)
    grad_back = lax.dot_general(
        mixed_rows, grad_branch_low, contract_rows, preferred_element_type=jnp.float32
    )
    grad_mixed = (
        lax.dot_general(grad_branch_low, w_back, contract_cols, preferred_element_type=jnp.float32)
        .astype(jnp.bfloat16)
        .reshape(slot_count, block_len, local_width)
    )
    grad_queries, grad_pairs = lax.map(
        lambda slot_items: slot_grads(
            slot_items[0],
            slot_items[1],
            slot_items[2],
            slot_items[3],
            slot_items[4],
            score_scale,
            head_dim,
        ),
        (queries, key_values, lengths, grad_mixed, log_totals),
    )
    grad_proj = jnp.concatenate(
        [grad_queries.astype(jnp.bfloat16)[:, None], grad_pairs.astype(jnp.bfloat16)], axis=1
    )
    grad_w_proj = jnp.einsum(
        "sbd,spbc->pdc", hidden_in, grad_proj, preferred_element_type=jnp.float32
    )
    grad_proj_bias = jnp.stack(
        [
            jnp.sum(grad_proj[:, 0], axis=(0, 1), dtype=jnp.float32),
            jnp.sum(grad_proj[:, 2], axis=(0, 1), dtype=jnp.float32),
        ]
    ).reshape(proj_bias.shape)
    grad_tokens = jnp.einsum(
        "spbc,pdc->sbd", grad_proj, w_proj, preferred_element_type=jnp.float32
    ).reshape(token_count, model_width)
    hidden_grad = (
        (grad_resid + lax.psum(grad_tokens.astype(jnp.bfloat16), "tp").astype(jnp.float32))
        .astype(jnp.bfloat16)
        .reshape(slot_count, block_len, model_width)
    )
    grad_biases = jnp.stack(
        [
            jnp.sum(grad_branch_low, axis=0, dtype=jnp.float32),
            jnp.sum(grad_second_low, axis=0, dtype=jnp.float32),
        ]
    )
    grad_gains = jnp.stack([grad_gain_one, grad_gain_two])
    grad_shifts = jnp.stack([grad_shift_one, grad_shift_two])
    grad_up_bias = jnp.sum(grad_pre_low, axis=0, dtype=jnp.float32)
    shares = (
        lax.psum_scatter(
            grad_w_proj.astype(jnp.bfloat16), "fsdp", scatter_dimension=1, tiled=True
        ).astype(jnp.float32),
        lax.psum_scatter(
            grad_proj_bias.astype(jnp.bfloat16), "fsdp", scatter_dimension=2, tiled=True
        ).astype(jnp.float32),
        lax.psum_scatter(
            grad_back.astype(jnp.bfloat16), "fsdp", scatter_dimension=1, tiled=True
        ).astype(jnp.float32),
        lax.psum_scatter(
            grad_biases.astype(jnp.bfloat16), "fsdp", scatter_dimension=1, tiled=True
        ).astype(jnp.float32),
        lax.psum_scatter(
            grad_gains.astype(jnp.bfloat16), "fsdp", scatter_dimension=1, tiled=True
        ).astype(jnp.float32),
        lax.psum_scatter(
            grad_shifts.astype(jnp.bfloat16), "fsdp", scatter_dimension=1, tiled=True
        ).astype(jnp.float32),
        lax.psum_scatter(
            grad_up.astype(jnp.bfloat16), "fsdp", scatter_dimension=1, tiled=True
        ).astype(jnp.float32),
        lax.psum_scatter(
            grad_up_bias.astype(jnp.bfloat16), "fsdp", scatter_dimension=0, tiled=True
        ).astype(jnp.float32),
        lax.psum_scatter(
            grad_down.astype(jnp.bfloat16), "fsdp", scatter_dimension=0, tiled=True
        ).astype(jnp.float32),
    )
    owned = (
        lax.psum(shares[0].astype(jnp.bfloat16), "ctx").astype(jnp.float32),
        lax.psum(shares[1].astype(jnp.bfloat16), "ctx").astype(jnp.float32),
        lax.psum(shares[2].astype(jnp.bfloat16), "ctx").astype(jnp.float32),
        lax.psum(shares[3].astype(jnp.bfloat16), "ctx").astype(jnp.float32),
        lax.psum(shares[4].astype(jnp.bfloat16), "ctx").astype(jnp.float32),
        lax.psum(shares[5].astype(jnp.bfloat16), "ctx").astype(jnp.float32),
        lax.psum(shares[6].astype(jnp.bfloat16), "ctx").astype(jnp.float32),
        lax.psum(shares[7].astype(jnp.bfloat16), "ctx").astype(jnp.float32),
        lax.psum(shares[8].astype(jnp.bfloat16), "ctx").astype(jnp.float32),
    )
    return (
        hidden_out,
        hidden_grad,
        owned[0],
        owned[1],
        owned[2],
        owned[3],
        owned[4],
        owned[5],
        owned[6],
        owned[7],
        owned[8],
    )


def solution(mesh):
    one_slot_each = (mesh.shape["fsdp"], mesh.shape["ctx"], mesh.shape["tp"]) == (4, 4, 2)
    return jax.shard_map(
        per_slot if one_slot_each else per_device,
        mesh=mesh,
        in_specs=(
            P("fsdp", "ctx", None),
            P("fsdp"),
            P("fsdp", "ctx", None),
            P(None, "fsdp", "tp"),
            P(None, "tp", "fsdp"),
            P("tp", "fsdp"),
            P(None, "fsdp"),
            P(None, "fsdp"),
            P(None, "fsdp"),
            P(None, ("fsdp", "tp")),
            P(("fsdp", "tp")),
            P(("fsdp", "tp"), None),
        ),
        out_specs=(
            P("fsdp", "ctx", None),
            P("fsdp", "ctx", None),
            P(None, "fsdp", "tp"),
            P(None, "tp", "fsdp"),
            P("tp", "fsdp"),
            P(None, "fsdp"),
            P(None, "fsdp"),
            P(None, "fsdp"),
            P(None, ("fsdp", "tp")),
            P(("fsdp", "tp")),
            P(("fsdp", "tp"), None),
        ),
        check_vma=False,
    )
```

```python
import functools

import jax
import jax.numpy as jnp
from jax import lax
from jax.experimental import pallas as pl
from jax.experimental.pallas import tpu as pltpu
from jax.sharding import PartitionSpec as P

f32 = jnp.float32
bf16 = jnp.bfloat16
MESH = pl.DeviceIdType.MESH
ANY = pl.BlockSpec(memory_space=pl.ANY)
VM = pl.BlockSpec(memory_space=pltpu.VMEM)
SM = pl.BlockSpec(memory_space=pltpu.SMEM)
DMA = pltpu.SemaphoreType.DMA
NN = (((1,), (0,)), ((), ()))
NT = (((1,), (1,)), ((), ()))
TN = (((0,), (0,)), ((), ()))
VMEM_BYTES = 60 << 20


def dot(left, right, dims=NN):
    return lax.dot_general(left, right, dims, preferred_element_type=f32)


def struct(shape, dtype):
    return jax.ShapeDtypeStruct(shape, dtype)


def place():
    z, c, t = lax.axis_index("fsdp"), lax.axis_index("ctx"), lax.axis_index("tp")
    along_x = c + 1 - 2 * (c % 2)
    along_y = c + 2 - 4 * (c // 2)
    n1 = along_x + t * (along_y - along_x)
    n2 = along_y + t * (along_x - along_y)
    return z, c, t, n1, n2, 3 - c


def remote(src, dst, send_sem, recv_sem, device):
    return pltpu.make_async_remote_copy(
        src_ref=src,
        dst_ref=dst,
        send_sem=send_sem,
        recv_sem=recv_sem,
        device_id=device,
        device_id_type=MESH,
    )


def meet(devices):
    barrier = pltpu.get_barrier_semaphore()
    for device in devices:
        pl.semaphore_signal(barrier, inc=1, device_id=device, device_id_type=MESH)
    pl.semaphore_wait(barrier, len(devices))


def tile(i, size):
    return pl.ds(pl.multiple_of(i * size, size), size)


def split3(v):
    hi = v.astype(bf16).astype(f32)
    rest = v - hi
    mid = rest.astype(bf16).astype(f32)
    return hi, mid, rest - mid


def key_bias(length, rows):
    r = lax.broadcasted_iota(jnp.int32, (rows, 128), 0)
    position = (r % 512) // 128 * 256 + r // 512 * 128 + r % 128
    return jnp.where(position < length, 0.0, -1e30)


def gelu_pair(h):
    cdf = 0.5 * (1.0 + lax.erf(h * 0.7071067811865476))
    density = jnp.exp(h * h * -0.5) * 0.3989422804014327
    return h * cdf, cdf + h * density


def unit_rows(r):
    centred = r - jnp.mean(r, axis=-1, keepdims=True)
    spread = jnp.mean(centred * centred, axis=-1, keepdims=True)
    inverse = lax.rsqrt(spread + 1e-5)
    return centred * inverse, inverse


def norm_back(g, n, inverse):
    return inverse * (g - jnp.mean(g, axis=-1, keepdims=True) - n * jnp.mean(g * n, axis=-1, keepdims=True))


def column_sum(v):
    return jnp.sum(v, axis=0, keepdims=True)


class Net:
    def __init__(self, sems):
        self.sems, self.count, self.sends = sems, 0, {}

    def semaphore(self):
        self.count += 1
        return self.sems.at[self.count - 1]

    def send(self, src, dst, device):
        cp = remote(src, dst, self.semaphore(), self.semaphore(), device)
        cp.start()
        self.sends[id(cp)] = cp
        return cp

    def sent(self, copies):
        for cp in copies:
            self.sends.pop(id(cp)).wait_send()

    def local(self, src, dst):
        cp = pltpu.make_async_copy(src, dst, self.semaphore())
        cp.start()
        return cp


class Queue:
    def __init__(self):
        self.steps = []

    def add(self, step):
        self.steps.append(step)

    def tick(self, n=1):
        for _ in range(n):
            if self.steps:
                self.steps.pop(0)()

    def drain(self):
        while self.steps:
            self.tick()


N_SEMS = 512


def layer_kernel(
    len_ref, x_in, og_in, qkv_in, out_in, up_in, down_in, ob_in, ng_in, nb_in, qv_in, fb_in,
    oqkv, oout, oup, odown, osmall, oh, odx,
    xs, ogs, wqkv, wout, wup, wdown, small, small_in, rowp, upb, bias,
    q_ref, k_ref, v_ref, mixed, gmixed, lse,
    qe, ke, ve, de, qz, dz, kt, dqt,
    p_own, p_send, p_recv, n1r, g2r, inv1, low1, low2, low3, act, slope,
    gup, gdown, gout, gqkv, gupb, gsm, gsr, gst, gsz, gsc,
    up1, up2, up3, down1, down2, down3, out1, out2, out3, qkv1, qkv2, qkv3, dna, dn1, dn2,
    sems,
):
    z, c, t, n1, n2, dg = place()
    u = 1 - t
    sibling = (z, c, u)
    planes = (n1, n2, dg)
    net, queue = Net(sems), Queue()
    across, along = (z, n1, t), (z, n2, t)

    def plane_z(d):
        return ((z + d) % 4, c, t)

    small_in[...] = jnp.zeros_like(small_in)
    for row, ref in ((0, ob_in), (2, ng_in), (4, nb_in)):
        small_in[row : row + 2, 0:192] = ref[...].astype(f32)
    small_in[8:9, :] = fb_in[...].astype(f32)
    for i in range(2):
        small_in[16 + 6 * i : 22 + 6 * i, 0:16] = qv_in[i].astype(f32)
    meet([(z, p, t) for p in planes] + [plane_z(d) for d in (1, 2, 3)] + [sibling])

    schemes = "qqqqhh"
    side = c % 2 + t * (c // 2 - c % 2)

    def part_of(w, q):
        begin, rows = ((0, 192), (0, 192), (0, 384), (384, 384), (0, 192), (192, 192))[w]
        size = rows // (4 if schemes[w] == "q" else 2)
        return pl.ds(pl.multiple_of(begin + q * size, 16), size)

    def region(w, zz, q):
        begin, rows = ((0, 192), (0, 192), (0, 384), (384, 384), (0, 192), (192, 192))[w]
        size = rows // (4 if schemes[w] == "q" else 2)
        if w < 2:
            rows = pl.ds(pl.multiple_of(zz * 192 + q * size, 16), size)
            return wqkv.at[:, rows, :] if w == 0 else wout.at[rows, :]
        return (wup if w < 4 else wdown).at[zz, part_of(w, q), :]

    def mine(w):
        rows = part_of(w, c if schemes[w] == "q" else side)
        return qkv_in.at[:, rows, :] if w == 0 else (out_in, up_in, up_in, down_in, down_in)[w - 1].at[rows, :]

    zcopies = {}

    def send_z(w):
        for d in (1, 2, 3):
            zcopies[w, d] = net.send(mine(w), region(w, z, c if schemes[w] == "q" else side), plane_z(d))

    spreads = {}

    def spread(w):
        for d in (1, 2, 3):
            zcopies[w, d].wait_recv()
            part = region(w, (z + 4 - d) % 4, c if schemes[w] == "q" else side)
            spreads[w, d] = [net.send(part, part, across)]
            if schemes[w] == "q":
                spreads[w, d].append(net.send(part, part, along))

    def finish(w):
        if schemes[w] == "q":
            for d in (1, 2, 3):
                spreads[w, d][0].wait_recv()
                part = region(w, (z + 4 - d) % 4, n1)
                spreads[w, d].append(net.send(part, part, along))

    def whole(w):
        for d in (1, 2, 3):
            for cp in spreads[w, d][1 if schemes[w] == "q" else 0 :]:
                cp.wait_recv()

    def slot_rows(h, b):
        return pl.ds(pl.multiple_of(h * 512 + b * 128, 128), 128)

    xcopies = [net.send(x_in.at[p, tile(t, 128), :], xs.at[slot_rows(t, c), :], (z, p, t)) for p in planes]
    send_z(0)
    smalls = [net.send(small_in, small.at[z], plane_z(d)) for d in (1, 2, 3)]
    local = [
        net.local(x_in.at[c, pl.ds(0, 128), :], xs.at[slot_rows(0, c), :]),
        net.local(x_in.at[c, pl.ds(128, 128), :], xs.at[slot_rows(1, c), :]),
        net.local(qkv_in, wqkv.at[:, tile(z, 192), :]),
        net.local(small_in, small.at[z]),
        net.local(og_in.at[c, tile(t, 128), :], ogs.at[tile(c, 128), :]),
        net.local(out_in, wout.at[tile(z, 192), :]),
        net.local(up_in, wup.at[z]),
        net.local(down_in, wdown.at[z]),
    ]
    spread(0)
    send_z(1)
    send_z(2)
    forwards = []
    for i, p in enumerate(planes):
        xcopies[i].wait_recv()
        forwards.append(net.send(xs.at[slot_rows(t, p), :], xs.at[slot_rows(t, p), :], sibling))
    finish(0)
    for cp in local[:4]:
        cp.wait()
    for cp in smalls:
        cp.wait_recv()

    def onehot(rows, cols, target):
        r, l = lax.broadcasted_iota(jnp.int32, (rows, cols), 0), lax.broadcasted_iota(jnp.int32, (rows, cols), 1)
        return jnp.where(l == target(r), 1.0, 0.0).astype(bf16)

    rows768 = jnp.zeros((32, 768), f32)
    rows384 = jnp.zeros((32, 384), f32)
    l16 = lax.broadcasted_iota(jnp.int32, (16, 384), 1)
    r16 = lax.broadcasted_iota(jnp.int32, (16, 384), 0)
    for j in range(4):
        s = small[j].astype(bf16)
        rows768 += dot(s[:, 0:192], onehot(192, 768, lambda r: r + 192 * j))
        rows384 += dot(s[:, 0:16], jnp.where(l16 % 64 == 16 * j + r16, 1.0, 0.0).astype(bf16))
        upb[j : j + 1, :] = small[j, 8:9, :]
    rowp[...] = rows768[0:8, :]
    head = lax.broadcasted_iota(jnp.int32, (32, 384), 0) - lax.broadcasted_iota(jnp.int32, (32, 384), 1) // 64
    for i in range(2):
        bias[6 + i : 7 + i, :] = column_sum(jnp.where(head == 16 + 6 * i, rows384, 0.0))
    bias0, bias1 = rowp[0:1, :], rowp[1:2, :]
    gain0, gain1 = rowp[2:3, :], rowp[3:4, :]
    shift0, shift1 = rowp[4:5, :], rowp[5:6, :]

    spread(1)
    for cp in forwards:
        cp.wait_recv()
    whole(0)

    ocopies = []

    def send_og():
        for p in planes:
            ocopies.append(net.send(og_in.at[p, tile(t, 128), :], ogs.at[tile(c, 128), :], (z, p, t)))

    def next_group(w):
        spread(w)
        if w < 4:
            send_z(w + 2)

    send_z(3)
    for step in (
        lambda: next_group(2),
        lambda: finish(1),
        lambda: next_group(3),
        lambda: finish(2),
        send_og,
        lambda: finish(3),
        lambda: next_group(4),
        lambda: next_group(5),
        lambda: finish(4),
        lambda: finish(5),
    ):
        queue.add(step)

    def project(i, _):
        rows = tile(i, 256)
        xr = xs[rows, :]
        q_ref[rows, :] = ((dot(xr, wqkv[0]) + bias[6:7, :]).astype(bf16).astype(f32) * 0.125).astype(bf16)
        k_ref[rows, :] = dot(xr, wqkv[1]).astype(bf16)
        v_ref[rows, :] = (dot(xr, wqkv[2]) + bias[7:8, :]).astype(bf16)
        return 0

    lax.fori_loop(0, 4, project, 0)
    queue.tick()
    kb = key_bias(len_ref[c], 1024)
    lane = lax.broadcasted_iota(jnp.int32, (1024, 128), 1)
    lse[...] = jnp.zeros_like(lse)

    def own_lanes(j):
        return ((lane < 64), 64) if j == 0 else ((lane >= 64), 0)

    for hp in range(3):
        cols = pl.ds(128 * hp, 128)
        q, k, v = q_ref[:, cols].astype(f32), k_ref[:, cols].astype(f32), v_ref[:, cols].astype(f32)
        for j in range(2):
            own, e = own_lanes(j)
            one = jnp.where(lane == e, 1.0, 0.0)
            qe[j] = jnp.where(own, q, one).astype(bf16)
            ke[j] = jnp.where(own, k, jnp.where(lane == e, kb, 0.0)).astype(bf16)
            ve[j] = jnp.where(own, v, one).astype(bf16)
        for b in range(2):
            rows = pl.ds(512 * b, 512)
            ln = lax.broadcasted_iota(jnp.int32, (512, 128), 1)
            outs, totals = [], []
            for j in range(2):
                e = 64 if j == 0 else 0
                s = dot(qe[j, rows, :], ke[j], NT)
                m = jnp.max(s, axis=1, keepdims=True)
                p = jnp.exp(s - m).astype(bf16)
                o = dot(p, ve[j])
                total = o[:, e : e + 1]
                outs.append(o * (1.0 / total))
                totals.append(m + jnp.log(total))
            mixed[rows, cols] = jnp.where(ln < 64, outs[0], outs[1]).astype(bf16)
            cur = jnp.where(ln == 2 * hp, totals[0], lse[rows, :])
            lse[rows, :] = jnp.where(ln == 2 * hp + 1, totals[1], cur)
            queue.tick()

    local[5].wait()
    whole(1)
    def rows_of(h, i):
        return pl.ds(pl.multiple_of(h * 512 + i * 256, 256), 256)

    def exchange_rows(ref, i):
        return net.send(ref.at[rows_of(t, i), :], ref.at[rows_of(t, i), :], sibling)

    def exchange_parts(value):
        copies = []
        for i in range(2):
            p_send[i] = value(u, i)
            copies.append(net.send(p_send.at[i], p_recv.at[i], sibling))
        for i in range(2):
            p_own[i] = value(t, i)
        return copies

    a = exchange_parts(lambda h, i: dot(mixed[rows_of(h, i), :], wout[...], NT))
    b = []
    for i in range(2):
        a[i].wait_recv()
        r = xs[rows_of(t, i), :].astype(f32) + (p_own[i] + p_recv[i] + bias0)
        n, inverse = unit_rows(r)
        n1r[i] = n
        inv1[i] = jnp.broadcast_to(inverse, (256, 128))
        low1[rows_of(t, i), :] = (n * gain0 + shift0).astype(bf16)
        b.append(exchange_rows(low1, i))
    queue.tick()
    local[6].wait()
    whole(2)
    whole(3)

    def up(h):
        def chunk(zz, _):
            hidden = dot(low1[tile(h, 512), :], wup[zz]) + upb[pl.ds(zz, 1), :]
            value, grad = gelu_pair(hidden)
            act[zz, tile(h, 512), :] = value.astype(bf16)
            slope[zz, tile(h, 512), :] = grad.astype(bf16)
            return 0

        lax.fori_loop(0, 4, chunk, 0)

    up(t)
    queue.tick(2)
    for i in range(2):
        b[i].wait_recv()
    up(u)
    queue.drain()
    local[7].wait()
    whole(4)
    whole(5)

    def down(h, i):
        rows = rows_of(h, i)
        total = dot(act[0, rows, :], wdown[0])
        for zz in range(1, 4):
            total += dot(act[zz, rows, :], wdown[zz])
        return total

    net.sent(a)
    a = exchange_parts(down)
    local[4].wait()
    for cp in ocopies:
        cp.wait_recv()
    hout = ogs
    b = []
    gg1 = gs1 = gb1 = 0.0
    hcopies = []

    def send_rows(src, dst, p, b):
        return net.send(src.at[pl.ds(pl.multiple_of(b * 128, 128), 128), :], dst.at[c, tile(t, 128), :], (z, p, t))

    for i in range(2):
        a[i].wait_recv()
        n, inverse = unit_rows((n1r[i] * gain0 + shift0) + (p_own[i] + p_recv[i] + bias1))
        r = lax.broadcasted_iota(jnp.int32, (256, 768), 0) + 256 * i
        live = (r // 128 * 256 + t * 128 + r % 128) < len_ref[c]
        g = jnp.where(live, ogs[pl.ds(256 * i, 256), :].astype(f32), 0.0)
        hout[pl.ds(256 * i, 256), :] = (n * gain1 + shift1).astype(bf16)
        gg1 = gg1 + column_sum(g * n)
        gs1 = gs1 + column_sum(g)
        g2 = norm_back(g * gain1, n, inverse)
        g2r[i] = g2
        low2[rows_of(t, i), :] = g2.astype(bf16)
        b.append(exchange_rows(low2, i))
        gb1 = gb1 + column_sum(g2.astype(bf16).astype(f32))
    for p in planes:
        hcopies.append(send_rows(hout, oh, p, p))
    hself = [net.send(hout.at[tile(c, 128), :], oh.at[c, tile(t, 128), :], sibling)]
    hlocal = net.local(hout.at[tile(c, 128), :], oh.at[c, tile(t, 128), :])

    quarter_rows = {"up": 192, "out": 96, "qkv": 48}
    final = {}

    def gather_out(ref_of, key):
        first = net.send(ref_of(c), ref_of(c), across)
        second = net.send(ref_of(c), ref_of(c), along)

        def relay():
            first.wait_recv()
            final[key] = [second, net.send(ref_of(n1), ref_of(n1), along)]

        queue.add(relay)

    def reduce_group(key, grad, first, second, third, out, split):
        s1 = [net.send(grad(n1), first.at[0], across), net.send(grad(dg), first.at[1], across)]

        def step2():
            s1[1].wait_recv()
            first[1] = (grad(n2)[...].astype(f32) + first[1].astype(f32)).astype(bf16)
            s2 = net.send(first.at[1], second, along)
            s1[0].wait_recv()

            def step3():
                s2.wait_recv()
                total = grad(c)[...].astype(f32) + first[0].astype(f32) + second[...].astype(f32)
                first[0] = total.astype(bf16)
                s3 = [net.send(split(first.at[0], (z + d) % 4), third.at[d - 1], plane_z(d)) for d in (1, 2, 3)]

                def step4():
                    for cp in s3:
                        cp.wait_recv()
                    v = split(first.at[0], z)[...].astype(f32) + third[0].astype(f32)
                    v = v + (third[1].astype(f32) + third[2].astype(f32))
                    out(c)[...] = v.astype(bf16)
                    gather_out(out, key)

                queue.add(step4)

            queue.add(step3)

        queue.add(step2)

    def reduce_shard(key, d, grad, first, second, third, out, sent):
        s1 = [net.send(grad(n1), first.at[d, 0], across), net.send(grad(dg), first.at[d, 1], across)]

        def step2():
            s1[1].wait_recv()
            first[d, 1] = (grad(n2)[...].astype(f32) + first[d, 1].astype(f32)).astype(bf16)
            s2 = net.send(first.at[d, 1], second.at[d], along)
            s1[0].wait_recv()

            def step3():
                s2.wait_recv()
                total = grad(c)[...].astype(f32) + first[d, 0].astype(f32) + second[d].astype(f32)
                first[d, 0] = total.astype(bf16)
                if d:
                    sent[d] = net.send(first.at[d, 0], third.at[d - 1], plane_z(d))
                else:
                    queue.add(step4)

            queue.add(step3)

        def step4():
            for cp in sent.values():
                cp.wait_recv()
            v = (first[0, 0].astype(f32) + third[0].astype(f32)) + (third[1].astype(f32) + third[2].astype(f32))
            out(c)[...] = v.astype(bf16)
            gather_out(out, key)

        queue.add(step2)

    up_sent, half_sent, down_sent = {}, {}, {}

    def reduce_down():
        for cp in down_sent.values():
            cp.wait_recv()
        rows = pl.ds(0, 192)
        v = (gdown[z, rows, :].astype(f32) + dna[0].astype(f32)) + (dna[1].astype(f32) + dna[2].astype(f32))
        gdown[z, rows, :] = v.astype(bf16)
        quarter = lambda q: gdown.at[z, tile(q, 48), :]
        s1 = [net.send(quarter(n1), dn1.at[0], across), net.send(quarter(dg), dn1.at[1], across)]

        def step2():
            s1[1].wait_recv()
            dn1[1] = (quarter(n2)[...].astype(f32) + dn1[1].astype(f32)).astype(bf16)
            s2 = net.send(dn1.at[1], dn2, along)
            s1[0].wait_recv()

            def step3():
                s2.wait_recv()
                total = quarter(c)[...].astype(f32) + dn1[0].astype(f32) + dn2[...].astype(f32)
                out = lambda q: odown.at[tile(q, 48), :]
                out(c)[...] = total.astype(bf16)
                gather_out(out, "down")

            queue.add(step3)

        queue.add(step2)

    gupb[...] = jnp.zeros_like(gupb)
    for i in range(2):
        b[i].wait_recv()
    low2_sends = b
    for d in (1, 2, 3, 0):
        zz = (z + d) % 4
        for k in range(3):
            g = dot(act[zz, :, pl.ds(128 * k, 128)], low2[...], TN)
            gdown[zz, pl.ds(128 * k, 128), :] = g.astype(bf16)
        if d:
            down_sent[d] = net.send(gdown.at[zz, pl.ds(0, 192), :], dna.at[d - 1], plane_z(d))
        reduce_shard(
            "half", d, lambda q, zz=zz: gdown.at[zz, pl.ds(pl.multiple_of(192 + q * 48, 16), 48), :], down1, down2, down3,
            lambda q: odown.at[pl.ds(pl.multiple_of(192 + q * 48, 16), 48), :], half_sent,
        )

        def back(i, _):
            rows = tile(i, 512)
            g = (dot(low2[rows, :], wdown[zz], NT) * slope[zz, rows, :].astype(f32)).astype(bf16)
            slope[zz, rows, :] = g
            gupb[pl.ds(zz, 1), :] += column_sum(g.astype(f32))
            return 0

        lax.fori_loop(0, 2, back, 0)
        for k in range(6):
            g = dot(low1[:, pl.ds(128 * k, 128)], slope[zz], TN)
            gup[zz, pl.ds(128 * k, 128), :] = g.astype(bf16)
        reduce_shard(
            "up", d, lambda q, zz=zz: gup.at[zz, tile(q, 192), :], up1, up2, up3, lambda q: oup.at[tile(q, 192), :], up_sent
        )
        if d == 0:
            queue.tick()

    def first_grad(h, i):
        rows = rows_of(h, i)
        total = dot(slope[0, rows, :], wup[0], NT)
        for zz in range(1, 4):
            total += dot(slope[zz, rows, :], wup[zz], NT)
        return total

    net.sent(a)
    a = exchange_parts(first_grad)
    queue.tick(2)
    b = []
    gg0 = gs0 = gb0 = 0.0
    for i in range(2):
        a[i].wait_recv()
        g1 = g2r[i] + (p_own[i] + p_recv[i])
        n = n1r[i]
        gg0 = gg0 + column_sum(g1 * n)
        gs0 = gs0 + column_sum(g1)
        g = norm_back(g1 * gain0, n, inv1[i][:, 0:1])
        g2r[i] = g
        low3[rows_of(t, i), :] = g.astype(bf16)
        b.append(exchange_rows(low3, i))
        gb0 = gb0 + column_sum(g.astype(bf16).astype(f32))
    gsm[...] = jnp.zeros_like(gsm)
    for row, v in enumerate((gb0, gb1, gg0, gg1, gs0, gs1)):
        for j in range(4):
            gsm[j, row : row + 1, 0:192] = v[:, 192 * j : 192 * j + 192]
    for j in range(4):
        gsm[j, 8:9, :] = gupb[j : j + 1, :]
    queue.tick(2)
    for i in range(2):
        b[i].wait_recv()
    for h in range(2):
        gmixed[tile(h, 512), :] = dot(low3[tile(h, 512), :], wout[...]).astype(bf16)
    for k in range(6):
        g = dot(low3[:, pl.ds(128 * k, 128)], mixed[...], TN).astype(bf16)
        for s in range(2):
            at = 128 * k + 64 * s
            gout[at // 192, pl.ds(at % 192, 64), :] = g[64 * s : 64 * s + 64, :]
    reduce_group(
        "out", lambda q: gout.at[:, tile(q, 48), :], out1, out2, out3, lambda q: oout.at[tile(q, 48), :],
        lambda ref, zz: ref.at[zz],
    )
    dcat, wcat = act, wup
    net.sent([cp for w in (2, 3) for d in (1, 2, 3) for cp in spreads[w, d]])
    queue.add(reduce_down)
    for p in range(3):
        for hp in range(3):
            wcat[hp, :, pl.ds(128 * p, 128)] = wqkv[p, :, pl.ds(128 * hp, 128)]

    def forward_rows(copies, dst):
        out = []
        for cp, p in zip(copies, planes):
            cp.wait_recv()
            part = dst.at[p, tile(t, 128), :]
            out.append(net.send(part, part, sibling))
        return out

    hforward = []
    queue.add(lambda: hforward.extend(forward_rows(hcopies, oh)))

    for hp in range(3):
        cols = pl.ds(128 * hp, 128)
        q, k, v = q_ref[:, cols].astype(f32), k_ref[:, cols].astype(f32), v_ref[:, cols].astype(f32)
        do = gmixed[:, cols].astype(f32)
        pr = do * mixed[:, cols].astype(f32)
        for j in range(2):
            own, e = own_lanes(j)
            delta = jnp.sum(jnp.where(own, pr, 0.0), axis=1, keepdims=True)
            log_total = jnp.sum(jnp.where(lane == 2 * hp + j, lse[...], 0.0), axis=1, keepdims=True)
            lh, lm, ll = split3(-log_total)
            dh, dm, dl = split3(-delta)
            qz[j] = jnp.where(own, q, 0.0).astype(bf16)
            dz[j] = jnp.where(own, do, 0.0).astype(bf16)
            side = jnp.where(lane == e, 1.0, 0.0)
            side = jnp.where(lane == e + 1, lh, side)
            side = jnp.where(lane == e + 2, lm, side)
            side = jnp.where(lane == e + 3, ll, side)
            qe[j] = jnp.where(own, q, side).astype(bf16)
            ones3 = jnp.where((lane > e) & (lane < e + 4), 1.0, 0.0)
            ke[j] = jnp.where(own, k, jnp.where(lane == e, kb, ones3)).astype(bf16)
            side = jnp.where(lane == e + 1, dh, 0.0)
            side = jnp.where(lane == e + 2, dm, side)
            side = jnp.where(lane == e + 3, dl, side)
            de[j] = jnp.where(own, do, side).astype(bf16)
            ve[j] = jnp.where(own, v, ones3).astype(bf16)
        kt[...] = k.T.astype(bf16)
        for b in range(2):
            rows = pl.ds(512 * b, 512)
            dv, dk = None, None
            for j in range(2):
                p = jnp.exp(dot(ke[j, rows, :], qe[j], NT))
                g = dot(ve[j, rows, :], de[j], NT)
                ds = (p * g).astype(bf16)
                a_ = dot(p.astype(bf16), dz[j])
                b_ = dot(ds, qz[j])
                dv = a_ if dv is None else dv + a_
                dk = b_ if dk is None else dk + b_
                half = slice(64 * j, 64 * j + 64)
                if b == 0:
                    dqt[half, :] = dot(kt[half, rows], ds)
                else:
                    dqt[half, :] += dot(kt[half, rows], ds)
            dcat[hp, rows, pl.ds(128, 128)] = dk.astype(bf16)
            dcat[hp, rows, pl.ds(256, 128)] = dv.astype(bf16)
            queue.tick(4)
        dcat[hp, :, pl.ds(0, 128)] = (dqt[...] * 0.125).T.astype(bf16)
        for k in range(6):
            g = dot(xs[:, pl.ds(128 * k, 128)], dcat[hp], TN).astype(bf16)
            for s in range(2):
                at = 128 * k + 64 * s
                gqkv[hp, at // 192, pl.ds(at % 192, 64), :] = g[64 * s : 64 * s + 64, :]

        def pair_group(hp):
            reduce_group(
                "qkv%d" % hp, lambda q: gqkv.at[hp, :, tile(q, 48), :], qkv1.at[hp], qkv2.at[hp], qkv3.at[hp],
                lambda q: oqkv.at[hp, tile(q, 48), :], lambda ref, zz: ref.at[zz],
            )

        pair_group(hp)
        queue.tick(2)

    def rows_back(h, i):
        rows = rows_of(h, i)
        total = dot(dcat[0, rows, :], wcat[0], NT)
        for hp in range(1, 3):
            total += dot(dcat[hp, rows, :], wcat[hp], NT)
        return total

    net.sent(a + low2_sends)
    dxl = low2
    a = exchange_parts(rows_back)
    for i in range(2):
        a[i].wait_recv()
        dxl[pl.ds(256 * i, 256), :] = (g2r[i] + (p_own[i] + p_recv[i])).astype(bf16)
    dcopies = [send_rows(dxl, odx, p, p) for p in planes]
    dself = net.send(dxl.at[tile(c, 128), :], odx.at[c, tile(t, 128), :], sibling)
    dlocal = net.local(dxl.at[tile(c, 128), :], odx.at[c, tile(t, 128), :])

    sums = []
    for p in (0, 2):
        v = jnp.concatenate([column_sum(dcat[hp, :, pl.ds(128 * p, 128)].astype(f32)) for hp in range(3)], axis=1)
        sums.append(jnp.broadcast_to(v, (64, 384)))
    r = lax.broadcasted_iota(jnp.int32, (64, 384), 0)
    l = lax.broadcasted_iota(jnp.int32, (64, 384), 1)
    mine_ = (l // 64 == r % 16 % 6) & (l % 64 // 16 == r // 16)
    spread_rows = jnp.where(mine_, jnp.where(r % 16 < 6, sums[0], sums[1]), 0.0)
    r = lax.broadcasted_iota(jnp.int32, (384, 128), 0)
    l = lax.broadcasted_iota(jnp.int32, (384, 128), 1)
    take = jnp.where(r % 16 == l, 1.0, 0.0).astype(bf16)
    picked = jnp.zeros((64, 128), f32)
    for piece in split3(spread_rows):
        picked += dot(piece.astype(bf16), take)
    for j in range(4):
        gsm[j, 16:32, 0:128] = picked[16 * j : 16 * j + 16, :]
    xsm = net.send(gsm, gsr, sibling)
    queue.tick(2)
    xsm.wait_recv()
    shared = lax.broadcasted_iota(jnp.int32, (4, 32, 384), 1) < 6
    gst[...] = gsm[...] + jnp.where(shared, gsr[...], 0.0)
    small1 = [net.send(gst.at[(z + d) % 4], gsz.at[d], plane_z(d)) for d in (1, 2, 3)]
    queue.tick(2)
    for cp in small1:
        cp.wait_recv()
    gsz[0] = (gst[z] + gsz[1]) + (gsz[2] + gsz[3])
    small2 = [net.send(gsz.at[0], gsc.at[i], (z, p, t)) for i, p in enumerate(planes)]
    queue.tick(2)
    dforward = []
    queue.add(lambda: dforward.extend(forward_rows(dcopies, odx)))
    queue.drain()
    for cp in small2:
        cp.wait_recv()
    osmall[...] = (gsz[0] + gsc[0]) + (gsc[1] + gsc[2])
    for copies in final.values():
        for cp in copies:
            cp.wait_recv()
    for cp in hforward + dforward + hself + [dself]:
        cp.wait_recv()
    hlocal.wait()
    dlocal.wait()
    net.sent(list(net.sends.values()))
    assert net.count <= N_SEMS


def finish_kernel(oqkv, oout, oup, odown, osmall, oh, odx, h, dx, gqkv, gqv, gout, gob, gng, gnb, gup, gfb, gdown):
    h[...] = oh[...]
    dx[...] = odx[...]
    for hp in range(3):
        for p in range(3):
            gqkv[p, :, pl.ds(128 * hp, 128)] = oqkv[hp, :, pl.ds(128 * p, 128)].astype(f32)
    gout[...] = oout[...].astype(f32)
    gup[...] = oup[...].astype(f32)
    gdown[...] = odown[...].astype(f32)
    for row, ref in ((0, gob), (2, gng), (4, gnb)):
        ref[...] = osmall[row : row + 2, 0:192]
    gfb[...] = osmall[8:9, :]
    for i in range(2):
        gqv[i] = osmall[16 + 6 * i : 22 + 6 * i, 0:16]


def per_slot(hidden_in, lengths, out_grad, w_qkv, qv_bias, w_out, out_biases, norm_gains, norm_biases, w_in, ffn_bias, w_ffo):
    def vm(*shape, dtype=bf16):
        return pltpu.VMEM(shape, dtype)

    small = (32, 384)
    raw = pl.pallas_call(
        layer_kernel,
        out_shape=(
            struct((3, 192, 384), bf16),
            struct((192, 384), bf16),
            struct((768, 384), bf16),
            struct((384, 768), bf16),
            struct(small, f32),
            struct((4, 256, 768), bf16),
            struct((4, 256, 768), bf16),
        ),
        in_specs=[SM] + [ANY] * 6 + [VM] * 5,
        out_specs=(VM,) * 5 + (ANY, ANY),
        scratch_shapes=[
            vm(1024, 768), vm(512, 768), vm(3, 768, 384), vm(768, 384), vm(4, 768, 384), vm(4, 384, 768),
            vm(4, *small, dtype=f32), vm(*small, dtype=f32), vm(8, 768, dtype=f32), vm(4, 384, dtype=f32), vm(8, 384, dtype=f32),
            vm(1024, 384), vm(1024, 384), vm(1024, 384), vm(1024, 384), vm(1024, 384), vm(1024, 128, dtype=f32),
        ]
        + [vm(2, 1024, 128)] * 6
        + [vm(128, 1024), vm(128, 1024, dtype=f32)]
        + [vm(2, 256, 768, dtype=f32)] * 5
        + [
            vm(2, 256, 128, dtype=f32), vm(1024, 768), vm(1024, 768), vm(1024, 768), vm(4, 1024, 384), vm(4, 1024, 384),
            vm(4, 768, 384), vm(4, 384, 768), vm(4, 192, 384), vm(3, 4, 192, 384), vm(4, 384, dtype=f32),
        ]
        + [vm(4, *small, dtype=f32)] * 4
        + [
            vm(3, *small, dtype=f32),
            vm(4, 2, 192, 384), vm(4, 192, 384), vm(3, 192, 384),
            vm(4, 2, 48, 768), vm(4, 48, 768), vm(3, 48, 768),
            vm(2, 4, 48, 384), vm(4, 48, 384), vm(3, 48, 384),
            vm(3, 2, 4, 48, 384), vm(3, 4, 48, 384), vm(3, 3, 48, 384),
            vm(3, 192, 768), vm(2, 48, 768), vm(48, 768),
            DMA((N_SEMS,)),
        ],
        compiler_params=pltpu.CompilerParams(collective_id=0, has_side_effects=True, vmem_limit_bytes=VMEM_BYTES),
        name="layer",
    )(
        lengths, hidden_in, out_grad, w_qkv, w_out.T, w_in, w_ffo,
        out_biases, norm_gains, norm_biases, qv_bias, ffn_bias.reshape(1, 384),
    )
    h, dx, gqkv, gqv, gout, gob, gng, gnb, gup, gfb, gdown = pl.pallas_call(
        finish_kernel,
        out_shape=(
            struct((4, 256, 768), bf16),
            struct((4, 256, 768), bf16),
            struct((3, 192, 384), f32),
            struct((2, 6, 16), f32),
            struct((192, 384), f32),
            struct((2, 192), f32),
            struct((2, 192), f32),
            struct((2, 192), f32),
            struct((768, 384), f32),
            struct((1, 384), f32),
            struct((384, 768), f32),
        ),
        in_specs=[VM] * 7,
        out_specs=(VM,) * 11,
        compiler_params=pltpu.CompilerParams(vmem_limit_bytes=VMEM_BYTES),
        name="finish",
    )(*raw)
    return h, dx, gqkv, gqv, gout.T, gob, gng, gnb, gup, gfb.reshape(384), gdown


epsilon = 1e-05
masked_value = -1e30
heads_together = 2


def norm_rows(residual, gain_row, shift_row):
    centre = jnp.mean(residual, axis=-1, keepdims=True)
    centred = residual - centre
    spread = jnp.mean(centred * centred, axis=-1, keepdims=True)
    return centred * lax.rsqrt(spread + epsilon) * gain_row + shift_row


def gelu_exact(values):
    return jax.nn.gelu(values, approximate=False)


def split_heads(matrix, head_dim):
    return matrix.reshape(matrix.shape[0], matrix.shape[1] // head_dim, head_dim)


def block_scores(query_heads, key_heads, key_mask, score_scale):
    scores = (
        jnp.einsum("qhd,khd->hqk", query_heads, key_heads, preferred_element_type=jnp.float32)
        * score_scale
    )
    return jnp.where(key_mask[None, None, :], scores, masked_value)


def attend_slot(queries, key_value, length, score_scale, head_dim):
    gathered = lax.all_gather(key_value, "ctx", axis=1, tiled=True)
    seq_len = gathered.shape[1]
    key_mask = lax.iota(jnp.int32, seq_len) < length
    block_width = heads_together * head_dim
    outputs = []
    totals = []
    for head_block in range(queries.shape[1] // block_width):
        columns = slice(head_block * block_width, (head_block + 1) * block_width)
        query_heads = split_heads(queries[:, columns], head_dim)
        key_heads = split_heads(gathered[0][:, columns], head_dim)
        value_heads = split_heads(gathered[1][:, columns], head_dim)
        scores = block_scores(query_heads, key_heads, key_mask, score_scale)
        highest = jnp.max(scores, axis=-1, keepdims=True)
        log_total = highest + jnp.log(jnp.sum(jnp.exp(scores - highest), axis=-1, keepdims=True))
        weights_low = jnp.exp(scores - log_total).astype(jnp.bfloat16)
        attended = jnp.einsum(
            "hqk,khd->qhd", weights_low, value_heads, preferred_element_type=jnp.float32
        )
        outputs.append(attended.reshape(attended.shape[0], block_width))
        totals.append(log_total[:, :, 0])
    return (jnp.concatenate(outputs, axis=1).astype(jnp.bfloat16), jnp.concatenate(totals, axis=0))


def slot_grads(queries, key_value, length, grad_mixed, log_totals, score_scale, head_dim):
    gathered = lax.all_gather(key_value, "ctx", axis=1, tiled=True)
    seq_len = gathered.shape[1]
    key_mask = lax.iota(jnp.int32, seq_len) < length
    block_width = heads_together * head_dim
    query_grads = []
    key_grads = []
    value_grads = []
    inner_parts = []
    for head_block in range(queries.shape[1] // block_width):
        columns = slice(head_block * block_width, (head_block + 1) * block_width)
        heads_range = slice(head_block * heads_together, (head_block + 1) * heads_together)
        query_heads = split_heads(queries[:, columns], head_dim)
        key_heads = split_heads(gathered[0][:, columns], head_dim)
        value_heads = split_heads(gathered[1][:, columns], head_dim)
        grad_heads = split_heads(grad_mixed[:, columns], head_dim)
        scores = block_scores(query_heads, key_heads, key_mask, score_scale)
        softmax_rows = jnp.exp(scores - log_totals[heads_range, :, None])
        grad_weights = jnp.einsum(
            "qhd,khd->hqk", grad_heads, value_heads, preferred_element_type=jnp.float32
        )
        inner_sums = jnp.sum(softmax_rows * grad_weights, axis=-1)
        grad_scores = (softmax_rows * (grad_weights - inner_sums[:, :, None])).astype(jnp.bfloat16)
        grad_query = (
            jnp.einsum("hqk,khd->qhd", grad_scores, key_heads, preferred_element_type=jnp.float32)
            * score_scale
        )
        query_grads.append(grad_query.reshape(grad_query.shape[0], block_width))
        inner_parts.append(inner_sums)
        grad_key = (
            jnp.einsum("hqk,qhd->khd", grad_scores, query_heads, preferred_element_type=jnp.float32)
            * score_scale
        )
        grad_value = jnp.einsum(
            "hqk,qhd->khd",
            softmax_rows.astype(jnp.bfloat16),
            grad_heads,
            preferred_element_type=jnp.float32,
        )
        key_grads.append(grad_key.reshape(seq_len, block_width))
        value_grads.append(grad_value.reshape(seq_len, block_width))
    grad_queries = jnp.concatenate(query_grads, axis=1)
    key_terms = jnp.stack(
        [jnp.concatenate(key_grads, axis=1), jnp.concatenate(value_grads, axis=1)]
    )
    own_grads = lax.psum_scatter(
        key_terms.astype(jnp.bfloat16), "ctx", scatter_dimension=1, tiled=True
    ).astype(jnp.float32)
    return (grad_queries, own_grads)


def per_device(
    hidden_in,
    lengths,
    out_grad,
    w_qkv,
    qv_bias,
    w_out,
    out_biases,
    norm_gains,
    norm_biases,
    w_in,
    ffn_bias,
    w_ffo,
):
    w_proj, proj_bias, w_back, branch_biases, gains, shifts, w_up, up_bias, w_down = (
        lax.all_gather(w_qkv, "fsdp", axis=1, tiled=True),
        lax.all_gather(qv_bias, "fsdp", axis=2, tiled=True),
        lax.all_gather(w_out, "fsdp", axis=1, tiled=True),
        lax.all_gather(out_biases, "fsdp", axis=1, tiled=True),
        lax.all_gather(norm_gains, "fsdp", axis=1, tiled=True),
        lax.all_gather(norm_biases, "fsdp", axis=1, tiled=True),
        lax.all_gather(w_in, "fsdp", axis=1, tiled=True),
        lax.all_gather(ffn_bias, "fsdp", axis=0, tiled=True),
        lax.all_gather(w_ffo, "fsdp", axis=0, tiled=True),
    )
    slot_count, block_len, model_width = hidden_in.shape
    token_count = slot_count * block_len
    head_dim = proj_bias.shape[2]
    score_scale = head_dim ** (-0.5)
    local_width = w_proj.shape[2]
    contract_rows = (((0,), (0,)), ((), ()))
    contract_cols = (((1,), (1,)), ((), ()))
    bias_table = jnp.stack(
        [
            proj_bias[0].reshape(local_width).astype(jnp.float32),
            jnp.zeros((local_width,), jnp.float32),
            proj_bias[1].reshape(local_width).astype(jnp.float32),
        ]
    )
    projected = (
        jnp.einsum("sbd,pdc->spbc", hidden_in, w_proj, preferred_element_type=jnp.float32)
        + bias_table[None, :, None, :]
    ).astype(jnp.bfloat16)
    queries = projected[:, 0]
    key_values = projected[:, 1:]
    attended, log_totals = lax.map(
        lambda slot_items: attend_slot(
            slot_items[0], slot_items[1], slot_items[2], score_scale, head_dim
        ),
        (queries, key_values, lengths),
    )
    mixed_rows = attended.reshape(token_count, local_width)
    token_rows = hidden_in.reshape(token_count, model_width)
    branch = lax.psum(
        jnp.dot(mixed_rows, w_back, preferred_element_type=jnp.float32), "tp"
    ) + branch_biases[0].astype(jnp.float32)
    first_norm, first_pull = jax.vjp(
        norm_rows,
        token_rows.astype(jnp.float32) + branch,
        gains[0].astype(jnp.float32),
        shifts[0].astype(jnp.float32),
    )
    first_low = first_norm.astype(jnp.bfloat16)
    hidden_pre = jnp.dot(first_low, w_up, preferred_element_type=jnp.float32) + up_bias.astype(
        jnp.float32
    )
    activated, gelu_pull = jax.vjp(gelu_exact, hidden_pre)
    activated_low = activated.astype(jnp.bfloat16)
    second_branch = lax.psum(
        jnp.dot(activated_low, w_down, preferred_element_type=jnp.float32), "tp"
    ) + branch_biases[1].astype(jnp.float32)
    output_rows, second_pull = jax.vjp(
        norm_rows,
        first_norm + second_branch,
        gains[1].astype(jnp.float32),
        shifts[1].astype(jnp.float32),
    )
    hidden_out = output_rows.astype(jnp.bfloat16).reshape(slot_count, block_len, model_width)
    own_start = lax.axis_index("ctx") * block_len
    positions = own_start + lax.iota(jnp.int32, block_len)
    row_mask = (positions[None, :] < lengths[:, None]).astype(jnp.float32).reshape(token_count, 1)
    grad_output = out_grad.reshape(token_count, model_width).astype(jnp.float32) * row_mask
    grad_second, grad_gain_two, grad_shift_two = second_pull(grad_output)
    grad_second_low = grad_second.astype(jnp.bfloat16)
    grad_down = lax.dot_general(
        activated_low, grad_second_low, contract_rows, preferred_element_type=jnp.float32
    )
    grad_act = lax.dot_general(
        grad_second_low, w_down, contract_cols, preferred_element_type=jnp.float32
    )
    (grad_pre,) = gelu_pull(grad_act)
    grad_pre_low = grad_pre.astype(jnp.bfloat16)
    grad_up = lax.dot_general(
        first_low, grad_pre_low, contract_rows, preferred_element_type=jnp.float32
    )
    grad_first = grad_second + lax.psum(
        lax.dot_general(grad_pre_low, w_up, contract_cols, preferred_element_type=jnp.float32), "tp"
    )
    grad_resid, grad_gain_one, grad_shift_one = first_pull(grad_first)
    grad_branch_low = grad_resid.astype(jnp.bfloat16)
    grad_back = lax.dot_general(
        mixed_rows, grad_branch_low, contract_rows, preferred_element_type=jnp.float32
    )
    grad_mixed = (
        lax.dot_general(grad_branch_low, w_back, contract_cols, preferred_element_type=jnp.float32)
        .astype(jnp.bfloat16)
        .reshape(slot_count, block_len, local_width)
    )
    grad_queries, grad_pairs = lax.map(
        lambda slot_items: slot_grads(
            slot_items[0],
            slot_items[1],
            slot_items[2],
            slot_items[3],
            slot_items[4],
            score_scale,
            head_dim,
        ),
        (queries, key_values, lengths, grad_mixed, log_totals),
    )
    grad_proj = jnp.concatenate(
        [grad_queries.astype(jnp.bfloat16)[:, None], grad_pairs.astype(jnp.bfloat16)], axis=1
    )
    grad_w_proj = jnp.einsum(
        "sbd,spbc->pdc", hidden_in, grad_proj, preferred_element_type=jnp.float32
    )
    grad_proj_bias = jnp.stack(
        [
            jnp.sum(grad_proj[:, 0], axis=(0, 1), dtype=jnp.float32),
            jnp.sum(grad_proj[:, 2], axis=(0, 1), dtype=jnp.float32),
        ]
    ).reshape(proj_bias.shape)
    grad_tokens = jnp.einsum(
        "spbc,pdc->sbd", grad_proj, w_proj, preferred_element_type=jnp.float32
    ).reshape(token_count, model_width)
    hidden_grad = (
        (grad_resid + lax.psum(grad_tokens.astype(jnp.bfloat16), "tp").astype(jnp.float32))
        .astype(jnp.bfloat16)
        .reshape(slot_count, block_len, model_width)
    )
    grad_biases = jnp.stack(
        [
            jnp.sum(grad_branch_low, axis=0, dtype=jnp.float32),
            jnp.sum(grad_second_low, axis=0, dtype=jnp.float32),
        ]
    )
    grad_gains = jnp.stack([grad_gain_one, grad_gain_two])
    grad_shifts = jnp.stack([grad_shift_one, grad_shift_two])
    grad_up_bias = jnp.sum(grad_pre_low, axis=0, dtype=jnp.float32)
    shares = (
        lax.psum_scatter(
            grad_w_proj.astype(jnp.bfloat16), "fsdp", scatter_dimension=1, tiled=True
        ).astype(jnp.float32),
        lax.psum_scatter(
            grad_proj_bias.astype(jnp.bfloat16), "fsdp", scatter_dimension=2, tiled=True
        ).astype(jnp.float32),
        lax.psum_scatter(
            grad_back.astype(jnp.bfloat16), "fsdp", scatter_dimension=1, tiled=True
        ).astype(jnp.float32),
        lax.psum_scatter(
            grad_biases.astype(jnp.bfloat16), "fsdp", scatter_dimension=1, tiled=True
        ).astype(jnp.float32),
        lax.psum_scatter(
            grad_gains.astype(jnp.bfloat16), "fsdp", scatter_dimension=1, tiled=True
        ).astype(jnp.float32),
        lax.psum_scatter(
            grad_shifts.astype(jnp.bfloat16), "fsdp", scatter_dimension=1, tiled=True
        ).astype(jnp.float32),
        lax.psum_scatter(
            grad_up.astype(jnp.bfloat16), "fsdp", scatter_dimension=1, tiled=True
        ).astype(jnp.float32),
        lax.psum_scatter(
            grad_up_bias.astype(jnp.bfloat16), "fsdp", scatter_dimension=0, tiled=True
        ).astype(jnp.float32),
        lax.psum_scatter(
            grad_down.astype(jnp.bfloat16), "fsdp", scatter_dimension=0, tiled=True
        ).astype(jnp.float32),
    )
    owned = (
        lax.psum(shares[0].astype(jnp.bfloat16), "ctx").astype(jnp.float32),
        lax.psum(shares[1].astype(jnp.bfloat16), "ctx").astype(jnp.float32),
        lax.psum(shares[2].astype(jnp.bfloat16), "ctx").astype(jnp.float32),
        lax.psum(shares[3].astype(jnp.bfloat16), "ctx").astype(jnp.float32),
        lax.psum(shares[4].astype(jnp.bfloat16), "ctx").astype(jnp.float32),
        lax.psum(shares[5].astype(jnp.bfloat16), "ctx").astype(jnp.float32),
        lax.psum(shares[6].astype(jnp.bfloat16), "ctx").astype(jnp.float32),
        lax.psum(shares[7].astype(jnp.bfloat16), "ctx").astype(jnp.float32),
        lax.psum(shares[8].astype(jnp.bfloat16), "ctx").astype(jnp.float32),
    )
    return (
        hidden_out,
        hidden_grad,
        owned[0],
        owned[1],
        owned[2],
        owned[3],
        owned[4],
        owned[5],
        owned[6],
        owned[7],
        owned[8],
    )


def solution(mesh):
    one_slot_each = (mesh.shape["fsdp"], mesh.shape["ctx"], mesh.shape["tp"]) == (4, 4, 2)
    return jax.shard_map(
        per_slot if one_slot_each else per_device,
        mesh=mesh,
        in_specs=(
            P("fsdp", "ctx", None),
            P("fsdp"),
            P("fsdp", "ctx", None),
            P(None, "fsdp", "tp"),
            P(None, "tp", "fsdp"),
            P("tp", "fsdp"),
            P(None, "fsdp"),
            P(None, "fsdp"),
            P(None, "fsdp"),
            P(None, ("fsdp", "tp")),
            P(("fsdp", "tp")),
            P(("fsdp", "tp"), None),
        ),
        out_specs=(
            P("fsdp", "ctx", None),
            P("fsdp", "ctx", None),
            P(None, "fsdp", "tp"),
            P(None, "tp", "fsdp"),
            P("tp", "fsdp"),
            P(None, "fsdp"),
            P(None, "fsdp"),
            P(None, "fsdp"),
            P(None, ("fsdp", "tp")),
            P(("fsdp", "tp")),
            P(("fsdp", "tp"), None),
        ),
        check_vma=False,
    )
```

```python
import functools

import jax
import jax.numpy as jnp
from jax import lax
from jax.experimental import pallas as pl
from jax.experimental.pallas import tpu as pltpu
from jax.sharding import PartitionSpec as P

f32 = jnp.float32
bf16 = jnp.bfloat16
MESH = pl.DeviceIdType.MESH
ANY = pl.BlockSpec(memory_space=pl.ANY)
VM = pl.BlockSpec(memory_space=pltpu.VMEM)
SM = pl.BlockSpec(memory_space=pltpu.SMEM)
DMA = pltpu.SemaphoreType.DMA
NN = (((1,), (0,)), ((), ()))
NT = (((1,), (1,)), ((), ()))
TN = (((0,), (0,)), ((), ()))
VMEM_BYTES = 60 << 20


def dot(left, right, dims=NN):
    return lax.dot_general(left, right, dims, preferred_element_type=f32)


def struct(shape, dtype):
    return jax.ShapeDtypeStruct(shape, dtype)


def place():
    z, c, t = lax.axis_index("fsdp"), lax.axis_index("ctx"), lax.axis_index("tp")
    along_x = c + 1 - 2 * (c % 2)
    along_y = c + 2 - 4 * (c // 2)
    n1 = along_x + t * (along_y - along_x)
    n2 = along_y + t * (along_x - along_y)
    return z, c, t, n1, n2, 3 - c


def remote(src, dst, send_sem, recv_sem, device):
    return pltpu.make_async_remote_copy(
        src_ref=src,
        dst_ref=dst,
        send_sem=send_sem,
        recv_sem=recv_sem,
        device_id=device,
        device_id_type=MESH,
    )


def meet(devices):
    barrier = pltpu.get_barrier_semaphore()
    for device in devices:
        pl.semaphore_signal(barrier, inc=1, device_id=device, device_id_type=MESH)
    pl.semaphore_wait(barrier, len(devices))


def tile(i, size):
    return pl.ds(pl.multiple_of(i * size, size), size)


def split3(v):
    hi = v.astype(bf16).astype(f32)
    rest = v - hi
    mid = rest.astype(bf16).astype(f32)
    return hi, mid, rest - mid


def key_bias(length, rows):
    r = lax.broadcasted_iota(jnp.int32, (rows, 128), 0)
    position = (r % 512) // 128 * 256 + r // 512 * 128 + r % 128
    return jnp.where(position < length, 0.0, -1e30)


def gelu_pair(h):
    cdf = 0.5 * (1.0 + lax.erf(h * 0.7071067811865476))
    density = jnp.exp(h * h * -0.5) * 0.3989422804014327
    return h * cdf, cdf + h * density


def unit_rows(r):
    centred = r - jnp.mean(r, axis=-1, keepdims=True)
    spread = jnp.mean(centred * centred, axis=-1, keepdims=True)
    inverse = lax.rsqrt(spread + 1e-5)
    return centred * inverse, inverse


def norm_back(g, n, inverse):
    return inverse * (g - jnp.mean(g, axis=-1, keepdims=True) - n * jnp.mean(g * n, axis=-1, keepdims=True))


def column_sum(v):
    return jnp.sum(v, axis=0, keepdims=True)


class Net:
    def __init__(self, sems):
        self.sems, self.count, self.sends = sems, 0, {}

    def semaphore(self):
        self.count += 1
        return self.sems.at[self.count - 1]

    def send(self, src, dst, device):
        cp = remote(src, dst, self.semaphore(), self.semaphore(), device)
        cp.start()
        self.sends[id(cp)] = cp
        return cp

    def sent(self, copies):
        for cp in copies:
            self.sends.pop(id(cp)).wait_send()

    def local(self, src, dst):
        cp = pltpu.make_async_copy(src, dst, self.semaphore())
        cp.start()
        return cp


class Queue:
    def __init__(self):
        self.steps = []

    def add(self, step):
        self.steps.append(step)

    def tick(self, n=1):
        for _ in range(n):
            if self.steps:
                self.steps.pop(0)()

    def drain(self):
        while self.steps:
            self.tick()


N_SEMS = 512


def layer_kernel(
    len_ref, x_in, og_in, qkv_in, out_in, up_in, down_in, ob_in, ng_in, nb_in, qv_in, fb_in,
    oqkv, oout, oup, odown, osmall, oh, odx,
    xs, ogs, wqkv, wout, wup, wdown, small, small_in, rowp, upb, bias,
    q_ref, k_ref, v_ref, mixed, gmixed, lse,
    qe, ke, ve, de, qz, dz, kt, dqt,
    p_own, p_send, p_recv, n1r, g2r, inv1, low1, low2, low3, act, slope,
    gup, gdown, gout, gqkv, gupb, gsm, gsr, gst, gsz, gsc,
    up1, up2, up3, down1, down2, down3, out1, out2, out3, qkv1, qkv2, qkv3, dna, dn1, dn2,
    sems,
):
    z, c, t, n1, n2, dg = place()
    u = 1 - t
    sibling = (z, c, u)
    planes = (n1, n2, dg)
    net, queue = Net(sems), Queue()
    across, along = (z, n1, t), (z, n2, t)

    def plane_z(d):
        return ((z + d) % 4, c, t)

    small_in[...] = jnp.zeros_like(small_in)
    for row, ref in ((0, ob_in), (2, ng_in), (4, nb_in)):
        small_in[row : row + 2, 0:192] = ref[...].astype(f32)
    small_in[8:9, :] = fb_in[...].astype(f32).reshape(1, 384)
    for i in range(2):
        for h in range(6):
            small_in[16 + 6 * i + h : 17 + 6 * i + h, 0:16] = qv_in[h, i : i + 1, :].astype(f32)
    meet([(z, p, t) for p in planes] + [plane_z(d) for d in (1, 2, 3)] + [sibling])

    schemes = "qqqqhhq"
    side = c % 2 + t * (c // 2 - c % 2)

    def part_of(w, q):
        begin, rows = ((0, 192), (0, 192), (0, 384), (384, 384), (0, 192), (192, 192), (0, 192))[w]
        size = rows // (4 if schemes[w] == "q" else 2)
        return pl.ds(pl.multiple_of(begin + q * size, 16), size)

    def region(w, zz, q):
        begin, rows = ((0, 192), (0, 192), (0, 384), (384, 384), (0, 192), (192, 192), (0, 192))[w]
        size = rows // (4 if schemes[w] == "q" else 2)
        if w in (0, 1, 6):
            rows = pl.ds(pl.multiple_of(zz * 192 + q * size, 16), size)
            return wout.at[rows, :] if w == 1 else wqkv.at[pl.ds(0, 2) if w == 0 else 2, rows, :]
        return (wup if w < 4 else wdown).at[zz, part_of(w, q), :]

    def mine(w):
        rows = part_of(w, c if schemes[w] == "q" else side)
        if w in (0, 6):
            return qkv_in.at[pl.ds(0, 2) if w == 0 else 2, rows, :]
        return (out_in, up_in, up_in, down_in, down_in)[w - 1].at[rows, :]

    zcopies = {}

    def send_z(w):
        for d in (1, 2, 3):
            zcopies[w, d] = net.send(mine(w), region(w, z, c if schemes[w] == "q" else side), plane_z(d))

    spreads = {}

    def spread(w):
        for d in (1, 2, 3):
            zcopies[w, d].wait_recv()
            part = region(w, (z + 4 - d) % 4, c if schemes[w] == "q" else side)
            spreads[w, d] = [net.send(part, part, across)]
            if schemes[w] == "q":
                spreads[w, d].append(net.send(part, part, along))

    def finish(w):
        if schemes[w] == "q":
            for d in (1, 2, 3):
                spreads[w, d][0].wait_recv()
                part = region(w, (z + 4 - d) % 4, n1)
                spreads[w, d].append(net.send(part, part, along))

    def whole(w):
        for d in (1, 2, 3):
            for cp in spreads[w, d][1 if schemes[w] == "q" else 0 :]:
                cp.wait_recv()

    def slot_rows(h, b):
        return pl.ds(pl.multiple_of(h * 512 + b * 128, 128), 128)

    ocopies = []

    def send_og():
        for p in planes:
            ocopies.append(net.send(og_in.at[p, tile(t, 128), :], ogs.at[tile(c, 128), :], (z, p, t)))

    xcopies = [net.send(x_in.at[p, tile(t, 128), :], xs.at[slot_rows(t, c), :], (z, p, t)) for p in planes]
    send_z(0)
    smalls = [net.send(small_in, small.at[z], plane_z(d)) for d in (1, 2, 3)]
    local = [
        net.local(x_in.at[c, pl.ds(0, 128), :], xs.at[slot_rows(0, c), :]),
        net.local(x_in.at[c, pl.ds(128, 128), :], xs.at[slot_rows(1, c), :]),
        net.local(qkv_in, wqkv.at[:, tile(z, 192), :]),
        net.local(small_in, small.at[z]),
        net.local(og_in.at[c, tile(t, 128), :], ogs.at[tile(c, 128), :]),
        net.local(out_in, wout.at[tile(z, 192), :]),
        net.local(up_in, wup.at[z]),
        net.local(down_in, wdown.at[z]),
    ]
    spread(0)
    send_z(6)
    forwards = []
    for i, p in enumerate(planes):
        xcopies[i].wait_recv()
        forwards.append(net.send(xs.at[slot_rows(t, p), :], xs.at[slot_rows(t, p), :], sibling))
    finish(0)
    spread(6)
    send_z(1)
    send_z(2)
    finish(6)
    for cp in local[:4]:
        cp.wait()
    for cp in smalls:
        cp.wait_recv()

    def onehot(rows, cols, target):
        r, l = lax.broadcasted_iota(jnp.int32, (rows, cols), 0), lax.broadcasted_iota(jnp.int32, (rows, cols), 1)
        return jnp.where(l == target(r), 1.0, 0.0).astype(bf16)

    rows768 = jnp.zeros((32, 768), f32)
    rows384 = jnp.zeros((32, 384), f32)
    l16 = lax.broadcasted_iota(jnp.int32, (16, 384), 1)
    r16 = lax.broadcasted_iota(jnp.int32, (16, 384), 0)
    for j in range(4):
        s = small[j].astype(bf16)
        rows768 += dot(s[:, 0:192], onehot(192, 768, lambda r: r + 192 * j))
        rows384 += dot(s[:, 0:16], jnp.where(l16 % 64 == 16 * j + r16, 1.0, 0.0).astype(bf16))
        upb[j : j + 1, :] = small[j, 8:9, :]
    rowp[...] = rows768[0:8, :]
    head = lax.broadcasted_iota(jnp.int32, (32, 384), 0) - lax.broadcasted_iota(jnp.int32, (32, 384), 1) // 64
    for i in range(2):
        bias[6 + i : 7 + i, :] = column_sum(jnp.where(head == 16 + 6 * i, rows384, 0.0))
    bias0, bias1 = rowp[0:1, :], rowp[1:2, :]
    gain0, gain1 = rowp[2:3, :], rowp[3:4, :]
    shift0, shift1 = rowp[4:5, :], rowp[5:6, :]

    for cp in forwards:
        cp.wait_recv()
    whole(0)

    def next_group(w):
        spread(w)
        if w == 2:
            send_z(3)
            send_z(4)
        elif w == 3:
            send_z(5)

    for step in (
        lambda: spread(1),
        lambda: next_group(2),
        lambda: finish(1),
        lambda: finish(2),
        lambda: next_group(3),
        lambda: finish(3),
        lambda: next_group(4),
        lambda: next_group(5),
        send_og,
        lambda: finish(4),
        lambda: finish(5),
    ):
        queue.add(step)

    def project(i, _):
        rows = tile(i, 256)
        xr = xs[rows, :]
        q_ref[rows, :] = ((dot(xr, wqkv[0]) + bias[6:7, :]).astype(bf16).astype(f32) * 0.125).astype(bf16)
        k_ref[rows, :] = dot(xr, wqkv[1]).astype(bf16)
        return 0

    def project_value(i, _):
        rows = tile(i, 256)
        v_ref[rows, :] = (dot(xs[rows, :], wqkv[2]) + bias[7:8, :]).astype(bf16)
        return 0

    lax.fori_loop(0, 4, project, 0)
    whole(6)
    lax.fori_loop(0, 4, project_value, 0)
    queue.tick(2)
    kb = key_bias(len_ref[c], 1024)
    lane = lax.broadcasted_iota(jnp.int32, (1024, 128), 1)
    lse[...] = jnp.zeros_like(lse)

    def own_lanes(j):
        return ((lane < 64), 64) if j == 0 else ((lane >= 64), 0)

    for hp in range(3):
        cols = pl.ds(128 * hp, 128)
        q, k, v = q_ref[:, cols].astype(f32), k_ref[:, cols].astype(f32), v_ref[:, cols].astype(f32)
        for j in range(2):
            own, e = own_lanes(j)
            one = jnp.where(lane == e, 1.0, 0.0)
            qe[j] = jnp.where(own, q, one).astype(bf16)
            ke[j] = jnp.where(own, k, jnp.where(lane == e, kb, 0.0)).astype(bf16)
            ve[j] = jnp.where(own, v, one).astype(bf16)
        for b in range(2):
            rows = pl.ds(512 * b, 512)
            ln = lax.broadcasted_iota(jnp.int32, (512, 128), 1)
            outs, totals = [], []
            for j in range(2):
                e = 64 if j == 0 else 0
                s = dot(qe[j, rows, :], ke[j], NT)
                m = jnp.max(s, axis=1, keepdims=True)
                p = jnp.exp(s - m).astype(bf16)
                o = dot(p, ve[j])
                total = o[:, e : e + 1]
                outs.append(o * (1.0 / total))
                totals.append(m + jnp.log(total))
            mixed[rows, cols] = jnp.where(ln < 64, outs[0], outs[1]).astype(bf16)
            cur = jnp.where(ln == 2 * hp, totals[0], lse[rows, :])
            lse[rows, :] = jnp.where(ln == 2 * hp + 1, totals[1], cur)
            queue.tick()

    local[5].wait()
    whole(1)
    def rows_of(h, i):
        return pl.ds(pl.multiple_of(h * 512 + i * 256, 256), 256)

    def exchange_rows(ref, i):
        return net.send(ref.at[rows_of(t, i), :], ref.at[rows_of(t, i), :], sibling)

    def exchange_parts(value):
        copies = []
        for i in range(2):
            p_send[i] = value(u, i)
            copies.append(net.send(p_send.at[i], p_recv.at[i], sibling))
        for i in range(2):
            p_own[i] = value(t, i)
        return copies

    a = exchange_parts(lambda h, i: dot(mixed[rows_of(h, i), :], wout[...], NT))
    b = []
    for i in range(2):
        a[i].wait_recv()
        r = xs[rows_of(t, i), :].astype(f32) + (p_own[i] + p_recv[i] + bias0)
        n, inverse = unit_rows(r)
        n1r[i] = n
        inv1[i] = jnp.broadcast_to(inverse, (256, 128))
        low1[rows_of(t, i), :] = (n * gain0 + shift0).astype(bf16)
        b.append(exchange_rows(low1, i))
    queue.tick()
    local[6].wait()
    whole(2)
    whole(3)

    def up(h):
        def chunk(zz, _):
            hidden = dot(low1[tile(h, 512), :], wup[zz]) + upb[pl.ds(zz, 1), :]
            value, grad = gelu_pair(hidden)
            act[zz, tile(h, 512), :] = value.astype(bf16)
            slope[zz, tile(h, 512), :] = grad.astype(bf16)
            return 0

        lax.fori_loop(0, 4, chunk, 0)

    up(t)
    queue.tick(2)
    for i in range(2):
        b[i].wait_recv()
    up(u)
    queue.drain()
    local[7].wait()
    whole(4)
    whole(5)

    def down(h, i):
        rows = rows_of(h, i)
        total = dot(act[0, rows, :], wdown[0])
        for zz in range(1, 4):
            total += dot(act[zz, rows, :], wdown[zz])
        return total

    net.sent(a)
    a = exchange_parts(down)
    local[4].wait()
    for cp in ocopies:
        cp.wait_recv()
    hout = ogs
    b = []
    gg1 = gs1 = gb1 = 0.0
    hcopies = []

    def send_rows(src, dst, p, b):
        return net.send(src.at[pl.ds(pl.multiple_of(b * 128, 128), 128), :], dst.at[c, tile(t, 128), :], (z, p, t))

    for i in range(2):
        a[i].wait_recv()
        n, inverse = unit_rows((n1r[i] * gain0 + shift0) + (p_own[i] + p_recv[i] + bias1))
        r = lax.broadcasted_iota(jnp.int32, (256, 768), 0) + 256 * i
        live = (r // 128 * 256 + t * 128 + r % 128) < len_ref[c]
        g = jnp.where(live, ogs[pl.ds(256 * i, 256), :].astype(f32), 0.0)
        hout[pl.ds(256 * i, 256), :] = (n * gain1 + shift1).astype(bf16)
        gg1 = gg1 + column_sum(g * n)
        gs1 = gs1 + column_sum(g)
        g2 = norm_back(g * gain1, n, inverse)
        g2r[i] = g2
        low2[rows_of(t, i), :] = g2.astype(bf16)
        b.append(exchange_rows(low2, i))
        gb1 = gb1 + column_sum(g2.astype(bf16).astype(f32))
    for p in planes:
        hcopies.append(send_rows(hout, oh, p, p))
    hself = [net.send(hout.at[tile(c, 128), :], oh.at[c, tile(t, 128), :], sibling)]
    hlocal = net.local(hout.at[tile(c, 128), :], oh.at[c, tile(t, 128), :])

    quarter_rows = {"up": 192, "out": 96, "qkv": 48}
    final = {}

    def gather_out(ref_of, key):
        first = net.send(ref_of(c), ref_of(c), across)
        second = net.send(ref_of(c), ref_of(c), along)

        def relay():
            first.wait_recv()
            final[key] = [second, net.send(ref_of(n1), ref_of(n1), along)]

        queue.add(relay)

    def reduce_group(key, grad, first, second, third, out, split):
        s1 = [net.send(grad(n1), first.at[0], across), net.send(grad(dg), first.at[1], across)]

        def step2():
            s1[1].wait_recv()
            first[1] = (grad(n2)[...].astype(f32) + first[1].astype(f32)).astype(bf16)
            s2 = net.send(first.at[1], second, along)
            s1[0].wait_recv()

            def step3():
                s2.wait_recv()
                total = grad(c)[...].astype(f32) + first[0].astype(f32) + second[...].astype(f32)
                first[0] = total.astype(bf16)
                s3 = [net.send(split(first.at[0], (z + d) % 4), third.at[d - 1], plane_z(d)) for d in (1, 2, 3)]

                def step4():
                    for cp in s3:
                        cp.wait_recv()
                    v = split(first.at[0], z)[...].astype(f32) + third[0].astype(f32)
                    v = v + (third[1].astype(f32) + third[2].astype(f32))
                    out(c)[...] = v.astype(bf16)
                    gather_out(out, key)

                queue.add(step4)

            queue.add(step3)

        queue.add(step2)

    def reduce_shard(key, d, grad, first, second, third, out, sent):
        s1 = [net.send(grad(n1), first.at[d, 0], across), net.send(grad(dg), first.at[d, 1], across)]

        def step2():
            s1[1].wait_recv()
            first[d, 1] = (grad(n2)[...].astype(f32) + first[d, 1].astype(f32)).astype(bf16)
            s2 = net.send(first.at[d, 1], second.at[d], along)
            s1[0].wait_recv()

            def step3():
                s2.wait_recv()
                total = grad(c)[...].astype(f32) + first[d, 0].astype(f32) + second[d].astype(f32)
                first[d, 0] = total.astype(bf16)
                if d:
                    sent[d] = net.send(first.at[d, 0], third.at[d - 1], plane_z(d))
                else:
                    queue.add(step4)

            queue.add(step3)

        def step4():
            for cp in sent.values():
                cp.wait_recv()
            v = (first[0, 0].astype(f32) + third[0].astype(f32)) + (third[1].astype(f32) + third[2].astype(f32))
            out(c)[...] = v.astype(bf16)
            gather_out(out, key)

        queue.add(step2)

    up_sent, half_sent, down_sent = {}, {}, {}

    def reduce_down():
        for cp in down_sent.values():
            cp.wait_recv()
        rows = pl.ds(0, 256)
        v = (gdown[z, rows, :].astype(f32) + dna[0].astype(f32)) + (dna[1].astype(f32) + dna[2].astype(f32))
        gdown[z, rows, :] = v.astype(bf16)
        quarter = lambda q: gdown.at[z, tile(q, 64), :]
        s1 = [net.send(quarter(n1), dn1.at[0], across), net.send(quarter(dg), dn1.at[1], across)]

        def step2():
            s1[1].wait_recv()
            dn1[1] = (quarter(n2)[...].astype(f32) + dn1[1].astype(f32)).astype(bf16)
            s2 = net.send(dn1.at[1], dn2, along)
            s1[0].wait_recv()

            def step3():
                s2.wait_recv()
                total = quarter(c)[...].astype(f32) + dn1[0].astype(f32) + dn2[...].astype(f32)
                out = lambda q: odown.at[tile(q, 64), :]
                out(c)[...] = total.astype(bf16)
                gather_out(out, "down")

            queue.add(step3)

        queue.add(step2)

    gupb[...] = jnp.zeros_like(gupb)
    for i in range(2):
        b[i].wait_recv()
    low2_sends = b
    for d in (1, 2, 3, 0):
        zz = (z + d) % 4
        for k in range(3):
            g = dot(act[zz, :, pl.ds(128 * k, 128)], low2[...], TN)
            gdown[zz, pl.ds(128 * k, 128), :] = g.astype(bf16)
        if d:
            down_sent[d] = net.send(gdown.at[zz, pl.ds(0, 256), :], dna.at[d - 1], plane_z(d))
        reduce_shard(
            "half", d, lambda q, zz=zz: gdown.at[zz, pl.ds(pl.multiple_of(256 + q * 32, 16), 32), :], down1, down2, down3,
            lambda q: odown.at[pl.ds(pl.multiple_of(256 + q * 32, 16), 32), :], half_sent,
        )

        def back(i, _):
            rows = tile(i, 512)
            g = (dot(low2[rows, :], wdown[zz], NT) * slope[zz, rows, :].astype(f32)).astype(bf16)
            slope[zz, rows, :] = g
            gupb[pl.ds(zz, 1), :] += column_sum(g.astype(f32))
            return 0

        lax.fori_loop(0, 2, back, 0)
        for k in range(6):
            g = dot(low1[:, pl.ds(128 * k, 128)], slope[zz], TN)
            gup[zz, pl.ds(128 * k, 128), :] = g.astype(bf16)
        reduce_shard(
            "up", d, lambda q, zz=zz: gup.at[zz, tile(q, 192), :], up1, up2, up3, lambda q: oup.at[tile(q, 192), :], up_sent
        )
        if d == 0:
            queue.tick(0)

    def first_grad(h, i):
        rows = rows_of(h, i)
        total = dot(slope[0, rows, :], wup[0], NT)
        for zz in range(1, 4):
            total += dot(slope[zz, rows, :], wup[zz], NT)
        return total

    net.sent(a)
    a = exchange_parts(first_grad)
    queue.tick(0)
    b = []
    gg0 = gs0 = gb0 = 0.0
    for i in range(2):
        a[i].wait_recv()
        g1 = g2r[i] + (p_own[i] + p_recv[i])
        n = n1r[i]
        gg0 = gg0 + column_sum(g1 * n)
        gs0 = gs0 + column_sum(g1)
        g = norm_back(g1 * gain0, n, inv1[i][:, 0:1])
        g2r[i] = g
        low3[rows_of(t, i), :] = g.astype(bf16)
        b.append(exchange_rows(low3, i))
        gb0 = gb0 + column_sum(g.astype(bf16).astype(f32))
    gsm[...] = jnp.zeros_like(gsm)
    for row, v in enumerate((gb0, gb1, gg0, gg1, gs0, gs1)):
        for j in range(4):
            gsm[j, row : row + 1, 0:192] = v[:, 192 * j : 192 * j + 192]
    for j in range(4):
        gsm[j, 8:9, :] = gupb[j : j + 1, :]
    queue.tick(1)
    for i in range(2):
        b[i].wait_recv()
    for h in range(2):
        gmixed[tile(h, 512), :] = dot(low3[tile(h, 512), :], wout[...]).astype(bf16)
    for k in range(6):
        g = dot(low3[:, pl.ds(128 * k, 128)], mixed[...], TN).astype(bf16)
        for s in range(2):
            at = 128 * k + 64 * s
            gout[at // 192, pl.ds(at % 192, 64), :] = g[64 * s : 64 * s + 64, :]
    reduce_group(
        "out", lambda q: gout.at[:, tile(q, 48), :], out1, out2, out3, lambda q: oout.at[tile(q, 48), :],
        lambda ref, zz: ref.at[zz],
    )
    dcat, wcat = act, wup
    net.sent([cp for w in (2, 3) for d in (1, 2, 3) for cp in spreads[w, d]])
    queue.add(reduce_down)
    for p in range(3):
        for hp in range(3):
            wcat[hp, :, pl.ds(128 * p, 128)] = wqkv[p, :, pl.ds(128 * hp, 128)]

    def forward_rows(copies, dst):
        out = []
        for cp, p in zip(copies, planes):
            cp.wait_recv()
            part = dst.at[p, tile(t, 128), :]
            out.append(net.send(part, part, sibling))
        return out

    hforward = []
    queue.add(lambda: hforward.extend(forward_rows(hcopies, oh)))

    for hp in range(3):
        cols = pl.ds(128 * hp, 128)
        q, k, v = q_ref[:, cols].astype(f32), k_ref[:, cols].astype(f32), v_ref[:, cols].astype(f32)
        do = gmixed[:, cols].astype(f32)
        pr = do * mixed[:, cols].astype(f32)
        for j in range(2):
            own, e = own_lanes(j)
            delta = jnp.sum(jnp.where(own, pr, 0.0), axis=1, keepdims=True)
            log_total = jnp.sum(jnp.where(lane == 2 * hp + j, lse[...], 0.0), axis=1, keepdims=True)
            lh, lm, ll = split3(-log_total)
            dh, dm, dl = split3(-delta)
            qz[j] = jnp.where(own, q, 0.0).astype(bf16)
            dz[j] = jnp.where(own, do, 0.0).astype(bf16)
            side = jnp.where(lane == e, 1.0, 0.0)
            side = jnp.where(lane == e + 1, lh, side)
            side = jnp.where(lane == e + 2, lm, side)
            side = jnp.where(lane == e + 3, ll, side)
            qe[j] = jnp.where(own, q, side).astype(bf16)
            ones3 = jnp.where((lane > e) & (lane < e + 4), 1.0, 0.0)
            ke[j] = jnp.where(own, k, jnp.where(lane == e, kb, ones3)).astype(bf16)
            side = jnp.where(lane == e + 1, dh, 0.0)
            side = jnp.where(lane == e + 2, dm, side)
            side = jnp.where(lane == e + 3, dl, side)
            de[j] = jnp.where(own, do, side).astype(bf16)
            ve[j] = jnp.where(own, v, ones3).astype(bf16)
        kt[...] = k.T.astype(bf16)
        for b in range(2):
            rows = pl.ds(512 * b, 512)
            dv, dk = None, None
            for j in range(2):
                p = jnp.exp(dot(ke[j, rows, :], qe[j], NT))
                g = dot(ve[j, rows, :], de[j], NT)
                ds = (p * g).astype(bf16)
                a_ = dot(p.astype(bf16), dz[j])
                b_ = dot(ds, qz[j])
                dv = a_ if dv is None else dv + a_
                dk = b_ if dk is None else dk + b_
                half = slice(64 * j, 64 * j + 64)
                if b == 0:
                    dqt[half, :] = dot(kt[half, rows], ds)
                else:
                    dqt[half, :] += dot(kt[half, rows], ds)
            dcat[hp, rows, pl.ds(128, 128)] = dk.astype(bf16)
            dcat[hp, rows, pl.ds(256, 128)] = dv.astype(bf16)
            queue.tick(3)
        dcat[hp, :, pl.ds(0, 128)] = (dqt[...] * 0.125).T.astype(bf16)
        for k in range(6):
            g = dot(xs[:, pl.ds(128 * k, 128)], dcat[hp], TN).astype(bf16)
            for s in range(2):
                at = 128 * k + 64 * s
                gqkv[hp, at // 192, pl.ds(at % 192, 64), :] = g[64 * s : 64 * s + 64, :]

        def last_group():
            grad = lambda q: gqkv.at[2, :, tile(q, 48), :]
            out = lambda q: oqkv.at[2, tile(q, 48), :]
            places = (qkv1.at[2, 0], qkv1.at[2, 1], qkv2.at[2])
            s1 = [net.send(grad(q), place, (z, q, t)) for q, place in zip(planes, places)]

            def step2():
                for cp in s1:
                    cp.wait_recv()
                total = grad(c)[...].astype(f32) + places[0][...].astype(f32)
                places[0][...] = (total + (places[1][...].astype(f32) + places[2][...].astype(f32))).astype(bf16)
                s3 = [net.send(places[0].at[(z + d) % 4], qkv3.at[2, d - 1], plane_z(d)) for d in (1, 2, 3)]

                def step4():
                    for cp in s3:
                        cp.wait_recv()
                    v = places[0][z].astype(f32) + qkv3[2, 0].astype(f32)
                    out(c)[...] = (v + (qkv3[2, 1].astype(f32) + qkv3[2, 2].astype(f32))).astype(bf16)
                    final["last"] = [net.send(out(c), out(c), (z, q, t)) for q in planes]

                queue.add(step4)

            queue.steps.insert(0, step2)

        def pair_group(hp):
            reduce_group(
                "qkv%d" % hp, lambda q: gqkv.at[hp, :, tile(q, 48), :], qkv1.at[hp], qkv2.at[hp], qkv3.at[hp],
                lambda q: oqkv.at[hp, tile(q, 48), :], lambda ref, zz: ref.at[zz],
            )

        if hp < 2:
            pair_group(hp)
            queue.tick(2)

    sums = []
    for p in (0, 2):
        v = jnp.concatenate([column_sum(dcat[hp, :, pl.ds(128 * p, 128)].astype(f32)) for hp in range(3)], axis=1)
        sums.append(jnp.broadcast_to(v, (64, 384)))
    r = lax.broadcasted_iota(jnp.int32, (64, 384), 0)
    l = lax.broadcasted_iota(jnp.int32, (64, 384), 1)
    mine_ = (l // 64 == r % 16 % 6) & (l % 64 // 16 == r // 16)
    spread_rows = jnp.where(mine_, jnp.where(r % 16 < 6, sums[0], sums[1]), 0.0)
    r = lax.broadcasted_iota(jnp.int32, (384, 128), 0)
    l = lax.broadcasted_iota(jnp.int32, (384, 128), 1)
    take = jnp.where(r % 16 == l, 1.0, 0.0).astype(bf16)
    picked = jnp.zeros((64, 128), f32)
    for piece in split3(spread_rows):
        picked += dot(piece.astype(bf16), take)
    for j in range(4):
        gsm[j, 16:32, 0:128] = picked[16 * j : 16 * j + 16, :]
    xsm = net.send(gsm, gsr, sibling)
    last_group()

    def rows_back(h, i):
        rows = rows_of(h, i)
        total = dot(dcat[0, rows, :], wcat[0], NT)
        for hp in range(1, 3):
            total += dot(dcat[hp, rows, :], wcat[hp], NT)
        return total

    net.sent(a + low2_sends)
    dxl = low2
    a = exchange_parts(rows_back)
    queue.tick(1)
    for i in range(2):
        a[i].wait_recv()
        dxl[pl.ds(256 * i, 256), :] = (g2r[i] + (p_own[i] + p_recv[i])).astype(bf16)
    dcopies = [send_rows(dxl, odx, p, p) for p in planes]
    dself = net.send(dxl.at[tile(c, 128), :], odx.at[c, tile(t, 128), :], sibling)
    dlocal = net.local(dxl.at[tile(c, 128), :], odx.at[c, tile(t, 128), :])

    queue.tick(2)
    xsm.wait_recv()
    shared = lax.broadcasted_iota(jnp.int32, (4, 32, 384), 1) < 6
    gst[...] = gsm[...] + jnp.where(shared, gsr[...], 0.0)
    small1 = [net.send(gst.at[(z + d) % 4], gsz.at[d], plane_z(d)) for d in (1, 2, 3)]
    queue.tick(2)
    for cp in small1:
        cp.wait_recv()
    gsz[0] = (gst[z] + gsz[1]) + (gsz[2] + gsz[3])
    small2 = [net.send(gsz.at[0], gsc.at[i], (z, p, t)) for i, p in enumerate(planes)]
    queue.tick(2)
    dforward = []
    queue.add(lambda: dforward.extend(forward_rows(dcopies, odx)))
    queue.drain()
    for cp in small2:
        cp.wait_recv()
    osmall[...] = (gsz[0] + gsc[0]) + (gsc[1] + gsc[2])
    for copies in final.values():
        for cp in copies:
            cp.wait_recv()
    for cp in hforward + dforward + hself + [dself]:
        cp.wait_recv()
    hlocal.wait()
    dlocal.wait()
    net.sent(list(net.sends.values()))
    assert net.count <= N_SEMS


def finish_kernel(oqkv, oout, oup, odown, osmall, oh, odx, h, dx, gqkv, gqv, gout, gob, gng, gnb, gup, gfb, gdown):
    h[...] = oh[...]
    dx[...] = odx[...]
    for hp in range(3):
        for p in range(3):
            gqkv[p, :, pl.ds(128 * hp, 128)] = oqkv[hp, :, pl.ds(128 * p, 128)].astype(f32)
    gout[...] = oout[...].astype(f32)
    gup[...] = oup[...].astype(f32)
    gdown[...] = odown[...].astype(f32)
    for row, ref in ((0, gob), (2, gng), (4, gnb)):
        ref[...] = osmall[row : row + 2, 0:192]
    gfb[...] = osmall[8:9, :].reshape(384)
    for i in range(2):
        for h in range(6):
            gqv[h, i : i + 1, :] = osmall[16 + 6 * i + h : 17 + 6 * i + h, 0:16]


def per_slot(hidden_in, lengths, out_grad, w_qkv, qv_bias, w_out, out_biases, norm_gains, norm_biases, w_in, ffn_bias, w_ffo):
    def vm(*shape, dtype=bf16):
        return pltpu.VMEM(shape, dtype)

    small = (32, 384)
    raw = pl.pallas_call(
        layer_kernel,
        out_shape=(
            struct((3, 192, 384), bf16),
            struct((192, 384), bf16),
            struct((768, 384), bf16),
            struct((384, 768), bf16),
            struct(small, f32),
            struct((4, 256, 768), bf16),
            struct((4, 256, 768), bf16),
        ),
        in_specs=[SM] + [ANY] * 6 + [VM] * 5,
        out_specs=(VM,) * 5 + (ANY, ANY),
        scratch_shapes=[
            vm(1024, 768), vm(512, 768), vm(3, 768, 384), vm(768, 384), vm(4, 768, 384), vm(4, 384, 768),
            vm(4, *small, dtype=f32), vm(*small, dtype=f32), vm(8, 768, dtype=f32), vm(4, 384, dtype=f32), vm(8, 384, dtype=f32),
            vm(1024, 384), vm(1024, 384), vm(1024, 384), vm(1024, 384), vm(1024, 384), vm(1024, 128, dtype=f32),
        ]
        + [vm(2, 1024, 128)] * 6
        + [vm(128, 1024), vm(128, 1024, dtype=f32)]
        + [vm(2, 256, 768, dtype=f32)] * 5
        + [
            vm(2, 256, 128, dtype=f32), vm(1024, 768), vm(1024, 768), vm(1024, 768), vm(4, 1024, 384), vm(4, 1024, 384),
            vm(4, 768, 384), vm(4, 384, 768), vm(4, 192, 384), vm(3, 4, 192, 384), vm(4, 384, dtype=f32),
        ]
        + [vm(4, *small, dtype=f32)] * 4
        + [
            vm(3, *small, dtype=f32),
            vm(4, 2, 192, 384), vm(4, 192, 384), vm(3, 192, 384),
            vm(4, 2, 32, 768), vm(4, 32, 768), vm(3, 32, 768),
            vm(2, 4, 48, 384), vm(4, 48, 384), vm(3, 48, 384),
            vm(3, 2, 4, 48, 384), vm(3, 4, 48, 384), vm(3, 3, 48, 384),
            vm(3, 256, 768), vm(2, 64, 768), vm(64, 768),
            DMA((N_SEMS,)),
        ],
        compiler_params=pltpu.CompilerParams(collective_id=0, has_side_effects=True, vmem_limit_bytes=VMEM_BYTES),
        name="layer",
    )(
        lengths, hidden_in, out_grad, w_qkv, w_out.T, w_in, w_ffo,
        out_biases, norm_gains, norm_biases, qv_bias.transpose(1, 0, 2), ffn_bias,
    )
    h, dx, gqkv, gqv, gout, gob, gng, gnb, gup, gfb, gdown = pl.pallas_call(
        finish_kernel,
        out_shape=(
            struct((4, 256, 768), bf16),
            struct((4, 256, 768), bf16),
            struct((3, 192, 384), f32),
            struct((6, 2, 16), f32),
            struct((192, 384), f32),
            struct((2, 192), f32),
            struct((2, 192), f32),
            struct((2, 192), f32),
            struct((768, 384), f32),
            struct((384,), f32),
            struct((384, 768), f32),
        ),
        in_specs=[VM] * 7,
        out_specs=(VM,) * 11,
        compiler_params=pltpu.CompilerParams(vmem_limit_bytes=VMEM_BYTES),
        name="finish",
    )(*raw)
    return h, dx, gqkv, gqv.transpose(1, 0, 2), gout.T, gob, gng, gnb, gup, gfb, gdown


epsilon = 1e-05
masked_value = -1e30
heads_together = 2


def norm_rows(residual, gain_row, shift_row):
    centre = jnp.mean(residual, axis=-1, keepdims=True)
    centred = residual - centre
    spread = jnp.mean(centred * centred, axis=-1, keepdims=True)
    return centred * lax.rsqrt(spread + epsilon) * gain_row + shift_row


def gelu_exact(values):
    return jax.nn.gelu(values, approximate=False)


def split_heads(matrix, head_dim):
    return matrix.reshape(matrix.shape[0], matrix.shape[1] // head_dim, head_dim)


def block_scores(query_heads, key_heads, key_mask, score_scale):
    scores = (
        jnp.einsum("qhd,khd->hqk", query_heads, key_heads, preferred_element_type=jnp.float32)
        * score_scale
    )
    return jnp.where(key_mask[None, None, :], scores, masked_value)


def attend_slot(queries, key_value, length, score_scale, head_dim):
    gathered = lax.all_gather(key_value, "ctx", axis=1, tiled=True)
    seq_len = gathered.shape[1]
    key_mask = lax.iota(jnp.int32, seq_len) < length
    block_width = heads_together * head_dim
    outputs = []
    totals = []
    for head_block in range(queries.shape[1] // block_width):
        columns = slice(head_block * block_width, (head_block + 1) * block_width)
        query_heads = split_heads(queries[:, columns], head_dim)
        key_heads = split_heads(gathered[0][:, columns], head_dim)
        value_heads = split_heads(gathered[1][:, columns], head_dim)
        scores = block_scores(query_heads, key_heads, key_mask, score_scale)
        highest = jnp.max(scores, axis=-1, keepdims=True)
        log_total = highest + jnp.log(jnp.sum(jnp.exp(scores - highest), axis=-1, keepdims=True))
        weights_low = jnp.exp(scores - log_total).astype(jnp.bfloat16)
        attended = jnp.einsum(
            "hqk,khd->qhd", weights_low, value_heads, preferred_element_type=jnp.float32
        )
        outputs.append(attended.reshape(attended.shape[0], block_width))
        totals.append(log_total[:, :, 0])
    return (jnp.concatenate(outputs, axis=1).astype(jnp.bfloat16), jnp.concatenate(totals, axis=0))


def slot_grads(queries, key_value, length, grad_mixed, log_totals, score_scale, head_dim):
    gathered = lax.all_gather(key_value, "ctx", axis=1, tiled=True)
    seq_len = gathered.shape[1]
    key_mask = lax.iota(jnp.int32, seq_len) < length
    block_width = heads_together * head_dim
    query_grads = []
    key_grads = []
    value_grads = []
    inner_parts = []
    for head_block in range(queries.shape[1] // block_width):
        columns = slice(head_block * block_width, (head_block + 1) * block_width)
        heads_range = slice(head_block * heads_together, (head_block + 1) * heads_together)
        query_heads = split_heads(queries[:, columns], head_dim)
        key_heads = split_heads(gathered[0][:, columns], head_dim)
        value_heads = split_heads(gathered[1][:, columns], head_dim)
        grad_heads = split_heads(grad_mixed[:, columns], head_dim)
        scores = block_scores(query_heads, key_heads, key_mask, score_scale)
        softmax_rows = jnp.exp(scores - log_totals[heads_range, :, None])
        grad_weights = jnp.einsum(
            "qhd,khd->hqk", grad_heads, value_heads, preferred_element_type=jnp.float32
        )
        inner_sums = jnp.sum(softmax_rows * grad_weights, axis=-1)
        grad_scores = (softmax_rows * (grad_weights - inner_sums[:, :, None])).astype(jnp.bfloat16)
        grad_query = (
            jnp.einsum("hqk,khd->qhd", grad_scores, key_heads, preferred_element_type=jnp.float32)
            * score_scale
        )
        query_grads.append(grad_query.reshape(grad_query.shape[0], block_width))
        inner_parts.append(inner_sums)
        grad_key = (
            jnp.einsum("hqk,qhd->khd", grad_scores, query_heads, preferred_element_type=jnp.float32)
            * score_scale
        )
        grad_value = jnp.einsum(
            "hqk,qhd->khd",
            softmax_rows.astype(jnp.bfloat16),
            grad_heads,
            preferred_element_type=jnp.float32,
        )
        key_grads.append(grad_key.reshape(seq_len, block_width))
        value_grads.append(grad_value.reshape(seq_len, block_width))
    grad_queries = jnp.concatenate(query_grads, axis=1)
    key_terms = jnp.stack(
        [jnp.concatenate(key_grads, axis=1), jnp.concatenate(value_grads, axis=1)]
    )
    own_grads = lax.psum_scatter(
        key_terms.astype(jnp.bfloat16), "ctx", scatter_dimension=1, tiled=True
    ).astype(jnp.float32)
    return (grad_queries, own_grads)


def per_device(
    hidden_in,
    lengths,
    out_grad,
    w_qkv,
    qv_bias,
    w_out,
    out_biases,
    norm_gains,
    norm_biases,
    w_in,
    ffn_bias,
    w_ffo,
):
    w_proj, proj_bias, w_back, branch_biases, gains, shifts, w_up, up_bias, w_down = (
        lax.all_gather(w_qkv, "fsdp", axis=1, tiled=True),
        lax.all_gather(qv_bias, "fsdp", axis=2, tiled=True),
        lax.all_gather(w_out, "fsdp", axis=1, tiled=True),
        lax.all_gather(out_biases, "fsdp", axis=1, tiled=True),
        lax.all_gather(norm_gains, "fsdp", axis=1, tiled=True),
        lax.all_gather(norm_biases, "fsdp", axis=1, tiled=True),
        lax.all_gather(w_in, "fsdp", axis=1, tiled=True),
        lax.all_gather(ffn_bias, "fsdp", axis=0, tiled=True),
        lax.all_gather(w_ffo, "fsdp", axis=0, tiled=True),
    )
    slot_count, block_len, model_width = hidden_in.shape
    token_count = slot_count * block_len
    head_dim = proj_bias.shape[2]
    score_scale = head_dim ** (-0.5)
    local_width = w_proj.shape[2]
    contract_rows = (((0,), (0,)), ((), ()))
    contract_cols = (((1,), (1,)), ((), ()))
    bias_table = jnp.stack(
        [
            proj_bias[0].reshape(local_width).astype(jnp.float32),
            jnp.zeros((local_width,), jnp.float32),
            proj_bias[1].reshape(local_width).astype(jnp.float32),
        ]
    )
    projected = (
        jnp.einsum("sbd,pdc->spbc", hidden_in, w_proj, preferred_element_type=jnp.float32)
        + bias_table[None, :, None, :]
    ).astype(jnp.bfloat16)
    queries = projected[:, 0]
    key_values = projected[:, 1:]
    attended, log_totals = lax.map(
        lambda slot_items: attend_slot(
            slot_items[0], slot_items[1], slot_items[2], score_scale, head_dim
        ),
        (queries, key_values, lengths),
    )
    mixed_rows = attended.reshape(token_count, local_width)
    token_rows = hidden_in.reshape(token_count, model_width)
    branch = lax.psum(
        jnp.dot(mixed_rows, w_back, preferred_element_type=jnp.float32), "tp"
    ) + branch_biases[0].astype(jnp.float32)
    first_norm, first_pull = jax.vjp(
        norm_rows,
        token_rows.astype(jnp.float32) + branch,
        gains[0].astype(jnp.float32),
        shifts[0].astype(jnp.float32),
    )
    first_low = first_norm.astype(jnp.bfloat16)
    hidden_pre = jnp.dot(first_low, w_up, preferred_element_type=jnp.float32) + up_bias.astype(
        jnp.float32
    )
    activated, gelu_pull = jax.vjp(gelu_exact, hidden_pre)
    activated_low = activated.astype(jnp.bfloat16)
    second_branch = lax.psum(
        jnp.dot(activated_low, w_down, preferred_element_type=jnp.float32), "tp"
    ) + branch_biases[1].astype(jnp.float32)
    output_rows, second_pull = jax.vjp(
        norm_rows,
        first_norm + second_branch,
        gains[1].astype(jnp.float32),
        shifts[1].astype(jnp.float32),
    )
    hidden_out = output_rows.astype(jnp.bfloat16).reshape(slot_count, block_len, model_width)
    own_start = lax.axis_index("ctx") * block_len
    positions = own_start + lax.iota(jnp.int32, block_len)
    row_mask = (positions[None, :] < lengths[:, None]).astype(jnp.float32).reshape(token_count, 1)
    grad_output = out_grad.reshape(token_count, model_width).astype(jnp.float32) * row_mask
    grad_second, grad_gain_two, grad_shift_two = second_pull(grad_output)
    grad_second_low = grad_second.astype(jnp.bfloat16)
    grad_down = lax.dot_general(
        activated_low, grad_second_low, contract_rows, preferred_element_type=jnp.float32
    )
    grad_act = lax.dot_general(
        grad_second_low, w_down, contract_cols, preferred_element_type=jnp.float32
    )
    (grad_pre,) = gelu_pull(grad_act)
    grad_pre_low = grad_pre.astype(jnp.bfloat16)
    grad_up = lax.dot_general(
        first_low, grad_pre_low, contract_rows, preferred_element_type=jnp.float32
    )
    grad_first = grad_second + lax.psum(
        lax.dot_general(grad_pre_low, w_up, contract_cols, preferred_element_type=jnp.float32), "tp"
    )
    grad_resid, grad_gain_one, grad_shift_one = first_pull(grad_first)
    grad_branch_low = grad_resid.astype(jnp.bfloat16)
    grad_back = lax.dot_general(
        mixed_rows, grad_branch_low, contract_rows, preferred_element_type=jnp.float32
    )
    grad_mixed = (
        lax.dot_general(grad_branch_low, w_back, contract_cols, preferred_element_type=jnp.float32)
        .astype(jnp.bfloat16)
        .reshape(slot_count, block_len, local_width)
    )
    grad_queries, grad_pairs = lax.map(
        lambda slot_items: slot_grads(
            slot_items[0],
            slot_items[1],
            slot_items[2],
            slot_items[3],
            slot_items[4],
            score_scale,
            head_dim,
        ),
        (queries, key_values, lengths, grad_mixed, log_totals),
    )
    grad_proj = jnp.concatenate(
        [grad_queries.astype(jnp.bfloat16)[:, None], grad_pairs.astype(jnp.bfloat16)], axis=1
    )
    grad_w_proj = jnp.einsum(
        "sbd,spbc->pdc", hidden_in, grad_proj, preferred_element_type=jnp.float32
    )
    grad_proj_bias = jnp.stack(
        [
            jnp.sum(grad_proj[:, 0], axis=(0, 1), dtype=jnp.float32),
            jnp.sum(grad_proj[:, 2], axis=(0, 1), dtype=jnp.float32),
        ]
    ).reshape(proj_bias.shape)
    grad_tokens = jnp.einsum(
        "spbc,pdc->sbd", grad_proj, w_proj, preferred_element_type=jnp.float32
    ).reshape(token_count, model_width)
    hidden_grad = (
        (grad_resid + lax.psum(grad_tokens.astype(jnp.bfloat16), "tp").astype(jnp.float32))
        .astype(jnp.bfloat16)
        .reshape(slot_count, block_len, model_width)
    )
    grad_biases = jnp.stack(
        [
            jnp.sum(grad_branch_low, axis=0, dtype=jnp.float32),
            jnp.sum(grad_second_low, axis=0, dtype=jnp.float32),
        ]
    )
    grad_gains = jnp.stack([grad_gain_one, grad_gain_two])
    grad_shifts = jnp.stack([grad_shift_one, grad_shift_two])
    grad_up_bias = jnp.sum(grad_pre_low, axis=0, dtype=jnp.float32)
    shares = (
        lax.psum_scatter(
            grad_w_proj.astype(jnp.bfloat16), "fsdp", scatter_dimension=1, tiled=True
        ).astype(jnp.float32),
        lax.psum_scatter(
            grad_proj_bias.astype(jnp.bfloat16), "fsdp", scatter_dimension=2, tiled=True
        ).astype(jnp.float32),
        lax.psum_scatter(
            grad_back.astype(jnp.bfloat16), "fsdp", scatter_dimension=1, tiled=True
        ).astype(jnp.float32),
        lax.psum_scatter(
            grad_biases.astype(jnp.bfloat16), "fsdp", scatter_dimension=1, tiled=True
        ).astype(jnp.float32),
        lax.psum_scatter(
            grad_gains.astype(jnp.bfloat16), "fsdp", scatter_dimension=1, tiled=True
        ).astype(jnp.float32),
        lax.psum_scatter(
            grad_shifts.astype(jnp.bfloat16), "fsdp", scatter_dimension=1, tiled=True
        ).astype(jnp.float32),
        lax.psum_scatter(
            grad_up.astype(jnp.bfloat16), "fsdp", scatter_dimension=1, tiled=True
        ).astype(jnp.float32),
        lax.psum_scatter(
            grad_up_bias.astype(jnp.bfloat16), "fsdp", scatter_dimension=0, tiled=True
        ).astype(jnp.float32),
        lax.psum_scatter(
            grad_down.astype(jnp.bfloat16), "fsdp", scatter_dimension=0, tiled=True
        ).astype(jnp.float32),
    )
    owned = (
        lax.psum(shares[0].astype(jnp.bfloat16), "ctx").astype(jnp.float32),
        lax.psum(shares[1].astype(jnp.bfloat16), "ctx").astype(jnp.float32),
        lax.psum(shares[2].astype(jnp.bfloat16), "ctx").astype(jnp.float32),
        lax.psum(shares[3].astype(jnp.bfloat16), "ctx").astype(jnp.float32),
        lax.psum(shares[4].astype(jnp.bfloat16), "ctx").astype(jnp.float32),
        lax.psum(shares[5].astype(jnp.bfloat16), "ctx").astype(jnp.float32),
        lax.psum(shares[6].astype(jnp.bfloat16), "ctx").astype(jnp.float32),
        lax.psum(shares[7].astype(jnp.bfloat16), "ctx").astype(jnp.float32),
        lax.psum(shares[8].astype(jnp.bfloat16), "ctx").astype(jnp.float32),
    )
    return (
        hidden_out,
        hidden_grad,
        owned[0],
        owned[1],
        owned[2],
        owned[3],
        owned[4],
        owned[5],
        owned[6],
        owned[7],
        owned[8],
    )


def solution(mesh):
    one_slot_each = (mesh.shape["fsdp"], mesh.shape["ctx"], mesh.shape["tp"]) == (4, 4, 2)
    return jax.shard_map(
        per_slot if one_slot_each else per_device,
        mesh=mesh,
        in_specs=(
            P("fsdp", "ctx", None),
            P("fsdp"),
            P("fsdp", "ctx", None),
            P(None, "fsdp", "tp"),
            P(None, "tp", "fsdp"),
            P("tp", "fsdp"),
            P(None, "fsdp"),
            P(None, "fsdp"),
            P(None, "fsdp"),
            P(None, ("fsdp", "tp")),
            P(("fsdp", "tp")),
            P(("fsdp", "tp"), None),
        ),
        out_specs=(
            P("fsdp", "ctx", None),
            P("fsdp", "ctx", None),
            P(None, "fsdp", "tp"),
            P(None, "tp", "fsdp"),
            P("tp", "fsdp"),
            P(None, "fsdp"),
            P(None, "fsdp"),
            P(None, "fsdp"),
            P(None, ("fsdp", "tp")),
            P(("fsdp", "tp")),
            P(("fsdp", "tp"), None),
        ),
        check_vma=False,
    )
```

```python
import functools

import jax
import jax.numpy as jnp
from jax import lax
from jax.experimental import pallas as pl
from jax.experimental.pallas import tpu as pltpu
from jax.sharding import PartitionSpec as P

f32 = jnp.float32
bf16 = jnp.bfloat16
MESH = pl.DeviceIdType.MESH
ANY = pl.BlockSpec(memory_space=pl.ANY)
VM = pl.BlockSpec(memory_space=pltpu.VMEM)
SM = pl.BlockSpec(memory_space=pltpu.SMEM)
DMA = pltpu.SemaphoreType.DMA
NN = (((1,), (0,)), ((), ()))
NT = (((1,), (1,)), ((), ()))
TN = (((0,), (0,)), ((), ()))
VMEM_BYTES = 60 << 20


def dot(left, right, dims=NN):
    return lax.dot_general(left, right, dims, preferred_element_type=f32)


def struct(shape, dtype):
    return jax.ShapeDtypeStruct(shape, dtype)


def place():
    z, c, t = lax.axis_index("fsdp"), lax.axis_index("ctx"), lax.axis_index("tp")
    along_x = c + 1 - 2 * (c % 2)
    along_y = c + 2 - 4 * (c // 2)
    n1 = along_x + t * (along_y - along_x)
    n2 = along_y + t * (along_x - along_y)
    return z, c, t, n1, n2, 3 - c


def remote(src, dst, send_sem, recv_sem, device):
    return pltpu.make_async_remote_copy(
        src_ref=src,
        dst_ref=dst,
        send_sem=send_sem,
        recv_sem=recv_sem,
        device_id=device,
        device_id_type=MESH,
    )


def meet(devices):
    barrier = pltpu.get_barrier_semaphore()
    for device in devices:
        pl.semaphore_signal(barrier, inc=1, device_id=device, device_id_type=MESH)
    pl.semaphore_wait(barrier, len(devices))


def tile(i, size):
    return pl.ds(pl.multiple_of(i * size, size), size)


def split3(v):
    hi = v.astype(bf16).astype(f32)
    rest = v - hi
    mid = rest.astype(bf16).astype(f32)
    return hi, mid, rest - mid


def key_bias(length, rows):
    r = lax.broadcasted_iota(jnp.int32, (rows, 128), 0)
    position = (r % 512) // 128 * 256 + r // 512 * 128 + r % 128
    return jnp.where(position < length, 0.0, -1e30)


def gelu_pair(h):
    cdf = 0.5 * (1.0 + lax.erf(h * 0.7071067811865476))
    density = jnp.exp(h * h * -0.5) * 0.3989422804014327
    return h * cdf, cdf + h * density


def unit_rows(r):
    centred = r - jnp.mean(r, axis=-1, keepdims=True)
    spread = jnp.mean(centred * centred, axis=-1, keepdims=True)
    inverse = lax.rsqrt(spread + 1e-5)
    return centred * inverse, inverse


def norm_back(g, n, inverse):
    return inverse * (g - jnp.mean(g, axis=-1, keepdims=True) - n * jnp.mean(g * n, axis=-1, keepdims=True))


def column_sum(v):
    return jnp.sum(v, axis=0, keepdims=True)


class Net:
    def __init__(self, sems):
        self.sems, self.count, self.sends = sems, 0, {}

    def semaphore(self):
        self.count += 1
        return self.sems.at[self.count - 1]

    def send(self, src, dst, device):
        cp = remote(src, dst, self.semaphore(), self.semaphore(), device)
        cp.start()
        self.sends[id(cp)] = cp
        return cp

    def sent(self, copies):
        for cp in copies:
            self.sends.pop(id(cp)).wait_send()

    def local(self, src, dst):
        cp = pltpu.make_async_copy(src, dst, self.semaphore())
        cp.start()
        return cp


class Queue:
    def __init__(self):
        self.steps = []

    def add(self, step):
        self.steps.append(step)

    def tick(self, n=1):
        for _ in range(n):
            if self.steps:
                self.steps.pop(0)()

    def drain(self):
        while self.steps:
            self.tick()


N_SEMS = 512


def layer_kernel(
    len_ref, x_in, og_in, qkv_in, out_in, up_in, down_in, ob_in, ng_in, nb_in, qv_in, fb_in,
    oqkv, oout, oup, odown, osmall, oh, odx,
    xs, ogs, wqkv, wout, wup, wdown, small, small_in, rowp, upb, bias,
    q_ref, k_ref, v_ref, mixed, gmixed, lse,
    qe, ke, ve, de, qz, dz, kt, dqt,
    p_own, p_send, p_recv, n1r, g2r, inv1, low1, low2, low3, act, slope,
    gup, gdown, gout, gqkv, gupb, gsm, gsr, gst, gsz, gsc,
    up1, up2, up3, down1, down2, down3, out1, out2, out3, qkv1, qkv2, qkv3, dna, dn1, dn2,
    sems,
):
    z, c, t, n1, n2, dg = place()
    u = 1 - t
    sibling = (z, c, u)
    planes = (n1, n2, dg)
    net, queue = Net(sems), Queue()
    across, along = (z, n1, t), (z, n2, t)

    def plane_z(d):
        return ((z + d) % 4, c, t)

    small_in[...] = jnp.zeros_like(small_in)
    for row, ref in ((0, ob_in), (2, ng_in), (4, nb_in)):
        small_in[row : row + 2, 0:192] = ref[...].astype(f32)
    small_in[8:9, :] = fb_in[...].astype(f32).reshape(1, 384)
    for i in range(2):
        for h in range(6):
            small_in[16 + 6 * i + h : 17 + 6 * i + h, 0:16] = qv_in[h, i : i + 1, :].astype(f32)
    meet([(z, p, t) for p in planes] + [plane_z(d) for d in (1, 2, 3)] + [sibling])

    schemes = "qqqqhhq"
    side = c % 2 + t * (c // 2 - c % 2)

    def part_of(w, q):
        begin, rows = ((0, 192), (0, 192), (0, 384), (384, 384), (0, 192), (192, 192), (0, 192))[w]
        size = rows // (4 if schemes[w] == "q" else 2)
        return pl.ds(pl.multiple_of(begin + q * size, 16), size)

    def region(w, zz, q):
        begin, rows = ((0, 192), (0, 192), (0, 384), (384, 384), (0, 192), (192, 192), (0, 192))[w]
        size = rows // (4 if schemes[w] == "q" else 2)
        if w in (0, 1, 6):
            rows = pl.ds(pl.multiple_of(zz * 192 + q * size, 16), size)
            return wout.at[rows, :] if w == 1 else wqkv.at[pl.ds(0, 2) if w == 0 else 2, rows, :]
        return (wup if w < 4 else wdown).at[zz, part_of(w, q), :]

    def mine(w):
        rows = part_of(w, c if schemes[w] == "q" else side)
        if w in (0, 6):
            return qkv_in.at[pl.ds(0, 2) if w == 0 else 2, rows, :]
        return (out_in, up_in, up_in, down_in, down_in)[w - 1].at[rows, :]

    zcopies = {}

    def send_z(w):
        for d in (1, 2, 3):
            zcopies[w, d] = net.send(mine(w), region(w, z, c if schemes[w] == "q" else side), plane_z(d))

    spreads = {}

    def spread(w):
        for d in (1, 2, 3):
            zcopies[w, d].wait_recv()
            part = region(w, (z + 4 - d) % 4, c if schemes[w] == "q" else side)
            spreads[w, d] = [net.send(part, part, across)]
            if schemes[w] == "q":
                spreads[w, d].append(net.send(part, part, along))

    def finish(w):
        if schemes[w] == "q":
            for d in (1, 2, 3):
                spreads[w, d][0].wait_recv()
                part = region(w, (z + 4 - d) % 4, n1)
                spreads[w, d].append(net.send(part, part, along))

    def whole(w):
        for d in (1, 2, 3):
            for cp in spreads[w, d][1 if schemes[w] == "q" else 0 :]:
                cp.wait_recv()

    def slot_rows(h, b):
        return pl.ds(pl.multiple_of(h * 512 + b * 128, 128), 128)

    ocopies = []

    def send_og():
        for p in planes:
            ocopies.append(net.send(og_in.at[p, tile(t, 128), :], ogs.at[tile(c, 128), :], (z, p, t)))

    xcopies = [net.send(x_in.at[p, tile(t, 128), :], xs.at[slot_rows(t, c), :], (z, p, t)) for p in planes]
    send_z(0)
    smalls = [net.send(small_in, small.at[z], plane_z(d)) for d in (1, 2, 3)]
    local = [
        net.local(x_in.at[c, pl.ds(0, 128), :], xs.at[slot_rows(0, c), :]),
        net.local(x_in.at[c, pl.ds(128, 128), :], xs.at[slot_rows(1, c), :]),
        net.local(qkv_in, wqkv.at[:, tile(z, 192), :]),
        net.local(small_in, small.at[z]),
        net.local(og_in.at[c, tile(t, 128), :], ogs.at[tile(c, 128), :]),
        net.local(out_in, wout.at[tile(z, 192), :]),
        net.local(up_in, wup.at[z]),
        net.local(down_in, wdown.at[z]),
    ]
    spread(0)
    send_z(6)
    forwards = []
    for i, p in enumerate(planes):
        xcopies[i].wait_recv()
        forwards.append(net.send(xs.at[slot_rows(t, p), :], xs.at[slot_rows(t, p), :], sibling))
    finish(0)
    spread(6)
    send_z(1)
    send_z(2)
    finish(6)
    for cp in local[:4]:
        cp.wait()
    for cp in smalls:
        cp.wait_recv()

    def onehot(rows, cols, target):
        r, l = lax.broadcasted_iota(jnp.int32, (rows, cols), 0), lax.broadcasted_iota(jnp.int32, (rows, cols), 1)
        return jnp.where(l == target(r), 1.0, 0.0).astype(bf16)

    rows768 = jnp.zeros((32, 768), f32)
    rows384 = jnp.zeros((32, 384), f32)
    l16 = lax.broadcasted_iota(jnp.int32, (16, 384), 1)
    r16 = lax.broadcasted_iota(jnp.int32, (16, 384), 0)
    for j in range(4):
        s = small[j].astype(bf16)
        rows768 += dot(s[:, 0:192], onehot(192, 768, lambda r: r + 192 * j))
        rows384 += dot(s[:, 0:16], jnp.where(l16 % 64 == 16 * j + r16, 1.0, 0.0).astype(bf16))
        upb[j : j + 1, :] = small[j, 8:9, :]
    rowp[...] = rows768[0:8, :]
    head = lax.broadcasted_iota(jnp.int32, (32, 384), 0) - lax.broadcasted_iota(jnp.int32, (32, 384), 1) // 64
    for i in range(2):
        bias[6 + i : 7 + i, :] = column_sum(jnp.where(head == 16 + 6 * i, rows384, 0.0))
    bias0, bias1 = rowp[0:1, :], rowp[1:2, :]
    gain0, gain1 = rowp[2:3, :], rowp[3:4, :]
    shift0, shift1 = rowp[4:5, :], rowp[5:6, :]

    for cp in forwards:
        cp.wait_recv()
    whole(0)

    def next_group(w):
        spread(w)
        if w == 2:
            send_z(3)
            send_z(4)
        elif w == 3:
            send_z(5)

    for step in (
        lambda: spread(1),
        lambda: next_group(2),
        lambda: finish(1),
        lambda: finish(2),
        lambda: next_group(3),
        lambda: finish(3),
        lambda: next_group(4),
        lambda: next_group(5),
        send_og,
        lambda: finish(4),
        lambda: finish(5),
    ):
        queue.add(step)

    def project(i, _):
        rows = tile(i, 256)
        xr = xs[rows, :]
        q_ref[rows, :] = ((dot(xr, wqkv[0]) + bias[6:7, :]).astype(bf16).astype(f32) * 0.125).astype(bf16)
        k_ref[rows, :] = dot(xr, wqkv[1]).astype(bf16)
        return 0

    def project_value(i, _):
        rows = tile(i, 256)
        v_ref[rows, :] = (dot(xs[rows, :], wqkv[2]) + bias[7:8, :]).astype(bf16)
        return 0

    lax.fori_loop(0, 4, project, 0)
    whole(6)
    lax.fori_loop(0, 4, project_value, 0)
    queue.tick(2)
    kb = key_bias(len_ref[c], 1024)
    lane = lax.broadcasted_iota(jnp.int32, (1024, 128), 1)
    lse[...] = jnp.zeros_like(lse)

    def own_lanes(j):
        return ((lane < 64), 64) if j == 0 else ((lane >= 64), 0)

    for hp in range(3):
        cols = pl.ds(128 * hp, 128)
        q, k, v = q_ref[:, cols].astype(f32), k_ref[:, cols].astype(f32), v_ref[:, cols].astype(f32)
        for j in range(2):
            own, e = own_lanes(j)
            one = jnp.where(lane == e, 1.0, 0.0)
            qe[j] = jnp.where(own, q, one).astype(bf16)
            ke[j] = jnp.where(own, k, jnp.where(lane == e, kb, 0.0)).astype(bf16)
            ve[j] = jnp.where(own, v, one).astype(bf16)
        for b in range(2):
            rows = pl.ds(512 * b, 512)
            ln = lax.broadcasted_iota(jnp.int32, (512, 128), 1)
            outs, totals = [], []
            for j in range(2):
                e = 64 if j == 0 else 0
                s = dot(qe[j, rows, :], ke[j], NT)
                m = jnp.max(s, axis=1, keepdims=True)
                p = jnp.exp(s - m).astype(bf16)
                o = dot(p, ve[j])
                total = o[:, e : e + 1]
                outs.append(o * (1.0 / total))
                totals.append(m + jnp.log(total))
            mixed[rows, cols] = jnp.where(ln < 64, outs[0], outs[1]).astype(bf16)
            cur = jnp.where(ln == 2 * hp, totals[0], lse[rows, :])
            lse[rows, :] = jnp.where(ln == 2 * hp + 1, totals[1], cur)
            queue.tick()

    local[5].wait()
    whole(1)
    def rows_of(h, i):
        return pl.ds(pl.multiple_of(h * 512 + i * 256, 256), 256)

    def exchange_rows(ref, i):
        return net.send(ref.at[rows_of(t, i), :], ref.at[rows_of(t, i), :], sibling)

    def exchange_parts(value):
        copies = []
        for i in range(2):
            p_send[i] = value(u, i)
            copies.append(net.send(p_send.at[i], p_recv.at[i], sibling))
        for i in range(2):
            p_own[i] = value(t, i)
        return copies

    a = exchange_parts(lambda h, i: dot(mixed[rows_of(h, i), :], wout[...], NT))
    b = []
    for i in range(2):
        a[i].wait_recv()
        r = xs[rows_of(t, i), :].astype(f32) + (p_own[i] + p_recv[i] + bias0)
        n, inverse = unit_rows(r)
        n1r[i] = n
        inv1[i] = jnp.broadcast_to(inverse, (256, 128))
        low1[rows_of(t, i), :] = (n * gain0 + shift0).astype(bf16)
        b.append(exchange_rows(low1, i))
    queue.tick()
    local[6].wait()
    whole(2)
    whole(3)

    def up(h):
        def chunk(zz, _):
            hidden = dot(low1[tile(h, 512), :], wup[zz]) + upb[pl.ds(zz, 1), :]
            value, grad = gelu_pair(hidden)
            act[zz, tile(h, 512), :] = value.astype(bf16)
            slope[zz, tile(h, 512), :] = grad.astype(bf16)
            return 0

        lax.fori_loop(0, 4, chunk, 0)

    up(t)
    queue.tick(2)
    for i in range(2):
        b[i].wait_recv()
    up(u)
    queue.drain()
    local[7].wait()
    whole(4)
    whole(5)

    def down(h, i):
        rows = rows_of(h, i)
        total = dot(act[0, rows, :], wdown[0])
        for zz in range(1, 4):
            total += dot(act[zz, rows, :], wdown[zz])
        return total

    net.sent(a)
    a = exchange_parts(down)
    local[4].wait()
    for cp in ocopies:
        cp.wait_recv()
    hout = ogs
    b = []
    gg1 = gs1 = gb1 = 0.0
    hcopies = []

    def send_rows(src, dst, p, b):
        return net.send(src.at[pl.ds(pl.multiple_of(b * 128, 128), 128), :], dst.at[c, tile(t, 128), :], (z, p, t))

    for i in range(2):
        a[i].wait_recv()
        n, inverse = unit_rows((n1r[i] * gain0 + shift0) + (p_own[i] + p_recv[i] + bias1))
        r = lax.broadcasted_iota(jnp.int32, (256, 768), 0) + 256 * i
        live = (r // 128 * 256 + t * 128 + r % 128) < len_ref[c]
        g = jnp.where(live, ogs[pl.ds(256 * i, 256), :].astype(f32), 0.0)
        hout[pl.ds(256 * i, 256), :] = (n * gain1 + shift1).astype(bf16)
        gg1 = gg1 + column_sum(g * n)
        gs1 = gs1 + column_sum(g)
        g2 = norm_back(g * gain1, n, inverse)
        g2r[i] = g2
        low2[rows_of(t, i), :] = g2.astype(bf16)
        b.append(exchange_rows(low2, i))
        gb1 = gb1 + column_sum(g2.astype(bf16).astype(f32))
    for p in planes:
        hcopies.append(send_rows(hout, oh, p, p))
    hself = [net.send(hout.at[tile(c, 128), :], oh.at[c, tile(t, 128), :], sibling)]
    hlocal = net.local(hout.at[tile(c, 128), :], oh.at[c, tile(t, 128), :])

    quarter_rows = {"up": 192, "out": 96, "qkv": 48}
    final = {}

    def gather_out(ref_of, key):
        first = net.send(ref_of(c), ref_of(c), across)
        second = net.send(ref_of(c), ref_of(c), along)

        def relay():
            first.wait_recv()
            final[key] = [second, net.send(ref_of(n1), ref_of(n1), along)]

        queue.add(relay)

    def reduce_group(key, grad, first, second, third, out, split):
        s1 = [net.send(grad(n1), first.at[0], across), net.send(grad(dg), first.at[1], across)]

        def step2():
            s1[1].wait_recv()
            first[1] = (grad(n2)[...].astype(f32) + first[1].astype(f32)).astype(bf16)
            s2 = net.send(first.at[1], second, along)
            s1[0].wait_recv()

            def step3():
                s2.wait_recv()
                total = grad(c)[...].astype(f32) + first[0].astype(f32) + second[...].astype(f32)
                first[0] = total.astype(bf16)
                s3 = [net.send(split(first.at[0], (z + d) % 4), third.at[d - 1], plane_z(d)) for d in (1, 2, 3)]

                def step4():
                    for cp in s3:
                        cp.wait_recv()
                    v = split(first.at[0], z)[...].astype(f32) + third[0].astype(f32)
                    v = v + (third[1].astype(f32) + third[2].astype(f32))
                    out(c)[...] = v.astype(bf16)
                    gather_out(out, key)

                queue.add(step4)

            queue.add(step3)

        queue.add(step2)

    def reduce_shard(key, d, grad, first, second, third, out, sent):
        s1 = [net.send(grad(n1), first.at[d, 0], across), net.send(grad(dg), first.at[d, 1], across)]

        def step2():
            s1[1].wait_recv()
            first[d, 1] = (grad(n2)[...].astype(f32) + first[d, 1].astype(f32)).astype(bf16)
            s2 = net.send(first.at[d, 1], second.at[d], along)
            s1[0].wait_recv()

            def step3():
                s2.wait_recv()
                total = grad(c)[...].astype(f32) + first[d, 0].astype(f32) + second[d].astype(f32)
                first[d, 0] = total.astype(bf16)
                if d:
                    sent[d] = net.send(first.at[d, 0], third.at[d - 1], plane_z(d))
                else:
                    queue.add(step4)

            queue.add(step3)

        def step4():
            for cp in sent.values():
                cp.wait_recv()
            v = (first[0, 0].astype(f32) + third[0].astype(f32)) + (third[1].astype(f32) + third[2].astype(f32))
            out(c)[...] = v.astype(bf16)
            gather_out(out, key)

        queue.add(step2)

    up_sent, half_sent, down_sent = {}, {}, {}

    def reduce_down():
        for cp in down_sent.values():
            cp.wait_recv()
        rows = pl.ds(0, 256)
        v = (gdown[z, rows, :].astype(f32) + dna[0].astype(f32)) + (dna[1].astype(f32) + dna[2].astype(f32))
        gdown[z, rows, :] = v.astype(bf16)
        quarter = lambda q: gdown.at[z, tile(q, 64), :]
        s1 = [net.send(quarter(n1), dn1.at[0], across), net.send(quarter(dg), dn1.at[1], across)]

        def step2():
            s1[1].wait_recv()
            dn1[1] = (quarter(n2)[...].astype(f32) + dn1[1].astype(f32)).astype(bf16)
            s2 = net.send(dn1.at[1], dn2, along)
            s1[0].wait_recv()

            def step3():
                s2.wait_recv()
                total = quarter(c)[...].astype(f32) + dn1[0].astype(f32) + dn2[...].astype(f32)
                out = lambda q: odown.at[tile(q, 64), :]
                out(c)[...] = total.astype(bf16)
                gather_out(out, "down")

            queue.add(step3)

        queue.add(step2)

    gupb[...] = jnp.zeros_like(gupb)
    for i in range(2):
        b[i].wait_recv()
    low2_sends = b
    for d in (1, 2, 3, 0):
        zz = (z + d) % 4
        for k in range(3):
            g = dot(act[zz, :, pl.ds(128 * k, 128)], low2[...], TN)
            gdown[zz, pl.ds(128 * k, 128), :] = g.astype(bf16)
        if d:
            down_sent[d] = net.send(gdown.at[zz, pl.ds(0, 256), :], dna.at[d - 1], plane_z(d))
        reduce_shard(
            "half", d, lambda q, zz=zz: gdown.at[zz, pl.ds(pl.multiple_of(256 + q * 32, 16), 32), :], down1, down2, down3,
            lambda q: odown.at[pl.ds(pl.multiple_of(256 + q * 32, 16), 32), :], half_sent,
        )

        def back(i, _):
            rows = tile(i, 512)
            g = (dot(low2[rows, :], wdown[zz], NT) * slope[zz, rows, :].astype(f32)).astype(bf16)
            slope[zz, rows, :] = g
            gupb[pl.ds(zz, 1), :] += column_sum(g.astype(f32))
            return 0

        lax.fori_loop(0, 2, back, 0)
        for k in range(6):
            g = dot(low1[:, pl.ds(128 * k, 128)], slope[zz], TN)
            gup[zz, pl.ds(128 * k, 128), :] = g.astype(bf16)
        reduce_shard(
            "up", d, lambda q, zz=zz: gup.at[zz, tile(q, 192), :], up1, up2, up3, lambda q: oup.at[tile(q, 192), :], up_sent
        )
        if d == 0:
            queue.tick(0)

    def first_grad(h, i):
        rows = rows_of(h, i)
        total = dot(slope[0, rows, :], wup[0], NT)
        for zz in range(1, 4):
            total += dot(slope[zz, rows, :], wup[zz], NT)
        return total

    net.sent(a)
    a = exchange_parts(first_grad)
    queue.tick(0)
    b = []
    gg0 = gs0 = gb0 = 0.0
    for i in range(2):
        a[i].wait_recv()
        g1 = g2r[i] + (p_own[i] + p_recv[i])
        n = n1r[i]
        gg0 = gg0 + column_sum(g1 * n)
        gs0 = gs0 + column_sum(g1)
        g = norm_back(g1 * gain0, n, inv1[i][:, 0:1])
        g2r[i] = g
        low3[rows_of(t, i), :] = g.astype(bf16)
        b.append(exchange_rows(low3, i))
        gb0 = gb0 + column_sum(g.astype(bf16).astype(f32))
    gsm[...] = jnp.zeros_like(gsm)
    for row, v in enumerate((gb0, gb1, gg0, gg1, gs0, gs1)):
        for j in range(4):
            gsm[j, row : row + 1, 0:192] = v[:, 192 * j : 192 * j + 192]
    for j in range(4):
        gsm[j, 8:9, :] = gupb[j : j + 1, :]
    queue.tick(1)
    for i in range(2):
        b[i].wait_recv()
    for h in range(2):
        gmixed[tile(h, 512), :] = dot(low3[tile(h, 512), :], wout[...]).astype(bf16)
    for k in range(6):
        g = dot(low3[:, pl.ds(128 * k, 128)], mixed[...], TN).astype(bf16)
        for s in range(2):
            at = 128 * k + 64 * s
            gout[at // 192, pl.ds(at % 192, 64), :] = g[64 * s : 64 * s + 64, :]
    reduce_group(
        "out", lambda q: gout.at[:, tile(q, 48), :], out1, out2, out3, lambda q: oout.at[tile(q, 48), :],
        lambda ref, zz: ref.at[zz],
    )
    dcat, wcat = act, wup
    net.sent([cp for w in (2, 3) for d in (1, 2, 3) for cp in spreads[w, d]])
    queue.add(reduce_down)
    for p in range(3):
        for hp in range(3):
            wcat[hp, :, pl.ds(128 * p, 128)] = wqkv[p, :, pl.ds(128 * hp, 128)]

    def forward_rows(copies, dst):
        out = []
        for cp, p in zip(copies, planes):
            cp.wait_recv()
            part = dst.at[p, tile(t, 128), :]
            out.append(net.send(part, part, sibling))
        return out

    hforward = []
    queue.add(lambda: hforward.extend(forward_rows(hcopies, oh)))

    for hp in range(3):
        cols = pl.ds(128 * hp, 128)
        q, k, v = q_ref[:, cols].astype(f32), k_ref[:, cols].astype(f32), v_ref[:, cols].astype(f32)
        do = gmixed[:, cols].astype(f32)
        pr = do * mixed[:, cols].astype(f32)
        for j in range(2):
            own, e = own_lanes(j)
            delta = jnp.sum(jnp.where(own, pr, 0.0), axis=1, keepdims=True)
            log_total = jnp.sum(jnp.where(lane == 2 * hp + j, lse[...], 0.0), axis=1, keepdims=True)
            lh, lm, ll = split3(-log_total)
            dh, dm, dl = split3(-delta)
            qz[j] = jnp.where(own, q, 0.0).astype(bf16)
            dz[j] = jnp.where(own, do, 0.0).astype(bf16)
            side = jnp.where(lane == e, 1.0, 0.0)
            side = jnp.where(lane == e + 1, lh, side)
            side = jnp.where(lane == e + 2, lm, side)
            side = jnp.where(lane == e + 3, ll, side)
            qe[j] = jnp.where(own, q, side).astype(bf16)
            ones3 = jnp.where((lane > e) & (lane < e + 4), 1.0, 0.0)
            ke[j] = jnp.where(own, k, jnp.where(lane == e, kb, ones3)).astype(bf16)
            side = jnp.where(lane == e + 1, dh, 0.0)
            side = jnp.where(lane == e + 2, dm, side)
            side = jnp.where(lane == e + 3, dl, side)
            de[j] = jnp.where(own, do, side).astype(bf16)
            ve[j] = jnp.where(own, v, ones3).astype(bf16)
        kt[...] = k.T.astype(bf16)
        for b in range(2):
            rows = pl.ds(512 * b, 512)
            dv, dk = None, None
            for j in range(2):
                p = jnp.exp(dot(ke[j, rows, :], qe[j], NT))
                g = dot(ve[j, rows, :], de[j], NT)
                ds = (p * g).astype(bf16)
                a_ = dot(p.astype(bf16), dz[j])
                b_ = dot(ds, qz[j])
                dv = a_ if dv is None else dv + a_
                dk = b_ if dk is None else dk + b_
                half = slice(64 * j, 64 * j + 64)
                if b == 0:
                    dqt[half, :] = dot(kt[half, rows], ds)
                else:
                    dqt[half, :] += dot(kt[half, rows], ds)
            dcat[hp, rows, pl.ds(128, 128)] = dk.astype(bf16)
            dcat[hp, rows, pl.ds(256, 128)] = dv.astype(bf16)
            queue.tick(3)
        dcat[hp, :, pl.ds(0, 128)] = (dqt[...] * 0.125).T.astype(bf16)
        for k in range(6):
            g = dot(xs[:, pl.ds(128 * k, 128)], dcat[hp], TN).astype(bf16)
            for s in range(2):
                at = 128 * k + 64 * s
                gqkv[hp, at // 192, pl.ds(at % 192, 64), :] = g[64 * s : 64 * s + 64, :]

        def last_group():
            grad = lambda q: gqkv.at[2, :, tile(q, 48), :]
            out = lambda q: oqkv.at[2, tile(q, 48), :]
            places = (qkv1.at[2, 0], qkv1.at[2, 1], qkv2.at[2])
            s1 = [net.send(grad(q), place, (z, q, t)) for q, place in zip(planes, places)]

            def step2():
                for cp in s1:
                    cp.wait_recv()
                total = grad(c)[...].astype(f32) + places[0][...].astype(f32)
                places[0][...] = (total + (places[1][...].astype(f32) + places[2][...].astype(f32))).astype(bf16)
                s3 = [net.send(places[0].at[(z + d) % 4], qkv3.at[2, d - 1], plane_z(d)) for d in (1, 2, 3)]

                def step4():
                    for cp in s3:
                        cp.wait_recv()
                    v = places[0][z].astype(f32) + qkv3[2, 0].astype(f32)
                    out(c)[...] = (v + (qkv3[2, 1].astype(f32) + qkv3[2, 2].astype(f32))).astype(bf16)
                    final["last"] = [net.send(out(c), out(c), (z, q, t)) for q in planes]

                queue.add(step4)

            queue.steps.insert(0, step2)

        def pair_group(hp):
            reduce_group(
                "qkv%d" % hp, lambda q: gqkv.at[hp, :, tile(q, 48), :], qkv1.at[hp], qkv2.at[hp], qkv3.at[hp],
                lambda q: oqkv.at[hp, tile(q, 48), :], lambda ref, zz: ref.at[zz],
            )

        if hp < 2:
            pair_group(hp)
            queue.tick(2)

    sums = []
    for p in (0, 2):
        v = jnp.concatenate([column_sum(dcat[hp, :, pl.ds(128 * p, 128)].astype(f32)) for hp in range(3)], axis=1)
        sums.append(jnp.broadcast_to(v, (64, 384)))
    r = lax.broadcasted_iota(jnp.int32, (64, 384), 0)
    l = lax.broadcasted_iota(jnp.int32, (64, 384), 1)
    mine_ = (l // 64 == r % 16 % 6) & (l % 64 // 16 == r // 16)
    spread_rows = jnp.where(mine_, jnp.where(r % 16 < 6, sums[0], sums[1]), 0.0)
    r = lax.broadcasted_iota(jnp.int32, (384, 128), 0)
    l = lax.broadcasted_iota(jnp.int32, (384, 128), 1)
    take = jnp.where(r % 16 == l, 1.0, 0.0).astype(bf16)
    picked = jnp.zeros((64, 128), f32)
    for piece in split3(spread_rows):
        picked += dot(piece.astype(bf16), take)
    for j in range(4):
        gsm[j, 16:32, 0:128] = picked[16 * j : 16 * j + 16, :]
    xsm = net.send(gsm, gsr, sibling)
    last_group()

    def rows_back(h, i):
        rows = rows_of(h, i)
        total = dot(dcat[0, rows, :], wcat[0], NT)
        for hp in range(1, 3):
            total += dot(dcat[hp, rows, :], wcat[hp], NT)
        return total

    net.sent(a + low2_sends)
    dxl = low2
    a = exchange_parts(rows_back)
    queue.tick(1)
    for i in range(2):
        a[i].wait_recv()
        dxl[pl.ds(256 * i, 256), :] = (g2r[i] + (p_own[i] + p_recv[i])).astype(bf16)
    dcopies = [send_rows(dxl, odx, p, p) for p in planes]
    dself = net.send(dxl.at[tile(c, 128), :], odx.at[c, tile(t, 128), :], sibling)
    dlocal = net.local(dxl.at[tile(c, 128), :], odx.at[c, tile(t, 128), :])

    queue.tick(2)
    xsm.wait_recv()
    shared = lax.broadcasted_iota(jnp.int32, (4, 32, 384), 1) < 6
    gst[...] = gsm[...] + jnp.where(shared, gsr[...], 0.0)
    small1 = [net.send(gst.at[(z + d) % 4], gsz.at[d], plane_z(d)) for d in (1, 2, 3)]
    queue.tick(2)
    for cp in small1:
        cp.wait_recv()
    gsz[0] = (gst[z] + gsz[1]) + (gsz[2] + gsz[3])
    small2 = [net.send(gsz.at[0], gsc.at[i], (z, p, t)) for i, p in enumerate(planes)]
    queue.tick(2)
    dforward = []
    queue.add(lambda: dforward.extend(forward_rows(dcopies, odx)))
    queue.drain()
    for cp in small2:
        cp.wait_recv()
    osmall[...] = (gsz[0] + gsc[0]) + (gsc[1] + gsc[2])
    for copies in final.values():
        for cp in copies:
            cp.wait_recv()
    for cp in hforward + dforward + hself + [dself]:
        cp.wait_recv()
    hlocal.wait()
    dlocal.wait()
    net.sent(list(net.sends.values()))
    assert net.count <= N_SEMS


def finish_kernel(oqkv, oout, oup, odown, osmall, oh, odx, h, dx, gqkv, gqv, gout, gob, gng, gnb, gup, gfb, gdown):
    h[...] = oh[...]
    dx[...] = odx[...]
    for hp in range(3):
        for p in range(3):
            gqkv[p, :, pl.ds(128 * hp, 128)] = oqkv[hp, :, pl.ds(128 * p, 128)].astype(f32)
    gout[...] = oout[...].astype(f32)
    gup[...] = oup[...].astype(f32)
    gdown[...] = odown[...].astype(f32)
    for row, ref in ((0, gob), (2, gng), (4, gnb)):
        ref[...] = osmall[row : row + 2, 0:192]
    gfb[...] = osmall[8:9, :].reshape(384)
    for i in range(2):
        for h in range(6):
            gqv[h, i : i + 1, :] = osmall[16 + 6 * i + h : 17 + 6 * i + h, 0:16]


def per_slot(hidden_in, lengths, out_grad, w_qkv, qv_bias, w_out, out_biases, norm_gains, norm_biases, w_in, ffn_bias, w_ffo):
    def vm(*shape, dtype=bf16):
        return pltpu.VMEM(shape, dtype)

    small = (32, 384)
    raw = pl.pallas_call(
        layer_kernel,
        out_shape=(
            struct((3, 192, 384), bf16),
            struct((192, 384), bf16),
            struct((768, 384), bf16),
            struct((384, 768), bf16),
            struct(small, f32),
            struct((4, 256, 768), bf16),
            struct((4, 256, 768), bf16),
        ),
        in_specs=[SM] + [ANY] * 6 + [VM] * 5,
        out_specs=(VM,) * 5 + (ANY, ANY),
        scratch_shapes=[
            vm(1024, 768), vm(512, 768), vm(3, 768, 384), vm(768, 384), vm(4, 768, 384), vm(4, 384, 768),
            vm(4, *small, dtype=f32), vm(*small, dtype=f32), vm(8, 768, dtype=f32), vm(4, 384, dtype=f32), vm(8, 384, dtype=f32),
            vm(1024, 384), vm(1024, 384), vm(1024, 384), vm(1024, 384), vm(1024, 384), vm(1024, 128, dtype=f32),
        ]
        + [vm(2, 1024, 128)] * 6
        + [vm(128, 1024), vm(128, 1024, dtype=f32)]
        + [vm(2, 256, 768, dtype=f32)] * 5
        + [
            vm(2, 256, 128, dtype=f32), vm(1024, 768), vm(1024, 768), vm(1024, 768), vm(4, 1024, 384), vm(4, 1024, 384),
            vm(4, 768, 384), vm(4, 384, 768), vm(4, 192, 384), vm(3, 4, 192, 384), vm(4, 384, dtype=f32),
        ]
        + [vm(4, *small, dtype=f32)] * 4
        + [
            vm(3, *small, dtype=f32),
            vm(4, 2, 192, 384), vm(4, 192, 384), vm(3, 192, 384),
            vm(4, 2, 32, 768), vm(4, 32, 768), vm(3, 32, 768),
            vm(2, 4, 48, 384), vm(4, 48, 384), vm(3, 48, 384),
            vm(3, 2, 4, 48, 384), vm(3, 4, 48, 384), vm(3, 3, 48, 384),
            vm(3, 256, 768), vm(2, 64, 768), vm(64, 768),
            DMA((N_SEMS,)),
        ],
        compiler_params=pltpu.CompilerParams(collective_id=0, has_side_effects=True, vmem_limit_bytes=VMEM_BYTES),
        name="layer",
    )(
        lengths, hidden_in, out_grad, w_qkv, w_out.T, w_in, w_ffo,
        out_biases, norm_gains, norm_biases, qv_bias.transpose(1, 0, 2), ffn_bias,
    )

    def rows_block(*shape):
        return pl.BlockSpec(shape, (lambda i: (i, 0)) if len(shape) == 2 else (lambda i: (0, i, 0)))

    def fixed(*shape):
        return pl.BlockSpec(shape, lambda i: (0,) * len(shape))

    slot_block = pl.BlockSpec((1, 256, 768), lambda i: (i, 0, 0))
    h, dx, gqkv, gqv, gout, gob, gng, gnb, gup, gfb, gdown = pl.pallas_call(
        finish_kernel,
        out_shape=(
            struct((4, 256, 768), bf16),
            struct((4, 256, 768), bf16),
            struct((3, 192, 384), f32),
            struct((6, 2, 16), f32),
            struct((192, 384), f32),
            struct((2, 192), f32),
            struct((2, 192), f32),
            struct((2, 192), f32),
            struct((768, 384), f32),
            struct((384,), f32),
            struct((384, 768), f32),
        ),
        grid=(4,),
        in_specs=[
            rows_block(3, 48, 384), rows_block(48, 384), rows_block(192, 384), rows_block(96, 768), fixed(*small),
            slot_block, slot_block,
        ],
        out_specs=(
            slot_block, slot_block, rows_block(3, 48, 384), fixed(6, 2, 16), rows_block(48, 384), fixed(2, 192), fixed(2, 192),
            fixed(2, 192), rows_block(192, 384), fixed(384), rows_block(96, 768),
        ),
        compiler_params=pltpu.CompilerParams(vmem_limit_bytes=VMEM_BYTES),
        name="finish",
    )(*raw)
    return h, dx, gqkv, gqv.transpose(1, 0, 2), gout.T, gob, gng, gnb, gup, gfb, gdown


epsilon = 1e-05
masked_value = -1e30
heads_together = 2


def norm_rows(residual, gain_row, shift_row):
    centre = jnp.mean(residual, axis=-1, keepdims=True)
    centred = residual - centre
    spread = jnp.mean(centred * centred, axis=-1, keepdims=True)
    return centred * lax.rsqrt(spread + epsilon) * gain_row + shift_row


def gelu_exact(values):
    return jax.nn.gelu(values, approximate=False)


def split_heads(matrix, head_dim):
    return matrix.reshape(matrix.shape[0], matrix.shape[1] // head_dim, head_dim)


def block_scores(query_heads, key_heads, key_mask, score_scale):
    scores = (
        jnp.einsum("qhd,khd->hqk", query_heads, key_heads, preferred_element_type=jnp.float32)
        * score_scale
    )
    return jnp.where(key_mask[None, None, :], scores, masked_value)


def attend_slot(queries, key_value, length, score_scale, head_dim):
    gathered = lax.all_gather(key_value, "ctx", axis=1, tiled=True)
    seq_len = gathered.shape[1]
    key_mask = lax.iota(jnp.int32, seq_len) < length
    block_width = heads_together * head_dim
    outputs = []
    totals = []
    for head_block in range(queries.shape[1] // block_width):
        columns = slice(head_block * block_width, (head_block + 1) * block_width)
        query_heads = split_heads(queries[:, columns], head_dim)
        key_heads = split_heads(gathered[0][:, columns], head_dim)
        value_heads = split_heads(gathered[1][:, columns], head_dim)
        scores = block_scores(query_heads, key_heads, key_mask, score_scale)
        highest = jnp.max(scores, axis=-1, keepdims=True)
        log_total = highest + jnp.log(jnp.sum(jnp.exp(scores - highest), axis=-1, keepdims=True))
        weights_low = jnp.exp(scores - log_total).astype(jnp.bfloat16)
        attended = jnp.einsum(
            "hqk,khd->qhd", weights_low, value_heads, preferred_element_type=jnp.float32
        )
        outputs.append(attended.reshape(attended.shape[0], block_width))
        totals.append(log_total[:, :, 0])
    return (jnp.concatenate(outputs, axis=1).astype(jnp.bfloat16), jnp.concatenate(totals, axis=0))


def slot_grads(queries, key_value, length, grad_mixed, log_totals, score_scale, head_dim):
    gathered = lax.all_gather(key_value, "ctx", axis=1, tiled=True)
    seq_len = gathered.shape[1]
    key_mask = lax.iota(jnp.int32, seq_len) < length
    block_width = heads_together * head_dim
    query_grads = []
    key_grads = []
    value_grads = []
    inner_parts = []
    for head_block in range(queries.shape[1] // block_width):
        columns = slice(head_block * block_width, (head_block + 1) * block_width)
        heads_range = slice(head_block * heads_together, (head_block + 1) * heads_together)
        query_heads = split_heads(queries[:, columns], head_dim)
        key_heads = split_heads(gathered[0][:, columns], head_dim)
        value_heads = split_heads(gathered[1][:, columns], head_dim)
        grad_heads = split_heads(grad_mixed[:, columns], head_dim)
        scores = block_scores(query_heads, key_heads, key_mask, score_scale)
        softmax_rows = jnp.exp(scores - log_totals[heads_range, :, None])
        grad_weights = jnp.einsum(
            "qhd,khd->hqk", grad_heads, value_heads, preferred_element_type=jnp.float32
        )
        inner_sums = jnp.sum(softmax_rows * grad_weights, axis=-1)
        grad_scores = (softmax_rows * (grad_weights - inner_sums[:, :, None])).astype(jnp.bfloat16)
        grad_query = (
            jnp.einsum("hqk,khd->qhd", grad_scores, key_heads, preferred_element_type=jnp.float32)
            * score_scale
        )
        query_grads.append(grad_query.reshape(grad_query.shape[0], block_width))
        inner_parts.append(inner_sums)
        grad_key = (
            jnp.einsum("hqk,qhd->khd", grad_scores, query_heads, preferred_element_type=jnp.float32)
            * score_scale
        )
        grad_value = jnp.einsum(
            "hqk,qhd->khd",
            softmax_rows.astype(jnp.bfloat16),
            grad_heads,
            preferred_element_type=jnp.float32,
        )
        key_grads.append(grad_key.reshape(seq_len, block_width))
        value_grads.append(grad_value.reshape(seq_len, block_width))
    grad_queries = jnp.concatenate(query_grads, axis=1)
    key_terms = jnp.stack(
        [jnp.concatenate(key_grads, axis=1), jnp.concatenate(value_grads, axis=1)]
    )
    own_grads = lax.psum_scatter(
        key_terms.astype(jnp.bfloat16), "ctx", scatter_dimension=1, tiled=True
    ).astype(jnp.float32)
    return (grad_queries, own_grads)


def per_device(
    hidden_in,
    lengths,
    out_grad,
    w_qkv,
    qv_bias,
    w_out,
    out_biases,
    norm_gains,
    norm_biases,
    w_in,
    ffn_bias,
    w_ffo,
):
    w_proj, proj_bias, w_back, branch_biases, gains, shifts, w_up, up_bias, w_down = (
        lax.all_gather(w_qkv, "fsdp", axis=1, tiled=True),
        lax.all_gather(qv_bias, "fsdp", axis=2, tiled=True),
        lax.all_gather(w_out, "fsdp", axis=1, tiled=True),
        lax.all_gather(out_biases, "fsdp", axis=1, tiled=True),
        lax.all_gather(norm_gains, "fsdp", axis=1, tiled=True),
        lax.all_gather(norm_biases, "fsdp", axis=1, tiled=True),
        lax.all_gather(w_in, "fsdp", axis=1, tiled=True),
        lax.all_gather(ffn_bias, "fsdp", axis=0, tiled=True),
        lax.all_gather(w_ffo, "fsdp", axis=0, tiled=True),
    )
    slot_count, block_len, model_width = hidden_in.shape
    token_count = slot_count * block_len
    head_dim = proj_bias.shape[2]
    score_scale = head_dim ** (-0.5)
    local_width = w_proj.shape[2]
    contract_rows = (((0,), (0,)), ((), ()))
    contract_cols = (((1,), (1,)), ((), ()))
    bias_table = jnp.stack(
        [
            proj_bias[0].reshape(local_width).astype(jnp.float32),
            jnp.zeros((local_width,), jnp.float32),
            proj_bias[1].reshape(local_width).astype(jnp.float32),
        ]
    )
    projected = (
        jnp.einsum("sbd,pdc->spbc", hidden_in, w_proj, preferred_element_type=jnp.float32)
        + bias_table[None, :, None, :]
    ).astype(jnp.bfloat16)
    queries = projected[:, 0]
    key_values = projected[:, 1:]
    attended, log_totals = lax.map(
        lambda slot_items: attend_slot(
            slot_items[0], slot_items[1], slot_items[2], score_scale, head_dim
        ),
        (queries, key_values, lengths),
    )
    mixed_rows = attended.reshape(token_count, local_width)
    token_rows = hidden_in.reshape(token_count, model_width)
    branch = lax.psum(
        jnp.dot(mixed_rows, w_back, preferred_element_type=jnp.float32), "tp"
    ) + branch_biases[0].astype(jnp.float32)
    first_norm, first_pull = jax.vjp(
        norm_rows,
        token_rows.astype(jnp.float32) + branch,
        gains[0].astype(jnp.float32),
        shifts[0].astype(jnp.float32),
    )
    first_low = first_norm.astype(jnp.bfloat16)
    hidden_pre = jnp.dot(first_low, w_up, preferred_element_type=jnp.float32) + up_bias.astype(
        jnp.float32
    )
    activated, gelu_pull = jax.vjp(gelu_exact, hidden_pre)
    activated_low = activated.astype(jnp.bfloat16)
    second_branch = lax.psum(
        jnp.dot(activated_low, w_down, preferred_element_type=jnp.float32), "tp"
    ) + branch_biases[1].astype(jnp.float32)
    output_rows, second_pull = jax.vjp(
        norm_rows,
        first_norm + second_branch,
        gains[1].astype(jnp.float32),
        shifts[1].astype(jnp.float32),
    )
    hidden_out = output_rows.astype(jnp.bfloat16).reshape(slot_count, block_len, model_width)
    own_start = lax.axis_index("ctx") * block_len
    positions = own_start + lax.iota(jnp.int32, block_len)
    row_mask = (positions[None, :] < lengths[:, None]).astype(jnp.float32).reshape(token_count, 1)
    grad_output = out_grad.reshape(token_count, model_width).astype(jnp.float32) * row_mask
    grad_second, grad_gain_two, grad_shift_two = second_pull(grad_output)
    grad_second_low = grad_second.astype(jnp.bfloat16)
    grad_down = lax.dot_general(
        activated_low, grad_second_low, contract_rows, preferred_element_type=jnp.float32
    )
    grad_act = lax.dot_general(
        grad_second_low, w_down, contract_cols, preferred_element_type=jnp.float32
    )
    (grad_pre,) = gelu_pull(grad_act)
    grad_pre_low = grad_pre.astype(jnp.bfloat16)
    grad_up = lax.dot_general(
        first_low, grad_pre_low, contract_rows, preferred_element_type=jnp.float32
    )
    grad_first = grad_second + lax.psum(
        lax.dot_general(grad_pre_low, w_up, contract_cols, preferred_element_type=jnp.float32), "tp"
    )
    grad_resid, grad_gain_one, grad_shift_one = first_pull(grad_first)
    grad_branch_low = grad_resid.astype(jnp.bfloat16)
    grad_back = lax.dot_general(
        mixed_rows, grad_branch_low, contract_rows, preferred_element_type=jnp.float32
    )
    grad_mixed = (
        lax.dot_general(grad_branch_low, w_back, contract_cols, preferred_element_type=jnp.float32)
        .astype(jnp.bfloat16)
        .reshape(slot_count, block_len, local_width)
    )
    grad_queries, grad_pairs = lax.map(
        lambda slot_items: slot_grads(
            slot_items[0],
            slot_items[1],
            slot_items[2],
            slot_items[3],
            slot_items[4],
            score_scale,
            head_dim,
        ),
        (queries, key_values, lengths, grad_mixed, log_totals),
    )
    grad_proj = jnp.concatenate(
        [grad_queries.astype(jnp.bfloat16)[:, None], grad_pairs.astype(jnp.bfloat16)], axis=1
    )
    grad_w_proj = jnp.einsum(
        "sbd,spbc->pdc", hidden_in, grad_proj, preferred_element_type=jnp.float32
    )
    grad_proj_bias = jnp.stack(
        [
            jnp.sum(grad_proj[:, 0], axis=(0, 1), dtype=jnp.float32),
            jnp.sum(grad_proj[:, 2], axis=(0, 1), dtype=jnp.float32),
        ]
    ).reshape(proj_bias.shape)
    grad_tokens = jnp.einsum(
        "spbc,pdc->sbd", grad_proj, w_proj, preferred_element_type=jnp.float32
    ).reshape(token_count, model_width)
    hidden_grad = (
        (grad_resid + lax.psum(grad_tokens.astype(jnp.bfloat16), "tp").astype(jnp.float32))
        .astype(jnp.bfloat16)
        .reshape(slot_count, block_len, model_width)
    )
    grad_biases = jnp.stack(
        [
            jnp.sum(grad_branch_low, axis=0, dtype=jnp.float32),
            jnp.sum(grad_second_low, axis=0, dtype=jnp.float32),
        ]
    )
    grad_gains = jnp.stack([grad_gain_one, grad_gain_two])
    grad_shifts = jnp.stack([grad_shift_one, grad_shift_two])
    grad_up_bias = jnp.sum(grad_pre_low, axis=0, dtype=jnp.float32)
    shares = (
        lax.psum_scatter(
            grad_w_proj.astype(jnp.bfloat16), "fsdp", scatter_dimension=1, tiled=True
        ).astype(jnp.float32),
        lax.psum_scatter(
            grad_proj_bias.astype(jnp.bfloat16), "fsdp", scatter_dimension=2, tiled=True
        ).astype(jnp.float32),
        lax.psum_scatter(
            grad_back.astype(jnp.bfloat16), "fsdp", scatter_dimension=1, tiled=True
        ).astype(jnp.float32),
        lax.psum_scatter(
            grad_biases.astype(jnp.bfloat16), "fsdp", scatter_dimension=1, tiled=True
        ).astype(jnp.float32),
        lax.psum_scatter(
            grad_gains.astype(jnp.bfloat16), "fsdp", scatter_dimension=1, tiled=True
        ).astype(jnp.float32),
        lax.psum_scatter(
            grad_shifts.astype(jnp.bfloat16), "fsdp", scatter_dimension=1, tiled=True
        ).astype(jnp.float32),
        lax.psum_scatter(
            grad_up.astype(jnp.bfloat16), "fsdp", scatter_dimension=1, tiled=True
        ).astype(jnp.float32),
        lax.psum_scatter(
            grad_up_bias.astype(jnp.bfloat16), "fsdp", scatter_dimension=0, tiled=True
        ).astype(jnp.float32),
        lax.psum_scatter(
            grad_down.astype(jnp.bfloat16), "fsdp", scatter_dimension=0, tiled=True
        ).astype(jnp.float32),
    )
    owned = (
        lax.psum(shares[0].astype(jnp.bfloat16), "ctx").astype(jnp.float32),
        lax.psum(shares[1].astype(jnp.bfloat16), "ctx").astype(jnp.float32),
        lax.psum(shares[2].astype(jnp.bfloat16), "ctx").astype(jnp.float32),
        lax.psum(shares[3].astype(jnp.bfloat16), "ctx").astype(jnp.float32),
        lax.psum(shares[4].astype(jnp.bfloat16), "ctx").astype(jnp.float32),
        lax.psum(shares[5].astype(jnp.bfloat16), "ctx").astype(jnp.float32),
        lax.psum(shares[6].astype(jnp.bfloat16), "ctx").astype(jnp.float32),
        lax.psum(shares[7].astype(jnp.bfloat16), "ctx").astype(jnp.float32),
        lax.psum(shares[8].astype(jnp.bfloat16), "ctx").astype(jnp.float32),
    )
    return (
        hidden_out,
        hidden_grad,
        owned[0],
        owned[1],
        owned[2],
        owned[3],
        owned[4],
        owned[5],
        owned[6],
        owned[7],
        owned[8],
    )


def solution(mesh):
    one_slot_each = (mesh.shape["fsdp"], mesh.shape["ctx"], mesh.shape["tp"]) == (4, 4, 2)
    return jax.shard_map(
        per_slot if one_slot_each else per_device,
        mesh=mesh,
        in_specs=(
            P("fsdp", "ctx", None),
            P("fsdp"),
            P("fsdp", "ctx", None),
            P(None, "fsdp", "tp"),
            P(None, "tp", "fsdp"),
            P("tp", "fsdp"),
            P(None, "fsdp"),
            P(None, "fsdp"),
            P(None, "fsdp"),
            P(None, ("fsdp", "tp")),
            P(("fsdp", "tp")),
            P(("fsdp", "tp"), None),
        ),
        out_specs=(
            P("fsdp", "ctx", None),
            P("fsdp", "ctx", None),
            P(None, "fsdp", "tp"),
            P(None, "tp", "fsdp"),
            P("tp", "fsdp"),
            P(None, "fsdp"),
            P(None, "fsdp"),
            P(None, "fsdp"),
            P(None, ("fsdp", "tp")),
            P(("fsdp", "tp")),
            P(("fsdp", "tp"), None),
        ),
        check_vma=False,
    )
```
